32 devices in a mesh: clip: 4 (over y, core), sess: 8 (over z, x).
Axes of the slice: x: 2, y: 2, z: 4, core: 2. Of those that a mesh axis runs over, the one named last changes fastest.
Arguments:
- video: bfloat16 [32, 8, 2304], P('clip', 'sess'), may hold values from -6 to 6
- responses: bfloat16 [32, 8, 4096], P('clip', 'sess'), may hold values from 0 to 0.5
- assignment: int32 [32], P('clip'), may hold values from 0 to 7, as said below
- counts: int32 [8], P('sess'), may hold values from 1024 to 4096, as said below
- conv_weight: bfloat16 [64, 147], replicated, may hold values from -0.5 to 0.5
- conv_bias: float32 [64], replicated, may hold values from -3 to 3
- mix_weight: bfloat16 [64, 64], replicated, may hold values from -0.75 to 0.75
- mix_bias: float32 [64], replicated, may hold values from -3 to 3
- masks: bfloat16 [8, 4096, 576], P('sess'), may hold values from -0.25 to 0.25
- feat_w: bfloat16 [8, 4096, 64], P('sess'), may hold values from -0.75 to 0.75
- readout_bias: float32 [8, 4096], P('sess'), may hold values from -1 to 1
Outputs:
- loss: float32 [], replicated
- grad_conv_weight: float32 [64, 147], replicated
- grad_conv_bias: float32 [64], replicated
- grad_mix_weight: float32 [64, 64], replicated
- grad_mix_bias: float32 [64], replicated
- grad_masks: float32 [8, 4096, 576], P('sess', 'clip')
- grad_feat_w: float32 [8, 4096, 64], P('sess', 'clip')
- grad_readout_bias: float32 [8, 4096], P('sess', 'clip')
The draws below stay inside these ranges and needn't reach their ends.
Inputs may be any that keep to these rules, and one draw needn't show every extreme that they name: `assignment`: in every aligned block of 8 clips, each of the 8 sessions is named by exactly one clip. `counts`: some session has exactly 4096 neurons.
All inputs are finite; a program needn't handle non-finite values.
Results may differ from the reference program's by a relative error of at most 0.0085.
Values may be sent and summed in bfloat16 or wider, within the bound.
No kernel may reach another device: no remote copies, remote signals or barrier semaphores. Data moves between devices by JAX's collectives and lax.ppermute only.
A program may use at most 192 MiB of HBM per device.

```python
import jax
import jax.numpy as jnp
from jax import lax

C = 64
N = 4096
HH = 36
WW = 64
KS = 7
KT = 3
SESS_DEV = 1
PIX = 2304
POOLED = 576
TAPS = 147
CLIP_DEV = 8
CLIPS = 32
FRAMES = 8
SESSIONS = 8


def draw_assignment(key, part):
    block_total = CLIPS // CLIP_DEV
    owner_total = SESSIONS // SESS_DEV
    owner_list = jnp.repeat(jnp.arange(owner_total, dtype=jnp.int32), CLIP_DEV // owner_total)
    block_keys = jax.random.split(jax.random.fold_in(key, 11), block_total)
    owners = jax.vmap(lambda block_key: jax.random.permutation(block_key, owner_list))(block_keys).reshape(-1)
    local_pick = jax.random.randint(jax.random.fold_in(key, 12), (CLIPS,), 0, SESS_DEV, dtype=jnp.int32)
    return (owners * SESS_DEV + local_pick).astype(jnp.int32)


def draw_counts(key, part):
    drawn = jax.random.randint(jax.random.fold_in(key, 21), (SESSIONS,), N // 4, N + 1, dtype=jnp.int32)
    fullest = jax.random.randint(jax.random.fold_in(key, 22), (), 0, SESSIONS, dtype=jnp.int32)
    return jnp.where(jnp.arange(SESSIONS, dtype=jnp.int32) == fullest, N, drawn).astype(jnp.int32)


def shard_levels(own_key, shape, cuts, low, high):
    def one(axis_at, shards_of):
        steps = jax.random.uniform(jax.random.fold_in(jax.random.fold_in(own_key, 6), axis_at), (shards_of,), jnp.float32, low / len(cuts), high / len(cuts))
        return jnp.repeat(jnp.exp(steps), shape[axis_at] // shards_of).reshape((-1,) + (1,) * (len(shape) - axis_at - 1))

    gain = one(*cuts[0])
    for cut in cuts[1:]:
        gain = gain * one(*cut)
    return gain


def normal_values(key, dims, width, limit, cuts=(), kind=jnp.bfloat16):
    array = width * jax.random.normal(key, dims, jnp.float32)
    if cuts:
        array = array * shard_levels(key, dims, cuts, -0.22, 0.18)
    return jnp.clip(array, -limit, limit).astype(kind)


def setup_inputs(seed: int = 0) -> dict:
    keys = jax.random.split(jax.random.key(seed), 12)
    return {
        "video": normal_values(keys[0], (CLIPS, FRAMES, PIX), 1.0, 6.0, ((0, 4), (1, 8))),
        "responses": jnp.clip(0.5 * jax.random.uniform(keys[1], (CLIPS, FRAMES, N), jnp.float32) ** shard_levels(keys[1], (CLIPS, FRAMES, N), ((0, 4), (1, 8)), -0.2, 0.2), 0.0, 0.5).astype(jnp.bfloat16),
        "assignment": draw_assignment(jax.random.fold_in(keys[11], 71), 0),
        "counts": draw_counts(jax.random.fold_in(keys[11], 71), 0),
        "conv_weight": normal_values(keys[4], (C, TAPS), TAPS ** -0.5, 0.5),
        "conv_bias": normal_values(keys[5], (C,), 0.5, 3.0, (), jnp.float32),
        "mix_weight": normal_values(keys[6], (C, C), C ** -0.5, 0.75),
        "mix_bias": normal_values(keys[7], (C,), 0.5, 3.0, (), jnp.float32),
        "masks": normal_values(keys[8], (SESSIONS, N, POOLED), POOLED ** -0.5, 0.25, ((0, 8),)),
        "feat_w": normal_values(keys[9], (SESSIONS, N, C), C ** -0.5, 0.75, ((0, 8),)),
        "readout_bias": jnp.clip(jax.random.uniform(keys[10], (SESSIONS, N), jnp.float32, -1.0, 1.0) * shard_levels(keys[10], (SESSIONS, N), ((0, 8),), -0.4, 0.0), -1.0, 1.0),
    }


def elu_slope(values):
    return jnp.where(values > 0, 1.0, jnp.exp(jnp.minimum(values, 0.0)))


def core_forward(video_pad, frames, conv_weight, conv_bias, mix_weight, mix_bias):
    clip_count = video_pad.shape[0]
    margin = KS // 2
    padded_grid = video_pad.reshape(clip_count, frames + 2, HH, WW)
    padded_grid = jnp.pad(padded_grid, ((0, 0), (0, 0), (margin, margin), (margin, margin)))
    tap_list = []
    for time_shift in range(KT):
        for row_shift in range(KS):
            for col_shift in range(KS):
                window = padded_grid[:, time_shift:time_shift + frames, row_shift:row_shift + HH, col_shift:col_shift + WW]
                tap_list.append(window.reshape(clip_count, frames, HH * WW))
    patches = jnp.stack(tap_list, 0)
    pre1 = jnp.einsum('ot,tkfp->kfop', conv_weight.astype(jnp.float32), patches.astype(jnp.float32)) + conv_bias[:, None]
    act1 = jax.nn.elu(pre1).astype(jnp.bfloat16)
    pre2 = jnp.einsum('oc,kfcp->kfop', mix_weight.astype(jnp.float32), act1.astype(jnp.float32)) + mix_bias[:, None]
    feats = jax.nn.elu(pre2).astype(jnp.bfloat16)
    return patches, pre1, act1, pre2, feats


def pool_map(feats):
    clip_count, frames, channels = feats.shape[0], feats.shape[1], feats.shape[2]
    blocks = feats.astype(jnp.float32).reshape(clip_count, frames, channels, HH // 2, 2, WW // 2, 2)
    return jnp.mean(blocks, axis=(4, 6)).reshape(clip_count, frames, channels, -1).astype(jnp.bfloat16)


def unpool_map(pooled_grad):
    clip_count, frames, channels = pooled_grad.shape[0], pooled_grad.shape[1], pooled_grad.shape[2]
    blocks = pooled_grad.reshape(clip_count, frames, channels, HH // 2, 1, WW // 2, 1)
    blocks = jnp.broadcast_to(blocks, (clip_count, frames, channels, HH // 2, 2, WW // 2, 2))
    return (blocks * 0.25).astype(jnp.bfloat16).reshape(clip_count, frames, channels, HH * WW)


def core_backward(feats_grad, patches, pre1, act1, pre2, mix_weight):
    pre2_grad = (feats_grad.astype(jnp.float32) * elu_slope(pre2)).astype(jnp.bfloat16)
    grad_mix = jnp.einsum('kfop,kfcp->oc', pre2_grad.astype(jnp.float32), act1.astype(jnp.float32))
    grad_mix_b = jnp.sum(pre2_grad.astype(jnp.float32), axis=(0, 1, 3))
    act1_grad = jnp.einsum('oc,kfop->kfcp', mix_weight.astype(jnp.float32), pre2_grad.astype(jnp.float32))
    pre1_grad = (act1_grad * elu_slope(pre1)).astype(jnp.bfloat16)
    grad_conv = jnp.einsum('kfop,tkfp->ot', pre1_grad.astype(jnp.float32), patches.astype(jnp.float32))
    grad_conv_b = jnp.sum(pre1_grad.astype(jnp.float32), axis=(0, 1, 3))
    return grad_conv, grad_conv_b, grad_mix, grad_mix_b


def readout(pooled_flat, target_all, mask, weight, rbias, live_count, row_start, row_count, loss_scale):
    frames = target_all.shape[0]
    channels = weight.shape[1]
    mask_rows = lax.dynamic_slice_in_dim(mask, row_start, row_count, 0)
    weight_rows = lax.dynamic_slice_in_dim(weight, row_start, row_count, 0).astype(jnp.float32)
    bias_rows = lax.dynamic_slice_in_dim(rbias, row_start, row_count, 0)
    target = lax.dynamic_slice_in_dim(target_all, row_start, row_count, 1).astype(jnp.float32).T
    projected = jnp.dot(mask_rows, pooled_flat.T, preferred_element_type=jnp.float32)
    w_tile = jnp.tile(weight_rows, (1, frames))
    drive = (projected * w_tile).reshape(row_count, frames, channels).sum(-1) + bias_rows[:, None]
    rate_pred = jax.nn.softplus(drive) + 0.1
    alive_rows = ((row_start + jnp.arange(row_count, dtype=jnp.int32)) < live_count)[:, None]
    loss_sum = jnp.sum(jnp.where(alive_rows, rate_pred - target * jnp.log(rate_pred), 0.0)) * loss_scale
    grad_drive = jnp.where(alive_rows, (1.0 - target / rate_pred) * jax.nn.sigmoid(drive), 0.0) * loss_scale
    spread = jnp.repeat(grad_drive, channels, axis=1)
    feat_grad = (spread * projected).reshape(row_count, frames, channels).sum(1)
    mixed = (spread * w_tile).astype(jnp.bfloat16)
    mask_grad = jnp.dot(mixed, pooled_flat, preferred_element_type=jnp.float32)
    pooled_grad = jnp.dot(mixed.T, mask_rows, preferred_element_type=jnp.float32)
    return loss_sum, pooled_grad, mask_grad, feat_grad, jnp.sum(grad_drive, axis=1)


def reference(video, responses, assignment, counts, conv_weight, conv_bias, mix_weight, mix_bias, masks, feat_w, readout_bias):
    loss_scale = 1.0 / (CLIPS * FRAMES)

    def one_clip(carried, inputs):
        clip_video, clip_target, session = inputs
        video_pad = jnp.pad(clip_video, ((1, 1), (0, 0)))[None]
        patches, pre1, act1, pre2, feats = core_forward(video_pad, FRAMES, conv_weight, conv_bias, mix_weight, mix_bias)
        pooled = pool_map(feats)
        pooled_flat = pooled[0].reshape(FRAMES * C, -1)
        mask = lax.dynamic_index_in_dim(masks, session, 0, keepdims=False)
        weight = lax.dynamic_index_in_dim(feat_w, session, 0, keepdims=False)
        rbias = lax.dynamic_index_in_dim(readout_bias, session, 0, keepdims=False)
        live_count = lax.dynamic_index_in_dim(counts, session, 0, keepdims=False)
        loss_sum, pooled_grad, mask_grad, feat_grad, bias_grad = readout(pooled_flat, clip_target, mask, weight, rbias, live_count, 0, N, loss_scale)
        pooled_grad = pooled_grad.astype(jnp.bfloat16).reshape(1, FRAMES, C, -1)
        feats_grad = unpool_map(pooled_grad)
        core_parts = core_backward(feats_grad, patches, pre1, act1, pre2, mix_weight)
        new_carry = (carried[0] + loss_sum,
                     carried[1] + core_parts[0], carried[2] + core_parts[1],
                     carried[3] + core_parts[2], carried[4] + core_parts[3],
                     carried[5].at[session].add(mask_grad),
                     carried[6].at[session].add(feat_grad),
                     carried[7].at[session].add(bias_grad))
        return new_carry, None

    start_carry = (jnp.zeros((), jnp.float32),
                   jnp.zeros((C, TAPS), jnp.float32), jnp.zeros((C,), jnp.float32),
                   jnp.zeros((C, C), jnp.float32), jnp.zeros((C,), jnp.float32),
                   jnp.zeros((SESSIONS, N, POOLED), jnp.float32),
                   jnp.zeros((SESSIONS, N, C), jnp.float32),
                   jnp.zeros((SESSIONS, N), jnp.float32))
    final, _ = lax.scan(one_clip, start_carry, (video, responses, assignment.astype(jnp.int32)))
    return (final[0], final[1], final[2], final[3], final[4], final[5], final[6], final[7])
```

```python
import functools

import jax
import jax.numpy as jnp
import numpy as np
from jax import lax
from jax.experimental import pallas as pl
from jax.experimental.pallas import tpu as pltpu
from jax.sharding import PartitionSpec as P

HH = 36
WW = 64
KS = 7
KT = 3
DX = 8
PACK = 256
SEG = 64
BF = jnp.bfloat16
F32 = jnp.float32
NT = (((1,), (1,)), ((), ()))
TN = (((0,), (0,)), ((), ()))


def dot(a, b, dims=(((1,), (0,)), ((), ())), precision=None):
    return lax.dot_general(a, b, dims, precision=precision, preferred_element_type=F32)


def iota(shape, axis):
    return lax.broadcasted_iota(jnp.int32, shape, axis)


def tap_table(frames):
    table = np.zeros((PACK, KS, DX, frames), np.float32)
    for dt in range(KT):
        for dy in range(KS):
            for dx in range(KS):
                table[dt * KS * KS + dy * KS + dx, dy, dx, :] = 1.0
    table[KT * KS * KS, 0, KS, 0] = 1.0
    return table.reshape(PACK, -1).astype(jnp.bfloat16)


def pool_table():
    table = np.zeros((4, 2, WW // 2, 2, 4, WW // 2), np.float32)
    for pair in range(4):
        for col in range(WW // 2):
            table[pair, :, col, :, pair, col] = 0.25
    return table.reshape(8 * WW, 2 * WW).astype(jnp.bfloat16)


def pixel_chunks(pix):
    step = 8 * WW
    return [(p, min(step, pix - p)) for p in range(0, pix, step)]


def mix_blocks(mix, group):
    channels = mix.shape[0]
    size = channels * group
    wide = jnp.concatenate([mix.astype(F32)] * group, axis=1)
    tall = jnp.concatenate([wide] * group, axis=0)
    same = (iota((size, size), 0) // channels) == (iota((size, size), 1) // channels)
    return jnp.where(same, tall, 0.0).astype(BF)


def core_forward_kernel(recv, weight, cbias, mix, mbias, table, pool, pay, act1, slope1, slope2, xcol, pre, feats, wbig):
    frames = recv.shape[0]
    rows, pix = act1.shape
    channels = mix.shape[0]
    neurons = recv.shape[1] - pix
    group = max(1, 256 // channels)
    patch_cols = xcol.shape[0]
    video = recv[:, neurons:].astype(F32)
    lane = iota((frames, pix), 1)
    col = lane % WW
    row = lane // WW
    per_store = max(1, 16 // frames)
    for dx0 in range(0, DX, per_store):
        shifted = []
        for dx in range(dx0, dx0 + per_store):
            s = dx - KS // 2
            if dx == KS:
                shifted.append(None)
            elif s == 0:
                shifted.append(video)
            else:
                rolled = pltpu.roll(video, (-s) % pix, 1)
                shifted.append(jnp.where((col + s >= 0) & (col + s < WW), rolled, 0.0))
        for dy in range(KS):
            t = dy - KS // 2
            parts = []
            for item in shifted:
                if item is None:
                    parts.append(jnp.ones((frames, pix), F32))
                elif t == 0:
                    parts.append(item)
                else:
                    moved = pltpu.roll(item, (-t * WW) % pix, 1)
                    parts.append(jnp.where((row + t >= 0) & (row + t < HH), moved, 0.0))
            base = (dy * DX + dx0) * frames
            block = parts[0] if len(parts) == 1 else jnp.concatenate(parts, axis=0)
            xcol[base : base + per_store * frames, :] = block.astype(BF)
    taps = weight.shape[1]
    tap = iota((channels, taps), 1)
    weights = weight[...].astype(F32)
    split = [
        jnp.where((tap >= dt * KS * KS) & (tap < (dt + 1) * KS * KS), weights, 0.0).astype(BF)
        for dt in range(KT)
    ]
    spread = dot(jnp.concatenate(split, axis=0), table[0:taps, :])
    source = iota((channels, patch_cols), 1) % frames
    for f in range(frames):
        total = jnp.zeros((channels, patch_cols), F32)
        for dt in range(KT):
            total = total + jnp.where(source == f + dt - 1, spread[dt * channels : (dt + 1) * channels], 0.0)
        wbig[f * channels : (f + 1) * channels, :] = total.astype(BF)
    wide = wbig[...]
    for p, size in pixel_chunks(pix):
        pre[:, p : p + size] = dot(wide, xcol[:, p : p + size])

    per_frame = channels // 16

    def first(i, carry):
        r = pl.multiple_of(i * 16, 16)
        b = pl.multiple_of((i % per_frame) * 16, 16)
        x = pre[pl.ds(r, 16), :] + cbias[pl.ds(b, 16), :]
        e = jnp.exp(jnp.minimum(x, 0.0))
        act1[pl.ds(r, 16), :] = (jnp.maximum(x, 0.0) + (e - 1.0)).astype(BF)
        slope1[pl.ds(r, 16), :] = e.astype(BF)
        return carry

    lax.fori_loop(0, rows // 16, first, 0)
    blocks = mix_blocks(mix[...], group)
    span = channels * group
    for r in range(0, rows, span):
        for p, size in pixel_chunks(pix):
            pre[r : r + span, p : p + size] = dot(blocks, act1[r : r + span, p : p + size])

    def second(i, carry):
        r = pl.multiple_of(i * 16, 16)
        b = pl.multiple_of((i % per_frame) * 16, 16)
        x = pre[pl.ds(r, 16), :] + mbias[pl.ds(b, 16), :]
        e = jnp.exp(jnp.minimum(x, 0.0))
        feats[pl.ds(r, 16), :] = (jnp.maximum(x, 0.0) + (e - 1.0)).astype(BF)
        slope2[pl.ds(r, 16), :] = e.astype(BF)
        return carry

    lax.fori_loop(0, rows // 16, second, 0)
    half = 2 * WW
    chunks = pixel_chunks(pix)
    for p, size in chunks[:-1]:
        pay[:, p // 4 : p // 4 + half] = dot(feats[:, p : p + size], pool[...]).astype(BF)
    p, size = chunks[-1]
    tail = dot(feats[:, p : p + size], pool[0:size, :])
    pieces = []
    for t in range(neurons // half):
        tile = recv[:, t * half : (t + 1) * half].astype(F32)
        pieces += [pltpu.roll(tile, SEG, 1), tile]
    packed = jnp.concatenate(pieces, axis=0)
    pay[:, p // 4 : p // 4 + half] = jnp.where(iota((rows, half), 1) < SEG, tail, packed).astype(BF)


def drive_terms(projected, target, w, rbias, alive, scale, channels):
    frames = target.shape[0]
    sums = [
        jnp.sum(projected[f * channels : (f + 1) * channels] * w, axis=0, keepdims=True)
        for f in range(frames)
    ]
    drive = jnp.concatenate(sums, axis=0) + rbias
    e = jnp.exp(-jnp.abs(drive))
    rate = jnp.maximum(drive, 0.0) + jnp.log(1.0 + e) + 0.1
    sig = jnp.where(drive >= 0, 1.0, e) / (1.0 + e)
    grad = jnp.where(alive, (1.0 - target / rate) * sig, 0.0) * scale
    return rate, grad


def mixed_rows(grad, w):
    frames = grad.shape[0]
    return jnp.concatenate([grad[f : f + 1] * w for f in range(frames)], axis=0).astype(BF)


def readout_kernel(scale, count, recv, pay, mask, wt, rbias, pooled_grad, loss, acc, loss_acc):
    i = pl.program_id(0)
    block = mask.shape[1]
    pooled_n = mask.shape[2]
    channels = wt.shape[0]
    frames = recv.shape[0]

    @pl.when(i == 0)
    def _():
        acc[...] = jnp.zeros_like(acc)
        loss_acc[...] = jnp.zeros_like(loss_acc)

    w = wt[...].astype(F32)
    m = mask[0]
    projected = dot(pay[:, 0:pooled_n], m, NT)
    target = recv[...].astype(F32)
    alive = (i * block + iota((frames, block), 1)) < count[0]
    rate, grad = drive_terms(projected, target, w, rbias[...], alive, scale, channels)
    loss_acc[...] += jnp.where(alive, rate - target * jnp.log(rate), 0.0)
    acc[...] += dot(mixed_rows(grad, w), m)

    @pl.when(i == pl.num_programs(0) - 1)
    def _():
        pooled_grad[...] = acc[...].astype(BF)
        loss[...] = jnp.broadcast_to(jnp.sum(loss_acc[...], keepdims=True) * scale, loss.shape)


def core_backward_kernel(pooled_grad, loss, act1, slope1, slope2, xcol, mix, table, unpool, out, grad, g2, g1):
    rows, pix = act1.shape
    channels = mix.shape[0]
    frames = rows // channels
    group = max(1, 256 // channels)
    span = channels * group
    patch_cols = xcol.shape[0]
    per_frame = channels // 16
    for p, size in pixel_chunks(pix):
        grad[:, p : p + size] = dot(pooled_grad[:, p // 4 : (p + size) // 4], unpool[0 : size // 4, 0:size])

    sums = []
    for q in range(per_frame):

        def second(f, total):
            r = pl.multiple_of(f * channels + q * 16, 16)
            g = (grad[pl.ds(r, 16), :] * slope2[pl.ds(r, 16), :].astype(F32)).astype(BF)
            g2[pl.ds(r, 16), :] = g
            return total + jnp.sum(g.astype(F32), axis=1, keepdims=True)

        sums.append(lax.fori_loop(0, frames, second, jnp.zeros((16, 1), F32)))
    mix_bias_grad = jnp.concatenate(sums, axis=0)
    blocks = mix_blocks(mix[...], group)
    mix_grad = jnp.zeros((channels, span), F32)
    same = (iota((span, span), 0) // channels) == (iota((span, span), 1) // channels)
    for r in range(0, rows, span):
        full = jnp.where(same, dot(g2[r : r + span, :], act1[r : r + span, :], NT), 0.0)
        for a in range(group):
            mix_grad = mix_grad + full[a * channels : (a + 1) * channels]
        for p, size in pixel_chunks(pix):
            grad[r : r + span, p : p + size] = dot(blocks, g2[r : r + span, p : p + size], TN)
    half = 2 * channels
    folded = mix_grad[:, 0:half]
    for k in range(half, span, half):
        folded = folded + mix_grad[:, k : k + half]
    folded = folded + pltpu.roll(folded, channels, 1)

    def first(i, carry):
        r = pl.multiple_of(i * 16, 16)
        g1[pl.ds(r, 16), :] = (grad[pl.ds(r, 16), :] * slope1[pl.ds(r, 16), :].astype(F32)).astype(BF)
        return carry

    lax.fori_loop(0, rows // 16, first, 0)
    full = dot(g1[...], xcol[...], NT)
    source = iota((channels, patch_cols), 1) % frames
    parts = [jnp.zeros((channels, patch_cols), F32) for _ in range(KT + 1)]
    for f in range(frames):
        piece = full[f * channels : (f + 1) * channels]
        for dt in range(KT):
            parts[dt] = parts[dt] + jnp.where(source == f + dt - 1, piece, 0.0)
        parts[KT] = parts[KT] + piece
    taps = dot(
        jnp.concatenate(parts, axis=0), table[...].astype(F32), NT, precision=lax.Precision.HIGHEST
    )
    lane = iota((channels, PACK), 1)
    conv = jnp.zeros((channels, PACK), F32)
    for dt in range(KT + 1):
        inside = (lane >= dt * KS * KS) & (lane < (dt + 1) * KS * KS)
        conv = conv + jnp.where(inside, taps[dt * channels : (dt + 1) * channels], 0.0)
    used = KT * KS * KS + 1
    low = lane[:, 0:128]
    out[:, 0:128] = conv[:, 0:128]
    upper = jnp.where(low < used - 128, conv[:, 128:256], 0.0)
    upper = jnp.where(low == used - 128, mix_bias_grad, upper)
    upper = jnp.where((low == used - 127) & (iota((channels, 128), 0) == 0), loss[0:1, 0:1], upper)
    out[:, 128:256] = jnp.where(low >= channels, folded, upper)


def owned_rows_kernel(scale, where, count, *refs):
    clips = len(refs) - 6
    pays = refs[:clips]
    mask, wt, rbias, mask_grad, feat_grad, bias_grad = refs[clips:]
    i = pl.program_id(0)
    block = mask.shape[1]
    pooled_n = mask.shape[2]
    channels = wt.shape[0]
    frames = pays[0].shape[0] // channels
    first = (where[0] * pl.num_programs(0) + i) * block
    m = mask[0]
    w = wt[...].astype(F32)
    alive = (first + iota((frames, block), 1)) < count[0]
    total = None
    feat = jnp.zeros((channels, block), F32)
    bias = jnp.zeros((frames, block), F32)
    segs = block // SEG
    base = pl.multiple_of(first // SEG * frames, segs * frames)
    low = iota((frames, 128), 1) < SEG
    for pay in pays:
        pooled = pay[:, 0:pooled_n]
        held = pay[pl.ds(base, segs * frames), pooled_n - SEG : pooled_n + SEG].astype(F32)
        tiles = []
        for j in range(0, segs, 2):
            even = held[j * frames : (j + 1) * frames]
            odd = held[(j + 1) * frames : (j + 2) * frames]
            tiles.append(jnp.where(low, pltpu.roll(even, SEG, 1), odd))
        target = jnp.concatenate(tiles, axis=1)
        projected = dot(pooled, m, NT)
        _, grad = drive_terms(projected, target, w, rbias[...], alive, scale, channels)
        for f in range(frames):
            feat = feat + grad[f : f + 1] * projected[f * channels : (f + 1) * channels]
        bias = bias + grad
        part = dot(mixed_rows(grad, w), pooled, TN)
        total = part if total is None else total + part
    mask_grad[0] = total
    feat_grad[0] = feat.T
    bias_grad[...] = jnp.sum(bias, axis=0, keepdims=True)


def params(limit=48):
    return pltpu.CompilerParams(vmem_limit_bytes=limit << 20)


def xor_pairs(size, mask):
    return [(i, i ^ mask) for i in range(size)]


def per_device(
    video, responses, assignment, counts, conv_weight, conv_bias, mix_weight, mix_bias, masks, feat_w, readout_bias
):
    sess_total = lax.axis_size("sess")
    clip_total = lax.axis_size("clip")
    total = sess_total * clip_total
    clip_block, frame_block, pix = video.shape
    neurons = responses.shape[2]
    pooled_n = masks.shape[2]
    channels, taps = conv_weight.shape
    frames = frame_block * sess_total
    rows = frames * channels
    own = neurons // clip_total
    block = min(512, own)
    assert clip_block == sess_total and frame_block == 1 and masks.shape[0] == 1
    assert neurons == channels * SEG and pooled_n % 128 == SEG and pix == HH * WW
    scale = 1.0 / (clip_block * clip_total * frames)

    sessions = lax.broadcasted_iota(jnp.int32, (sess_total, clip_block), 0)
    pick = (sessions == assignment[None, :]).astype(BF)
    both = jnp.concatenate([responses[:, 0, :], video[:, 0, :]], axis=1)
    send = jnp.dot(pick, both, preferred_element_type=F32).astype(BF)
    recv = lax.all_to_all(send, "sess", split_axis=0, concat_axis=0, tiled=True)

    table = jnp.asarray(tap_table(frames))
    pool = jnp.asarray(pool_table())
    unpool = jnp.asarray(pool_table().T)
    wt = feat_w[0].T
    patch_cols = KS * DX * frames
    width = pooled_n + SEG
    pay, act1, slope1, slope2, xcol = pl.pallas_call(
        core_forward_kernel,
        out_shape=(
            jax.ShapeDtypeStruct((rows, width), BF),
            jax.ShapeDtypeStruct((rows, pix), BF),
            jax.ShapeDtypeStruct((rows, pix), BF),
            jax.ShapeDtypeStruct((rows, pix), BF),
            jax.ShapeDtypeStruct((patch_cols, pix), BF),
        ),
        scratch_shapes=[
            pltpu.VMEM((rows, pix), F32),
            pltpu.VMEM((rows, pix), BF),
            pltpu.VMEM((rows, patch_cols), BF),
        ],
        compiler_params=params(),
        name="core_forward",
    )(recv, conv_weight, conv_bias[:, None], mix_weight, mix_bias[:, None], table, pool)

    pays = [pay]
    for mask in range(1, clip_total):
        if mask % 2 == 0 or mask == 1:
            pays.append(lax.ppermute(pay, "clip", xor_pairs(clip_total, mask)))
        else:
            pays.append(lax.ppermute(pays[mask - 1], "clip", xor_pairs(clip_total, 1)))

    smem = pl.BlockSpec(memory_space=pltpu.SMEM)
    big = min(512, neurons)
    pooled_grad, loss = pl.pallas_call(
        functools.partial(readout_kernel, scale),
        grid=(neurons // big,),
        in_specs=[
            smem,
            pl.BlockSpec((frames, big), lambda i: (0, i)),
            pl.BlockSpec((rows, width), lambda i: (0, 0)),
            pl.BlockSpec((1, big, pooled_n), lambda i: (0, i, 0)),
            pl.BlockSpec((channels, big), lambda i: (0, i)),
            pl.BlockSpec((1, big), lambda i: (0, i)),
        ],
        out_specs=(
            pl.BlockSpec((rows, pooled_n), lambda i: (0, 0)),
            pl.BlockSpec((8, 128), lambda i: (0, 0)),
        ),
        out_shape=(jax.ShapeDtypeStruct((rows, pooled_n), BF), jax.ShapeDtypeStruct((8, 128), F32)),
        scratch_shapes=[pltpu.VMEM((rows, pooled_n), F32), pltpu.VMEM((frames, big), F32)],
        compiler_params=params(),
        name="readout",
    )(counts, recv, pay, masks, wt, readout_bias)

    core = pl.pallas_call(
        core_backward_kernel,
        out_shape=jax.ShapeDtypeStruct((channels, PACK), F32),
        scratch_shapes=[
            pltpu.VMEM((rows, pix), F32),
            pltpu.VMEM((rows, pix), BF),
            pltpu.VMEM((rows, pix), BF),
        ],
        compiler_params=params(),
        name="core_backward",
    )(pooled_grad, loss, act1, slope1, slope2, xcol, mix_weight, table, unpool)

    axes = ("clip", "sess")
    flat = core.reshape(total, -1)
    mine = jnp.sum(lax.all_to_all(flat, axes, split_axis=0, concat_axis=0, tiled=True), axis=0)
    copies = jnp.broadcast_to(mine[None], (total, mine.shape[0]))
    summed = lax.all_to_all(copies, axes, split_axis=0, concat_axis=0, tiled=True).reshape(channels, PACK)

    where = lax.axis_index("clip").astype(jnp.int32)[None]
    steps = own // block
    grad_masks, grad_feat, grad_rbias = pl.pallas_call(
        functools.partial(owned_rows_kernel, scale),
        grid_spec=pltpu.PrefetchScalarGridSpec(
            num_scalar_prefetch=1,
            grid=(steps,),
            in_specs=[smem]
            + [pl.BlockSpec((rows, width), lambda i, at: (0, 0)) for _ in pays]
            + [
                pl.BlockSpec((1, block, pooled_n), lambda i, at: (0, at[0] * steps + i, 0)),
                pl.BlockSpec((channels, block), lambda i, at: (0, at[0] * steps + i)),
                pl.BlockSpec((1, block), lambda i, at: (0, at[0] * steps + i)),
            ],
            out_specs=(
                pl.BlockSpec((1, block, pooled_n), lambda i, at: (0, i, 0)),
                pl.BlockSpec((1, block, channels), lambda i, at: (0, i, 0)),
                pl.BlockSpec((1, block), lambda i, at: (0, i)),
            ),
        ),
        out_shape=(
            jax.ShapeDtypeStruct((1, own, pooled_n), F32),
            jax.ShapeDtypeStruct((1, own, channels), F32),
            jax.ShapeDtypeStruct((1, own), F32),
        ),
        compiler_params=params(),
        name="owned_rows",
    )(where, counts, *pays, masks, wt, readout_bias)

    used = taps + 1
    return (
        summed[0, used + 1],
        summed[:, :taps],
        summed[:, taps],
        summed[:, PACK - channels :],
        summed[:, used],
        grad_masks,
        grad_feat,
        grad_rbias,
    )


def solution(mesh):
    return jax.shard_map(
        per_device,
        mesh=mesh,
        in_specs=(
            P("clip", "sess", None),
            P("clip", "sess", None),
            P("clip"),
            P("sess"),
            P(),
            P(),
            P(),
            P(),
            P("sess", None, None),
            P("sess", None, None),
            P("sess", None),
        ),
        out_specs=(
            P(),
            P(),
            P(),
            P(),
            P(),
            P("sess", "clip", None),
            P("sess", "clip", None),
            P("sess", "clip"),
        ),
        check_vma=False,
    )
```

```python
import functools

import jax
import jax.numpy as jnp
from jax import lax
from jax.experimental import pallas as pl
from jax.experimental.pallas import tpu as pltpu
from jax.sharding import PartitionSpec as P

HH = 36
WW = 64
KS = 7
KT = 3
DX = 8
PACK = 256
SEG = 64
BF = jnp.bfloat16
F32 = jnp.float32
NT = (((1,), (1,)), ((), ()))
TN = (((0,), (0,)), ((), ()))


def dot(a, b, dims=(((1,), (0,)), ((), ())), precision=None):
    return lax.dot_general(a, b, dims, precision=precision, preferred_element_type=F32)


def iota(shape, axis):
    return lax.broadcasted_iota(jnp.int32, shape, axis)


def pixel_chunks(pix):
    step = 8 * WW
    return [(p, min(step, pix - p)) for p in range(0, pix, step)]


def bias_column(row):
    size = row.shape[1]
    return jnp.sum(jnp.where(iota((size, size), 0) == iota((size, size), 1), row, 0.0), axis=1, keepdims=True)


def select_kernel(assign, video, responses, out):
    owners, lines, width = out.shape
    clips, pix = video.shape
    neurons = responses.shape[1]
    pick = (iota((owners, clips), 0) == assign[...]).astype(BF)
    first = dot(pick, responses[...])
    second = dot(pick, video[...])
    rows = [first[:, p : p + width] for p in range(0, neurons, width)]
    for p in range(0, pix, width):
        piece = second[:, p : p + width]
        if piece.shape[1] < width:
            piece = jnp.concatenate([piece, jnp.zeros((owners, width - piece.shape[1]), F32)], axis=1)
        rows.append(piece)
    while len(rows) < lines:
        rows.append(jnp.zeros((owners, width), F32))
    out[...] = jnp.stack(rows, axis=1).astype(BF)


def prep_kernel(frames, weight, cbias, mix, mbias, wbig, blocks, blocks_t, bias, table, pool, unpool):
    channels, taps = weight.shape
    patch_cols = wbig.shape[1]
    group = blocks.shape[0] // channels
    t = iota(table.shape, 0)
    l = iota(table.shape, 1)
    dy = l // (DX * frames)
    dx = (l // frames) % DX
    place = dy * KS + dx
    hit = (t == place) | (t == place + KS * KS) | (t == place + 2 * KS * KS)
    last = (t == KT * KS * KS) & (l == KS * frames)
    table[...] = jnp.where(((dx < KS) & hit & (t < KT * KS * KS)) | last, 1.0, 0.0).astype(BF)
    r = iota(pool.shape, 0)
    c = iota(pool.shape, 1)
    target = (r // (2 * WW)) * (WW // 2) + (r % WW) // 2
    pool[...] = jnp.where(target == c, 0.25, 0.0).astype(BF)
    r = iota(unpool.shape, 1)
    c = iota(unpool.shape, 0)
    target = (r // (2 * WW)) * (WW // 2) + (r % WW) // 2
    unpool[...] = jnp.where(target == c, 0.25, 0.0).astype(BF)
    size = channels * group
    same = (iota((size, size), 0) // channels) == (iota((size, size), 1) // channels)
    square = mix[...].astype(F32)
    for ref, base in ((blocks, square), (blocks_t, square.T)):
        wide = jnp.concatenate([base] * group, axis=1)
        ref[...] = jnp.where(same, jnp.concatenate([wide] * group, axis=0), 0.0).astype(BF)
    lane = iota(bias.shape, 1)
    bias[...] = jnp.where(lane == 0, bias_column(cbias[...]), bias_column(mbias[...]))
    tap = iota((channels, taps), 1)
    weights = weight[...].astype(F32)
    split = [
        jnp.where((tap >= dt * KS * KS) & (tap < (dt + 1) * KS * KS), weights, 0.0).astype(BF)
        for dt in range(KT)
    ]
    spread = dot(jnp.concatenate(split, axis=0), table[0:taps, :])
    source = iota((channels, patch_cols), 1) % frames
    for f in range(frames):
        total = jnp.zeros((channels, patch_cols), F32)
        for dt in range(KT):
            total = total + jnp.where(source == f + dt - 1, spread[dt * channels : (dt + 1) * channels], 0.0)
        wbig[f * channels : (f + 1) * channels, :] = total.astype(BF)


def core_forward_kernel(recv, wbig, blocks, bias, pool, pay, target, act1, slope1, slope2, xcol, pre, feats):
    frames, _, width = recv.shape
    rows, pix = act1.shape
    channels = bias.shape[0]
    neurons = target.shape[1]
    span = blocks.shape[0]
    packet = recv[...].astype(F32)
    lines = [packet[:, j, :] for j in range((neurons + pix + width - 1) // width)]
    held = neurons // width
    for j in range(held):
        target[:, j * width : (j + 1) * width] = lines[j]
    video = jnp.concatenate(lines[held:], axis=1)[:, 0:pix]
    lane = iota((frames, pix), 1)
    col = lane % WW
    row = lane // WW
    per_store = max(1, 16 // frames)
    for dx0 in range(0, DX, per_store):
        shifted = []
        for dx in range(dx0, dx0 + per_store):
            s = dx - KS // 2
            if dx == KS:
                shifted.append(None)
            elif s == 0:
                shifted.append(video)
            else:
                rolled = pltpu.roll(video, (-s) % pix, 1)
                shifted.append(jnp.where((col + s >= 0) & (col + s < WW), rolled, 0.0))
        for dy in range(KS):
            t = dy - KS // 2
            parts = []
            for item in shifted:
                if item is None:
                    parts.append(jnp.ones((frames, pix), F32))
                elif t == 0:
                    parts.append(item)
                else:
                    moved = pltpu.roll(item, (-t * WW) % pix, 1)
                    parts.append(jnp.where((row + t >= 0) & (row + t < HH), moved, 0.0))
            base = (dy * DX + dx0) * frames
            block = parts[0] if len(parts) == 1 else jnp.concatenate(parts, axis=0)
            xcol[base : base + per_store * frames, :] = block.astype(BF)
    wide = wbig[...]
    for p, size in pixel_chunks(pix):
        pre[:, p : p + size] = dot(wide, xcol[:, p : p + size])

    per_frame = channels // 16

    def first(i, carry):
        r = pl.multiple_of(i * 16, 16)
        b = pl.multiple_of((i % per_frame) * 16, 16)
        x = pre[pl.ds(r, 16), :] + bias[pl.ds(b, 16), 0:1]
        e = jnp.exp(jnp.minimum(x, 0.0))
        act1[pl.ds(r, 16), :] = (jnp.maximum(x, 0.0) + (e - 1.0)).astype(BF)
        slope1[pl.ds(r, 16), :] = e.astype(BF)
        return carry

    lax.fori_loop(0, rows // 16, first, 0)
    for r in range(0, rows, span):
        for p, size in pixel_chunks(pix):
            pre[r : r + span, p : p + size] = dot(blocks[...], act1[r : r + span, p : p + size])

    def second(i, carry):
        r = pl.multiple_of(i * 16, 16)
        b = pl.multiple_of((i % per_frame) * 16, 16)
        x = pre[pl.ds(r, 16), :] + bias[pl.ds(b, 16), 1:2]
        e = jnp.exp(jnp.minimum(x, 0.0))
        feats[pl.ds(r, 16), :] = (jnp.maximum(x, 0.0) + (e - 1.0)).astype(BF)
        slope2[pl.ds(r, 16), :] = e.astype(BF)
        return carry

    lax.fori_loop(0, rows // 16, second, 0)
    half = 2 * WW
    chunks = pixel_chunks(pix)
    for p, size in chunks[:-1]:
        pay[:, p // 4 : p // 4 + half] = dot(feats[:, p : p + size], pool[...]).astype(BF)
    p, size = chunks[-1]
    tail = dot(feats[:, p : p + size], pool[0:size, :])
    pieces = []
    for t in range(neurons // half):
        at = t * half
        tile = lines[at // width][:, at % width : at % width + half]
        pieces += [pltpu.roll(tile, SEG, 1), tile]
    packed = jnp.concatenate(pieces, axis=0)
    pay[:, p // 4 : p // 4 + half] = jnp.where(iota((rows, half), 1) < SEG, tail, packed).astype(BF)


def drive_terms(projected, target, w, rbias, alive, scale, channels):
    frames = target.shape[0]
    sums = [
        jnp.sum(projected[f * channels : (f + 1) * channels] * w, axis=0, keepdims=True)
        for f in range(frames)
    ]
    drive = jnp.concatenate(sums, axis=0) + rbias
    e = jnp.exp(-jnp.abs(drive))
    rate = jnp.maximum(drive, 0.0) + jnp.log(1.0 + e) + 0.1
    sig = jnp.where(drive >= 0, 1.0, e) / (1.0 + e)
    grad = jnp.where(alive, (1.0 - target / rate) * sig, 0.0) * scale
    return rate, grad


def mixed_rows(grad, w):
    frames = grad.shape[0]
    return jnp.concatenate([grad[f : f + 1] * w for f in range(frames)], axis=0).astype(BF)


def readout_kernel(scale, count, target, pay, mask, wt, rbias, pooled_grad, loss, acc, loss_acc):
    i = pl.program_id(0)
    pooled_n, block = mask.shape
    channels = wt.shape[0]
    frames = target.shape[0]

    @pl.when(i == 0)
    def _():
        acc[...] = jnp.zeros_like(acc)
        loss_acc[...] = jnp.zeros_like(loss_acc)

    w = wt[...].astype(F32)
    m = mask[...]
    projected = dot(pay[:, 0:pooled_n], m)
    alive = (i * block + iota((frames, block), 1)) < count[0]
    rate, grad = drive_terms(projected, target[...], w, rbias[...], alive, scale, channels)
    loss_acc[...] += jnp.where(alive, rate - target[...] * jnp.log(rate), 0.0)
    acc[...] += dot(mixed_rows(grad, w), m, NT)

    @pl.when(i == pl.num_programs(0) - 1)
    def _():
        pooled_grad[...] = acc[...].astype(BF)
        loss[...] = jnp.broadcast_to(jnp.sum(loss_acc[...], keepdims=True) * scale, loss.shape)


def core_backward_kernel(
    channels, pooled_grad, loss, act1, slope1, slope2, xcol, blocks_t, table, unpool, out, grad, g2, g1
):
    rows, pix = act1.shape
    frames = rows // channels
    span = blocks_t.shape[0]
    group = span // channels
    patch_cols = xcol.shape[0]
    per_frame = channels // 16
    for p, size in pixel_chunks(pix):
        grad[:, p : p + size] = dot(pooled_grad[:, p // 4 : (p + size) // 4], unpool[0 : size // 4, 0:size])

    sums = []
    for q in range(per_frame):

        def second(f, total):
            r = pl.multiple_of(f * channels + q * 16, 16)
            g = (grad[pl.ds(r, 16), :] * slope2[pl.ds(r, 16), :].astype(F32)).astype(BF)
            g2[pl.ds(r, 16), :] = g
            return total + jnp.sum(g.astype(F32), axis=1, keepdims=True)

        sums.append(lax.fori_loop(0, frames, second, jnp.zeros((16, 1), F32)))
    mix_bias_grad = jnp.concatenate(sums, axis=0)
    mix_grad = jnp.zeros((channels, span), F32)
    same = (iota((span, span), 0) // channels) == (iota((span, span), 1) // channels)
    for r in range(0, rows, span):
        full = jnp.where(same, dot(g2[r : r + span, :], act1[r : r + span, :], NT), 0.0)
        for a in range(group):
            mix_grad = mix_grad + full[a * channels : (a + 1) * channels]
        for p, size in pixel_chunks(pix):
            grad[r : r + span, p : p + size] = dot(blocks_t[...], g2[r : r + span, p : p + size])
    half = 2 * channels
    folded = mix_grad[:, 0:half]
    for k in range(half, span, half):
        folded = folded + mix_grad[:, k : k + half]
    folded = folded + pltpu.roll(folded, channels, 1)

    def first(i, carry):
        r = pl.multiple_of(i * 16, 16)
        g1[pl.ds(r, 16), :] = (grad[pl.ds(r, 16), :] * slope1[pl.ds(r, 16), :].astype(F32)).astype(BF)
        return carry

    lax.fori_loop(0, rows // 16, first, 0)
    full = dot(g1[...], xcol[...], NT)
    source = iota((channels, patch_cols), 1) % frames
    parts = [jnp.zeros((channels, patch_cols), F32) for _ in range(KT + 1)]
    for f in range(frames):
        piece = full[f * channels : (f + 1) * channels]
        for dt in range(KT):
            parts[dt] = parts[dt] + jnp.where(source == f + dt - 1, piece, 0.0)
        parts[KT] = parts[KT] + piece
    taps = dot(
        jnp.concatenate(parts, axis=0), table[...].astype(F32), NT, precision=lax.Precision.HIGHEST
    )
    lane = iota((channels, PACK), 1)
    conv = jnp.zeros((channels, PACK), F32)
    for dt in range(KT + 1):
        inside = (lane >= dt * KS * KS) & (lane < (dt + 1) * KS * KS)
        conv = conv + jnp.where(inside, taps[dt * channels : (dt + 1) * channels], 0.0)
    used = KT * KS * KS + 1
    low = lane[:, 0:128]
    upper = jnp.where(low < used - 128, conv[:, 128:256], 0.0)
    upper = jnp.where(low == used - 128, mix_bias_grad, upper)
    upper = jnp.where((low == used - 127) & (iota((channels, 128), 0) == 0), loss[0:1, 0:1], upper)
    upper = jnp.where(low >= channels, folded, upper)
    tiles = channels // 8
    out[...] = jnp.zeros_like(out)
    for i in range(tiles):
        out[i] = conv[8 * i : 8 * i + 8, 0:128]
        out[tiles + i] = upper[8 * i : 8 * i + 8, :]


def share_kernel(total, parts, out):
    each = parts.shape[0] // total
    for k in range(each):
        tile = parts[k]
        for d in range(1, total):
            tile = tile + parts[d * each + k]
        for d in range(total):
            out[d * each + k] = tile


def unpack_kernel(parts, conv, conv_bias, mix, mix_bias, loss):
    channels, taps = conv.shape
    tiles = channels // 8
    low = jnp.concatenate([parts[i] for i in range(tiles)], axis=0)
    high = jnp.concatenate([parts[tiles + i] for i in range(tiles)], axis=0)
    rest = taps - 128
    conv[...] = jnp.concatenate([low, high], axis=1)[:, 0:taps]
    mix[...] = pltpu.roll(high, 128 - channels, 1)[:, 0:channels]
    same = iota((channels, channels), 0) == iota((channels, channels), 1)
    conv_bias[...] = jnp.sum(jnp.where(same, high[:, rest : rest + 1], 0.0), axis=0, keepdims=True)
    mix_bias[...] = jnp.sum(jnp.where(same, high[:, rest + 1 : rest + 2], 0.0), axis=0, keepdims=True)
    loss[...] = high[0:1, rest + 2 : rest + 3]


def owned_rows_kernel(scale, where, count, *refs):
    clips = len(refs) - 6
    pays = refs[:clips]
    mask, wt, rbias, mask_grad, feat_grad, bias_grad = refs[clips:]
    i = pl.program_id(0)
    pooled_n, block = mask.shape
    channels = wt.shape[0]
    frames = pays[0].shape[0] // channels
    first = (where[0] * pl.num_programs(0) + i) * block
    m = mask[...]
    w = wt[...].astype(F32)
    alive = (first + iota((frames, block), 1)) < count[0]
    total = None
    feat = jnp.zeros((channels, block), F32)
    bias = jnp.zeros((frames, block), F32)
    segs = block // SEG
    base = pl.multiple_of(first // SEG * frames, segs * frames)
    low = iota((frames, 128), 1) < SEG
    for pay in pays:
        pooled = pay[:, 0:pooled_n]
        held = pay[pl.ds(base, segs * frames), pooled_n - SEG : pooled_n + SEG].astype(F32)
        tiles = []
        for j in range(0, segs, 2):
            even = held[j * frames : (j + 1) * frames]
            odd = held[(j + 1) * frames : (j + 2) * frames]
            tiles.append(jnp.where(low, pltpu.roll(even, SEG, 1), odd))
        target = jnp.concatenate(tiles, axis=1)
        projected = dot(pooled, m)
        _, grad = drive_terms(projected, target, w, rbias[...], alive, scale, channels)
        for f in range(frames):
            feat = feat + grad[f : f + 1] * projected[f * channels : (f + 1) * channels]
        bias = bias + grad
        part = dot(pooled, mixed_rows(grad, w), TN)
        total = part if total is None else total + part
    mask_grad[...] = total
    feat_grad[...] = feat
    bias_grad[...] = jnp.sum(bias, axis=0, keepdims=True)


def params(limit=40):
    return pltpu.CompilerParams(vmem_limit_bytes=limit << 20)


def cost(flops, moved=1 << 20):
    return pl.CostEstimate(flops=int(flops), transcendentals=0, bytes_accessed=int(moved))


def in_hbm(*arrays):
    return [pltpu.with_memory_space_constraint(a, pltpu.HBM) for a in arrays]


def xor_pairs(size, mask):
    return [(i, i ^ mask) for i in range(size)]


def per_device(
    video, responses, assignment, counts, conv_weight, conv_bias, mix_weight, mix_bias, masks, feat_w, readout_bias
):
    sess_total = lax.axis_size("sess")
    clip_total = lax.axis_size("clip")
    total = sess_total * clip_total
    clip_block, frame_block, pix = video.shape
    neurons = responses.shape[2]
    pooled_n = masks.shape[2]
    channels, taps = conv_weight.shape
    frames = frame_block * sess_total
    rows = frames * channels
    own = neurons // clip_total
    block = min(512, own)
    assert clip_block == sess_total and frame_block == 1 and masks.shape[0] == 1
    assert neurons == channels * SEG and pooled_n % 128 == SEG and pix == HH * WW
    scale = 1.0 / (clip_block * clip_total * frames)

    group = max(1, 256 // channels)
    lines = 16
    packet = 512
    assert neurons + pix <= lines * packet
    send = pl.pallas_call(
        select_kernel,
        out_shape=jax.ShapeDtypeStruct((sess_total, lines, packet), BF),
        compiler_params=params(),
        name="select",
    )(*in_hbm(assignment[None, :], video.reshape(clip_block, pix), responses.reshape(clip_block, neurons)))
    recv = lax.all_to_all(send, "sess", split_axis=0, concat_axis=0, tiled=True)

    patch_cols = KS * DX * frames
    span = channels * group
    half = 2 * WW
    wbig, blocks, blocks_t, bias, table, pool, unpool = pl.pallas_call(
        functools.partial(prep_kernel, frames),
        out_shape=(
            jax.ShapeDtypeStruct((rows, patch_cols), BF),
            jax.ShapeDtypeStruct((span, span), BF),
            jax.ShapeDtypeStruct((span, span), BF),
            jax.ShapeDtypeStruct((channels, 128), F32),
            jax.ShapeDtypeStruct((PACK, patch_cols), BF),
            jax.ShapeDtypeStruct((4 * half, half), BF),
            jax.ShapeDtypeStruct((half, 4 * half), BF),
        ),
        compiler_params=params(),
        cost_estimate=cost(1 << 27),
        name="prep",
    )(*in_hbm(conv_weight, conv_bias[None, :], mix_weight, mix_bias[None, :]))

    wt = jnp.swapaxes(feat_w, 1, 2).reshape(channels, neurons)
    mask_t = jnp.swapaxes(masks, 1, 2).reshape(pooled_n, neurons)
    mask_t, wt, rbias = in_hbm(mask_t, wt, readout_bias)
    width = pooled_n + SEG
    pay, target, act1, slope1, slope2, xcol = pl.pallas_call(
        core_forward_kernel,
        out_shape=(
            jax.ShapeDtypeStruct((rows, width), BF),
            jax.ShapeDtypeStruct((frames, neurons), F32),
            jax.ShapeDtypeStruct((rows, pix), BF),
            jax.ShapeDtypeStruct((rows, pix), BF),
            jax.ShapeDtypeStruct((rows, pix), BF),
            jax.ShapeDtypeStruct((patch_cols, pix), BF),
        ),
        scratch_shapes=[pltpu.VMEM((rows, pix), F32), pltpu.VMEM((rows, pix), BF)],
        compiler_params=params(),
        cost_estimate=cost(2 * rows * pix * patch_cols, 8 * rows * pix),
        name="core_forward",
    )(recv, wbig, blocks, bias, pool)

    near = {0: pay}
    for mask in range(1, clip_total):
        if mask % 2 == 0 or mask == 1:
            near[mask] = lax.ppermute(pay, "clip", xor_pairs(clip_total, mask))

    smem = pl.BlockSpec(memory_space=pltpu.SMEM)
    big = min(512, neurons)
    work = 2 * rows * neurons * pooled_n
    pooled_grad, loss = pl.pallas_call(
        functools.partial(readout_kernel, scale),
        grid=(neurons // big,),
        in_specs=[
            smem,
            pl.BlockSpec((frames, big), lambda i: (0, i)),
            pl.BlockSpec((rows, width), lambda i: (0, 0)),
            pl.BlockSpec((pooled_n, big), lambda i: (0, i)),
            pl.BlockSpec((channels, big), lambda i: (0, i)),
            pl.BlockSpec((1, big), lambda i: (0, i)),
        ],
        out_specs=(
            pl.BlockSpec((rows, pooled_n), lambda i: (0, 0)),
            pl.BlockSpec((8, 128), lambda i: (0, 0)),
        ),
        out_shape=(jax.ShapeDtypeStruct((rows, pooled_n), BF), jax.ShapeDtypeStruct((8, 128), F32)),
        scratch_shapes=[pltpu.VMEM((rows, pooled_n), F32), pltpu.VMEM((frames, big), F32)],
        compiler_params=params(),
        cost_estimate=cost(2 * work, 2 * neurons * pooled_n),
        name="readout",
    )(counts, target, pay, mask_t, wt, rbias)

    pieces = total * max(1, (2 * channels // 8) // total)
    core = pl.pallas_call(
        functools.partial(core_backward_kernel, channels),
        out_shape=jax.ShapeDtypeStruct((pieces, 8, 128), F32),
        scratch_shapes=[
            pltpu.VMEM((rows, pix), F32),
            pltpu.VMEM((rows, pix), BF),
            pltpu.VMEM((rows, pix), BF),
        ],
        compiler_params=params(),
        cost_estimate=cost(2 * work, 8 * rows * pix),
        name="core_backward",
    )(pooled_grad, loss, act1, slope1, slope2, xcol, blocks_t, table, unpool)

    far = [mask for mask in near if mask > 1]
    held, core = lax.optimization_barrier(([near[mask] for mask in far], core))
    pays = [near[0], near[1]]
    for mask, value in zip(far, held):
        pays += [value, lax.ppermute(value, "clip", xor_pairs(clip_total, 1))]

    axes = ("clip", "sess")
    parts = lax.all_to_all(core, axes, split_axis=0, concat_axis=0, tiled=True)

    where = lax.axis_index("clip").astype(jnp.int32)[None]
    steps = own // block
    mask_grad, feat_grad, grad_rbias = pl.pallas_call(
        functools.partial(owned_rows_kernel, scale),
        grid_spec=pltpu.PrefetchScalarGridSpec(
            num_scalar_prefetch=1,
            grid=(steps,),
            in_specs=[smem]
            + [pl.BlockSpec((rows, width), lambda i, at: (0, 0)) for _ in pays]
            + [
                pl.BlockSpec((pooled_n, block), lambda i, at: (0, at[0] * steps + i)),
                pl.BlockSpec((channels, block), lambda i, at: (0, at[0] * steps + i)),
                pl.BlockSpec((1, block), lambda i, at: (0, at[0] * steps + i)),
            ],
            out_specs=(
                pl.BlockSpec((pooled_n, block), lambda i, at: (0, i)),
                pl.BlockSpec((channels, block), lambda i, at: (0, i)),
                pl.BlockSpec((1, block), lambda i, at: (0, i)),
            ),
        ),
        out_shape=(
            jax.ShapeDtypeStruct((pooled_n, own), F32),
            jax.ShapeDtypeStruct((channels, own), F32),
            jax.ShapeDtypeStruct((1, own), F32),
        ),
        compiler_params=params(),
        cost_estimate=cost(2 * work, 4 * own * pooled_n),
        name="owned_rows",
    )(where, counts, *pays, mask_t, wt, rbias)

    parts, mask_grad, feat_grad, grad_rbias = lax.optimization_barrier((parts, mask_grad, feat_grad, grad_rbias))
    copies = pl.pallas_call(
        functools.partial(share_kernel, total),
        out_shape=jax.ShapeDtypeStruct((pieces, 8, 128), F32),
        compiler_params=params(),
        name="share",
    )(parts)
    summed = lax.all_to_all(copies, axes, split_axis=0, concat_axis=0, tiled=True)
    grad_conv, grad_cb, grad_mix, grad_mb, loss = pl.pallas_call(
        unpack_kernel,
        out_shape=(
            jax.ShapeDtypeStruct((channels, taps), F32),
            jax.ShapeDtypeStruct((1, channels), F32),
            jax.ShapeDtypeStruct((channels, channels), F32),
            jax.ShapeDtypeStruct((1, channels), F32),
            jax.ShapeDtypeStruct((1, 1), F32),
        ),
        compiler_params=params(),
        name="unpack",
    )(summed)
    return (
        loss.reshape(()),
        grad_conv,
        grad_cb.reshape(channels),
        grad_mix,
        grad_mb.reshape(channels),
        jnp.swapaxes(mask_grad[None], 1, 2),
        jnp.swapaxes(feat_grad[None], 1, 2),
        grad_rbias,
    )


def solution(mesh):
    return jax.shard_map(
        per_device,
        mesh=mesh,
        in_specs=(
            P("clip", "sess", None),
            P("clip", "sess", None),
            P("clip"),
            P("sess"),
            P(),
            P(),
            P(),
            P(),
            P("sess", None, None),
            P("sess", None, None),
            P("sess", None),
        ),
        out_specs=(
            P(),
            P(),
            P(),
            P(),
            P(),
            P("sess", "clip", None),
            P("sess", "clip", None),
            P("sess", "clip"),
        ),
        check_vma=False,
    )
```

```python
import functools

import jax
import jax.numpy as jnp
from jax import lax
from jax.experimental import pallas as pl
from jax.experimental.pallas import tpu as pltpu
from jax.sharding import PartitionSpec as P

HH = 36
WW = 64
KS = 7
KT = 3
DX = 8
PACK = 256
SEG = 64
CHUNK = 4 * WW
BF = jnp.bfloat16
F32 = jnp.float32
NT = (((1,), (1,)), ((), ()))
TN = (((0,), (0,)), ((), ()))


def dot(a, b, dims=(((1,), (0,)), ((), ())), precision=None):
    return lax.dot_general(a, b, dims, precision=precision, preferred_element_type=F32)


def iota(shape, axis):
    return lax.broadcasted_iota(jnp.int32, shape, axis)


def bias_column(row):
    size = row.shape[1]
    return jnp.sum(jnp.where(iota((size, size), 0) == iota((size, size), 1), row, 0.0), axis=1, keepdims=True)


def select_kernel(assign, video, responses, out):
    owners, lines, width = out.shape
    clips, pix = video.shape
    neurons = responses.shape[1]
    pick = (iota((owners, clips), 0) == assign[...]).astype(BF)
    first = dot(pick, responses[...])
    second = dot(pick, video[...])
    rows = [first[:, p : p + width] for p in range(0, neurons, width)]
    for p in range(0, pix, width):
        piece = second[:, p : p + width]
        if piece.shape[1] < width:
            piece = jnp.concatenate([piece, jnp.zeros((owners, width - piece.shape[1]), F32)], axis=1)
        rows.append(piece)
    while len(rows) < lines:
        rows.append(jnp.zeros((owners, width), F32))
    out[...] = jnp.stack(rows, axis=1).astype(BF)


def prep_kernel(frames, weight, cbias, mix, mbias, wbig, blocks, blocks_t, bias, table, pool, unpool):
    channels, taps = weight.shape
    patch_cols = wbig.shape[1]
    group = blocks.shape[0] // channels
    t = iota(table.shape, 0)
    l = iota(table.shape, 1)
    dy = l // (DX * frames)
    dx = (l // frames) % DX
    place = dy * KS + dx
    hit = (t == place) | (t == place + KS * KS) | (t == place + 2 * KS * KS)
    last = (t == KT * KS * KS) & (l == KS * frames)
    table[...] = jnp.where(((dx < KS) & hit & (t < KT * KS * KS)) | last, 1.0, 0.0).astype(BF)
    r = iota(pool.shape, 0)
    c = iota(pool.shape, 1)
    target = (r // (2 * WW)) * (WW // 2) + (r % WW) // 2
    pool[...] = jnp.where(target == c, 0.25, 0.0).astype(BF)
    r = iota(unpool.shape, 1)
    c = iota(unpool.shape, 0)
    target = (r // (2 * WW)) * (WW // 2) + (r % WW) // 2
    unpool[...] = jnp.where(target == c, 0.25, 0.0).astype(BF)
    size = channels * group
    same = (iota((size, size), 0) // channels) == (iota((size, size), 1) // channels)
    square = mix[...].astype(F32)
    for ref, base in ((blocks, square), (blocks_t, square.T)):
        wide = jnp.concatenate([base] * group, axis=1)
        ref[...] = jnp.where(same, jnp.concatenate([wide] * group, axis=0), 0.0).astype(BF)
    bias[0] = jnp.broadcast_to(bias_column(cbias[...]), bias.shape[1:])
    bias[1] = jnp.broadcast_to(bias_column(mbias[...]), bias.shape[1:])
    tap = iota((channels, taps), 1)
    weights = weight[...].astype(F32)
    split = [
        jnp.where((tap >= dt * KS * KS) & (tap < (dt + 1) * KS * KS), weights, 0.0).astype(BF)
        for dt in range(KT)
    ]
    spread = dot(jnp.concatenate(split, axis=0), table[0:taps, :])
    source = iota((channels, patch_cols), 1) % frames
    for f in range(frames):
        total = jnp.zeros((channels, patch_cols), F32)
        for dt in range(KT):
            total = total + jnp.where(source == f + dt - 1, spread[dt * channels : (dt + 1) * channels], 0.0)
        wbig[f * channels : (f + 1) * channels, :] = total.astype(BF)


def core_forward_kernel(
    recv, wbig, blocks, bias, pool, pay, target, act1, slope1, slope2, xcol, pre0, pre1, mid0, mid1, feats
):
    frames, _, width = recv.shape
    rows, pix = act1.shape
    channels = bias.shape[1]
    neurons = target.shape[1]
    span = blocks.shape[0]
    packet = recv[...].astype(F32)
    lines = [packet[:, j, :] for j in range((neurons + pix + width - 1) // width)]
    held = neurons // width
    for j in range(held):
        target[:, j * width : (j + 1) * width] = lines[j]
    video = jnp.concatenate(lines[held:], axis=1)[:, 0:pix]
    lane = iota((frames, pix), 1)
    col = lane % WW
    row = lane // WW
    per_store = max(1, 16 // frames)
    for dx0 in range(0, DX, per_store):
        shifted = []
        for dx in range(dx0, dx0 + per_store):
            s = dx - KS // 2
            if dx == KS:
                shifted.append(None)
            elif s == 0:
                shifted.append(video)
            else:
                rolled = pltpu.roll(video, (-s) % pix, 1)
                shifted.append(jnp.where((col + s >= 0) & (col + s < WW), rolled, 0.0))
        for dy in range(KS):
            t = dy - KS // 2
            parts = []
            for item in shifted:
                if item is None:
                    parts.append(jnp.ones((frames, pix), F32))
                elif t == 0:
                    parts.append(item)
                else:
                    moved = pltpu.roll(item, (-t * WW) % pix, 1)
                    parts.append(jnp.where((row + t >= 0) & (row + t < HH), moved, 0.0))
            base = (dy * DX + dx0) * frames
            block = parts[0] if len(parts) == 1 else jnp.concatenate(parts, axis=0)
            xcol[base : base + per_store * frames, :] = block.astype(BF)
    half = 2 * WW
    pre = (pre0, pre1)
    mid = (mid0, mid1)
    count = pix // CHUNK
    wide = wbig[...]

    def activate(source, which, act, slope, at):
        add = jnp.concatenate([bias[which]] * (CHUNK // 128), axis=1)
        for r in range(0, rows, channels):
            x = source[r : r + channels, :] + add
            e = jnp.exp(jnp.minimum(x, 0.0))
            act[r : r + channels, at] = (jnp.maximum(x, 0.0) + (e - 1.0)).astype(BF)
            slope[r : r + channels, at] = e.astype(BF)

    for t in range(count + 2):
        if t < count:
            pre[t % 2][...] = dot(wide, xcol[:, t * CHUNK : (t + 1) * CHUNK])
        if 1 <= t <= count:
            at = slice((t - 1) * CHUNK, t * CHUNK)
            activate(pre[(t - 1) % 2], 0, act1, slope1, at)
            for r in range(0, rows, span):
                mid[(t - 1) % 2][r : r + span, :] = dot(blocks[...], act1[r : r + span, at])
        if t >= 2:
            at = slice((t - 2) * CHUNK, (t - 1) * CHUNK)
            activate(mid[t % 2], 1, feats, slope2, at)
            if t % 2 == 1:
                first = (t - 3) * CHUNK
                pooled = dot(feats[:, first : first + 2 * CHUNK], pool[...])
                pay[:, first // 4 : first // 4 + half] = pooled.astype(BF)
    p = pix - CHUNK
    tail = dot(feats[:, p:pix], pool[0:CHUNK, :])
    pieces = []
    for t in range(neurons // half):
        at = t * half
        tile = lines[at // width][:, at % width : at % width + half]
        pieces += [pltpu.roll(tile, SEG, 1), tile]
    packed = jnp.concatenate(pieces, axis=0)
    pay[:, p // 4 : p // 4 + half] = jnp.where(iota((rows, half), 1) < SEG, tail, packed).astype(BF)


def drive_terms(projected, target, w, rbias, alive, scale, channels):
    frames = target.shape[0]
    sums = [
        jnp.sum(projected[f * channels : (f + 1) * channels] * w, axis=0, keepdims=True)
        for f in range(frames)
    ]
    drive = jnp.concatenate(sums, axis=0) + rbias
    e = jnp.exp(-jnp.abs(drive))
    rate = jnp.maximum(drive, 0.0) + jnp.log(1.0 + e) + 0.1
    sig = jnp.where(drive >= 0, 1.0, e) / (1.0 + e)
    grad = jnp.where(alive, (1.0 - target / rate) * sig, 0.0) * scale
    return rate, grad


def mixed_rows(grad, w):
    frames = grad.shape[0]
    return jnp.concatenate([grad[f : f + 1] * w for f in range(frames)], axis=0).astype(BF)


def readout_kernel(scale, count, target, pay, mask, wt, rbias, pooled_grad, loss, acc, loss_acc):
    i = pl.program_id(0)
    pooled_n, block = mask.shape
    channels = wt.shape[0]
    frames = target.shape[0]

    @pl.when(i == 0)
    def _():
        acc[...] = jnp.zeros_like(acc)
        loss_acc[...] = jnp.zeros_like(loss_acc)

    w = wt[...].astype(F32)
    m = mask[...]
    projected = dot(pay[:, 0:pooled_n], m)
    alive = (i * block + iota((frames, block), 1)) < count[0]
    rate, grad = drive_terms(projected, target[...], w, rbias[...], alive, scale, channels)
    loss_acc[...] += jnp.where(alive, rate - target[...] * jnp.log(rate), 0.0)
    acc[...] += dot(m, mixed_rows(grad, w), NT)

    @pl.when(i == pl.num_programs(0) - 1)
    def _():
        pooled_grad[...] = acc[...].T.astype(BF)
        loss[...] = jnp.broadcast_to(jnp.sum(loss_acc[...], keepdims=True) * scale, loss.shape)


def core_backward_kernel(
    channels, pooled_grad, loss, act1, slope1, slope2, xcol, blocks_t, table, unpool, out, up0, up1, down0, down1, g2, g1
):
    rows, pix = act1.shape
    frames = rows // channels
    span = blocks_t.shape[0]
    group = span // channels
    patch_cols = xcol.shape[0]
    up = (up0, up1)
    down = (down0, down1)
    count = pix // CHUNK
    half = 2 * WW
    bias_sum = jnp.zeros((channels, 128), F32)
    for t in range(count + 2):
        if t < count:
            first = (t // 2) * half
            wide = min(half, pooled_grad.shape[1] - first)
            side = (t % 2) * CHUNK
            up[t % 2][...] = dot(pooled_grad[:, first : first + wide], unpool[0:wide, side : side + CHUNK])
        if 1 <= t <= count:
            at = slice((t - 1) * CHUNK, t * CHUNK)
            for r in range(0, rows, channels):
                g = (up[(t - 1) % 2][r : r + channels, :] * slope2[r : r + channels, at].astype(F32)).astype(BF)
                g2[r : r + channels, at] = g
                g = g.astype(F32)
                for c in range(0, CHUNK, 128):
                    bias_sum = bias_sum + g[:, c : c + 128]
            for r in range(0, rows, span):
                down[(t - 1) % 2][r : r + span, :] = dot(blocks_t[...], g2[r : r + span, at])
        if t >= 2:
            at = slice((t - 2) * CHUNK, (t - 1) * CHUNK)
            for r in range(0, rows, channels):
                g = down[t % 2][r : r + channels, :] * slope1[r : r + channels, at].astype(F32)
                g1[r : r + channels, at] = g.astype(BF)
    mix_bias_grad = jnp.sum(bias_sum, axis=1, keepdims=True)
    mix_grad = jnp.zeros((channels, span), F32)
    same = (iota((span, span), 0) // channels) == (iota((span, span), 1) // channels)
    for r in range(0, rows, span):
        full = jnp.where(same, dot(g2[r : r + span, :], act1[r : r + span, :], NT), 0.0)
        for a in range(group):
            mix_grad = mix_grad + full[a * channels : (a + 1) * channels]
    fold = 2 * channels
    folded = mix_grad[:, 0:fold]
    for k in range(fold, span, fold):
        folded = folded + mix_grad[:, k : k + fold]
    folded = folded + pltpu.roll(folded, channels, 1)
    full = dot(g1[...], xcol[...], NT)
    source = iota((channels, patch_cols), 1) % frames
    parts = [jnp.zeros((channels, patch_cols), F32) for _ in range(KT + 1)]
    for f in range(frames):
        piece = full[f * channels : (f + 1) * channels]
        for dt in range(KT):
            parts[dt] = parts[dt] + jnp.where(source == f + dt - 1, piece, 0.0)
        parts[KT] = parts[KT] + piece
    left = jnp.concatenate(parts, axis=0)
    taps = jnp.zeros((left.shape[0], PACK), F32)
    for _ in range(3):
        term = left.astype(BF)
        left = left - term.astype(F32)
        taps = taps + dot(term, table[...], NT)
    lane = iota((channels, PACK), 1)
    conv = jnp.zeros((channels, PACK), F32)
    for dt in range(KT + 1):
        inside = (lane >= dt * KS * KS) & (lane < (dt + 1) * KS * KS)
        conv = conv + jnp.where(inside, taps[dt * channels : (dt + 1) * channels], 0.0)
    used = KT * KS * KS + 1
    low = lane[:, 0:128]
    upper = jnp.where(low < used - 128, conv[:, 128:256], 0.0)
    upper = jnp.where(low == used - 128, mix_bias_grad, upper)
    upper = jnp.where((low == used - 127) & (iota((channels, 128), 0) == 0), loss[0:1, 0:1], upper)
    upper = jnp.where(low >= channels, folded, upper)
    tiles = channels // 8
    out[...] = jnp.zeros_like(out)
    for i in range(tiles):
        out[i] = conv[8 * i : 8 * i + 8, 0:128]
        out[tiles + i] = upper[8 * i : 8 * i + 8, :]


def share_kernel(total, parts, out):
    each = parts.shape[0] // total
    for k in range(each):
        tile = parts[k]
        for d in range(1, total):
            tile = tile + parts[d * each + k]
        for d in range(total):
            out[d * each + k] = tile


def unpack_kernel(parts, conv, conv_bias, mix, mix_bias, loss):
    channels, taps = conv.shape
    tiles = channels // 8
    low = jnp.concatenate([parts[i] for i in range(tiles)], axis=0)
    high = jnp.concatenate([parts[tiles + i] for i in range(tiles)], axis=0)
    rest = taps - 128
    conv[...] = jnp.concatenate([low, high], axis=1)[:, 0:taps]
    mix[...] = pltpu.roll(high, 128 - channels, 1)[:, 0:channels]
    same = iota((channels, channels), 0) == iota((channels, channels), 1)
    conv_bias[...] = jnp.sum(jnp.where(same, high[:, rest : rest + 1], 0.0), axis=0, keepdims=True)
    mix_bias[...] = jnp.sum(jnp.where(same, high[:, rest + 1 : rest + 2], 0.0), axis=0, keepdims=True)
    loss[...] = high[0:1, rest + 2 : rest + 3]


def owned_rows_kernel(scale, clips, steps, begin, where, count, *refs):
    pays = refs[:clips]
    mask, wt, rbias = refs[clips : clips + 3]
    mask_grad, feat_grad, bias_grad = refs[-3:]
    i = begin + pl.program_id(0)
    pooled_n, block = mask.shape
    channels = wt.shape[0]
    frames = pays[0].shape[0] // channels
    first = (where[0] * steps + i) * block
    m = mask[...]
    w = wt[...].astype(F32)
    alive = (first + iota((frames, block), 1)) < count[0]
    total = None
    feat = jnp.zeros((channels, block), F32)
    bias = jnp.zeros((frames, block), F32)
    segs = block // SEG
    base = pl.multiple_of(first // SEG * frames, segs * frames)
    low = iota((frames, 128), 1) < SEG
    for pay in pays:
        pooled = pay[:, 0:pooled_n]
        held = pay[pl.ds(base, segs * frames), pooled_n - SEG : pooled_n + SEG].astype(F32)
        tiles = []
        for j in range(0, segs, 2):
            even = held[j * frames : (j + 1) * frames]
            odd = held[(j + 1) * frames : (j + 2) * frames]
            tiles.append(jnp.where(low, pltpu.roll(even, SEG, 1), odd))
        target = jnp.concatenate(tiles, axis=1)
        projected = dot(pooled, m)
        _, grad = drive_terms(projected, target, w, rbias[...], alive, scale, channels)
        for f in range(frames):
            feat = feat + grad[f : f + 1] * projected[f * channels : (f + 1) * channels]
        bias = bias + grad
        part = dot(pooled, mixed_rows(grad, w), TN)
        total = part if total is None else total + part
    mask_grad[...] = total
    feat_grad[...] = feat
    bias_grad[...] = jnp.sum(bias, axis=0, keepdims=True)


def params(limit=40):
    return pltpu.CompilerParams(vmem_limit_bytes=limit << 20)


def cost(flops, moved=1 << 20):
    return pl.CostEstimate(flops=int(flops), transcendentals=0, bytes_accessed=int(moved))


def in_hbm(*arrays):
    return [pltpu.with_memory_space_constraint(a, pltpu.HBM) for a in arrays]


def xor_pairs(size, mask):
    return [(i, i ^ mask) for i in range(size)]


def per_device(
    video, responses, assignment, counts, conv_weight, conv_bias, mix_weight, mix_bias, masks, feat_w, readout_bias
):
    sess_total = lax.axis_size("sess")
    clip_total = lax.axis_size("clip")
    total = sess_total * clip_total
    clip_block, frame_block, pix = video.shape
    neurons = responses.shape[2]
    pooled_n = masks.shape[2]
    channels, taps = conv_weight.shape
    frames = frame_block * sess_total
    rows = frames * channels
    own = neurons // clip_total
    block = min(512, own)
    assert clip_block == sess_total and frame_block == 1 and masks.shape[0] == 1
    assert neurons == channels * SEG and pooled_n % 128 == SEG and pix == HH * WW
    scale = 1.0 / (clip_block * clip_total * frames)

    group = max(1, 256 // channels)
    lines = 16
    packet = 512
    assert neurons + pix <= lines * packet
    send = pl.pallas_call(
        select_kernel,
        out_shape=jax.ShapeDtypeStruct((sess_total, lines, packet), BF),
        compiler_params=params(),
        name="select",
    )(*in_hbm(assignment[None, :], video.reshape(clip_block, pix), responses.reshape(clip_block, neurons)))
    recv = lax.all_to_all(send, "sess", split_axis=0, concat_axis=0, tiled=True)

    patch_cols = KS * DX * frames
    span = channels * group
    half = 2 * WW
    wbig, blocks, blocks_t, bias, table, pool, unpool = pl.pallas_call(
        functools.partial(prep_kernel, frames),
        out_shape=(
            jax.ShapeDtypeStruct((rows, patch_cols), BF),
            jax.ShapeDtypeStruct((span, span), BF),
            jax.ShapeDtypeStruct((span, span), BF),
            jax.ShapeDtypeStruct((2, channels, 128), F32),
            jax.ShapeDtypeStruct((PACK, patch_cols), BF),
            jax.ShapeDtypeStruct((4 * half, half), BF),
            jax.ShapeDtypeStruct((half, 4 * half), BF),
        ),
        compiler_params=params(),
        cost_estimate=cost(1 << 27),
        name="prep",
    )(*in_hbm(conv_weight, conv_bias[None, :], mix_weight, mix_bias[None, :]))

    wt = jnp.swapaxes(feat_w, 1, 2).reshape(channels, neurons)
    mask_t = jnp.swapaxes(masks, 1, 2).reshape(pooled_n, neurons)
    mask_t, wt, rbias = in_hbm(mask_t, wt, readout_bias)
    width = pooled_n + SEG
    pay, target, act1, slope1, slope2, xcol = pl.pallas_call(
        core_forward_kernel,
        out_shape=(
            jax.ShapeDtypeStruct((rows, width), BF),
            jax.ShapeDtypeStruct((frames, neurons), F32),
            jax.ShapeDtypeStruct((rows, pix), BF),
            jax.ShapeDtypeStruct((rows, pix), BF),
            jax.ShapeDtypeStruct((rows, pix), BF),
            jax.ShapeDtypeStruct((patch_cols, pix), BF),
        ),
        scratch_shapes=[pltpu.VMEM((rows, CHUNK), F32)] * 4 + [pltpu.VMEM((rows, pix), BF)],
        compiler_params=params(),
        cost_estimate=cost(2 * rows * pix * patch_cols, 8 * rows * pix),
        name="core_forward",
    )(recv, wbig, blocks, bias, pool)

    near = {0: pay}
    for mask in range(1, clip_total):
        if mask % 2 == 0 or mask == 1:
            near[mask] = lax.ppermute(pay, "clip", xor_pairs(clip_total, mask))

    smem = pl.BlockSpec(memory_space=pltpu.SMEM)
    big = min(512, neurons)
    work = 2 * rows * neurons * pooled_n
    pooled_grad, loss = pl.pallas_call(
        functools.partial(readout_kernel, scale),
        grid=(neurons // big,),
        in_specs=[
            smem,
            pl.BlockSpec((frames, big), lambda i: (0, i)),
            pl.BlockSpec((rows, width), lambda i: (0, 0)),
            pl.BlockSpec((pooled_n, big), lambda i: (0, i)),
            pl.BlockSpec((channels, big), lambda i: (0, i)),
            pl.BlockSpec((1, big), lambda i: (0, i)),
        ],
        out_specs=(
            pl.BlockSpec((rows, pooled_n), lambda i: (0, 0)),
            pl.BlockSpec((8, 128), lambda i: (0, 0)),
        ),
        out_shape=(jax.ShapeDtypeStruct((rows, pooled_n), BF), jax.ShapeDtypeStruct((8, 128), F32)),
        scratch_shapes=[pltpu.VMEM((pooled_n, rows), F32), pltpu.VMEM((frames, big), F32)],
        compiler_params=params(),
        cost_estimate=cost(2 * work, 2 * neurons * pooled_n),
        name="readout",
    )(counts, target, pay, mask_t, wt, rbias)

    pieces = total * max(1, (2 * channels // 8) // total)
    core = pl.pallas_call(
        functools.partial(core_backward_kernel, channels),
        out_shape=jax.ShapeDtypeStruct((pieces, 8, 128), F32),
        scratch_shapes=[pltpu.VMEM((rows, CHUNK), F32)] * 4 + [pltpu.VMEM((rows, pix), BF)] * 2,
        compiler_params=params(),
        cost_estimate=cost(2 * work, 8 * rows * pix),
        name="core_backward",
    )(pooled_grad, loss, act1, slope1, slope2, xcol, blocks_t, table, unpool)

    far = [mask for mask in near if mask > 1]
    held, core = lax.optimization_barrier(([near[mask] for mask in far], core))
    pays = [near[0], near[1]]
    for mask, value in zip(far, held):
        pays += [value, lax.ppermute(value, "clip", xor_pairs(clip_total, 1))]

    axes = ("clip", "sess")
    parts = lax.all_to_all(core, axes, split_axis=0, concat_axis=0, tiled=True)

    where = lax.axis_index("clip").astype(jnp.int32)[None]
    steps = own // block

    def owned_rows(begin, number, held):
        whole = [pl.BlockSpec(memory_space=pl.ANY) for _ in held]
        return pl.pallas_call(
            functools.partial(owned_rows_kernel, scale, clip_total, steps, begin),
            grid_spec=pltpu.PrefetchScalarGridSpec(
                num_scalar_prefetch=1,
                grid=(number,),
                in_specs=[smem]
                + [pl.BlockSpec((rows, width), lambda i, at: (0, 0)) for _ in pays]
                + [
                    pl.BlockSpec((pooled_n, block), lambda i, at: (0, at[0] * steps + begin + i)),
                    pl.BlockSpec((channels, block), lambda i, at: (0, at[0] * steps + begin + i)),
                    pl.BlockSpec((1, block), lambda i, at: (0, at[0] * steps + begin + i)),
                ]
                + whole,
                out_specs=(
                    pl.BlockSpec((pooled_n, block), lambda i, at: (0, begin + i)),
                    pl.BlockSpec((channels, block), lambda i, at: (0, begin + i)),
                    pl.BlockSpec((1, block), lambda i, at: (0, begin + i)),
                ),
            ),
            out_shape=(
                jax.ShapeDtypeStruct((pooled_n, own), F32),
                jax.ShapeDtypeStruct((channels, own), F32),
                jax.ShapeDtypeStruct((1, own), F32),
            ),
            input_output_aliases={5 + clip_total + k: k for k in range(len(held))},
            compiler_params=params(),
            cost_estimate=cost(2 * work * number // steps, 4 * own * pooled_n),
            name="owned_rows",
        )(where, counts, *pays, mask_t, wt, rbias, *held)

    early = max(1, steps // 2)
    readout_grads = owned_rows(0, early, ())
    parts, readout_grads = lax.optimization_barrier((parts, readout_grads))
    copies = pl.pallas_call(
        functools.partial(share_kernel, total),
        out_shape=jax.ShapeDtypeStruct((pieces, 8, 128), F32),
        compiler_params=params(),
        name="share",
    )(parts)
    summed = lax.all_to_all(copies, axes, split_axis=0, concat_axis=0, tiled=True)
    if early < steps:
        readout_grads = owned_rows(early, steps - early, readout_grads)
        summed, readout_grads = lax.optimization_barrier((summed, readout_grads))
    mask_grad, feat_grad, grad_rbias = readout_grads
    grad_conv, grad_cb, grad_mix, grad_mb, loss = pl.pallas_call(
        unpack_kernel,
        out_shape=(
            jax.ShapeDtypeStruct((channels, taps), F32),
            jax.ShapeDtypeStruct((1, channels), F32),
            jax.ShapeDtypeStruct((channels, channels), F32),
            jax.ShapeDtypeStruct((1, channels), F32),
            jax.ShapeDtypeStruct((1, 1), F32),
        ),
        compiler_params=params(),
        name="unpack",
    )(summed)
    return (
        loss.reshape(()),
        grad_conv,
        grad_cb.reshape(channels),
        grad_mix,
        grad_mb.reshape(channels),
        jnp.swapaxes(mask_grad[None], 1, 2),
        jnp.swapaxes(feat_grad[None], 1, 2),
        grad_rbias,
    )


def solution(mesh):
    return jax.shard_map(
        per_device,
        mesh=mesh,
        in_specs=(
            P("clip", "sess", None),
            P("clip", "sess", None),
            P("clip"),
            P("sess"),
            P(),
            P(),
            P(),
            P(),
            P("sess", None, None),
            P("sess", None, None),
            P("sess", None),
        ),
        out_specs=(
            P(),
            P(),
            P(),
            P(),
            P(),
            P("sess", "clip", None),
            P("sess", "clip", None),
            P("sess", "clip"),
        ),
        check_vma=False,
    )
```

```python
import functools

import jax
import jax.numpy as jnp
from jax import lax
from jax.experimental import pallas as pl
from jax.experimental.pallas import tpu as pltpu
from jax.sharding import PartitionSpec as P

HH = 36
WW = 64
KS = 7
KT = 3
DX = 8
PACK = 256
SEG = 64
CHUNK = 4 * WW
BF = jnp.bfloat16
F32 = jnp.float32
NT = (((1,), (1,)), ((), ()))
TN = (((0,), (0,)), ((), ()))


def dot(a, b, dims=(((1,), (0,)), ((), ())), precision=None):
    return lax.dot_general(a, b, dims, precision=precision, preferred_element_type=F32)


def iota(shape, axis):
    return lax.broadcasted_iota(jnp.int32, shape, axis)


def bias_column(row):
    size = row.shape[1]
    return jnp.sum(jnp.where(iota((size, size), 0) == iota((size, size), 1), row, 0.0), axis=1, keepdims=True)


def select_kernel(assign, video, responses, out):
    owners, lines, width = out.shape
    clips, pix = video.shape
    neurons = responses.shape[1]
    pick = (iota((owners, clips), 0) == assign[...]).astype(BF)
    first = dot(pick, responses[...])
    second = dot(pick, video[...])
    rows = [first[:, p : p + width] for p in range(0, neurons, width)]
    for p in range(0, pix, width):
        piece = second[:, p : p + width]
        if piece.shape[1] < width:
            piece = jnp.concatenate([piece, jnp.zeros((owners, width - piece.shape[1]), F32)], axis=1)
        rows.append(piece)
    while len(rows) < lines:
        rows.append(jnp.zeros((owners, width), F32))
    out[...] = jnp.stack(rows, axis=1).astype(BF)


def prep_kernel(frames, weight, cbias, mix, mbias, wbig, blocks, blocks_t, bias, table, pool, unpool):
    channels, taps = weight.shape
    patch_cols = wbig.shape[1]
    group = blocks.shape[0] // channels
    t = iota(table.shape, 0)
    l = iota(table.shape, 1)
    dy = l // (DX * frames)
    dx = (l // frames) % DX
    place = dy * KS + dx
    hit = (t == place) | (t == place + KS * KS) | (t == place + 2 * KS * KS)
    last = (t == KT * KS * KS) & (l == KS * frames)
    table[...] = jnp.where(((dx < KS) & hit & (t < KT * KS * KS)) | last, 1.0, 0.0).astype(BF)
    r = iota(pool.shape, 0)
    c = iota(pool.shape, 1)
    target = (r // (2 * WW)) * (WW // 2) + (r % WW) // 2
    pool[...] = jnp.where(target == c, 0.25, 0.0).astype(BF)
    r = iota(unpool.shape, 1)
    c = iota(unpool.shape, 0)
    target = (r // (2 * WW)) * (WW // 2) + (r % WW) // 2
    unpool[...] = jnp.where(target == c, 0.25, 0.0).astype(BF)
    size = channels * group
    same = (iota((size, size), 0) // channels) == (iota((size, size), 1) // channels)
    square = mix[...].astype(F32)
    for ref, base in ((blocks, square), (blocks_t, square.T)):
        wide = jnp.concatenate([base] * group, axis=1)
        ref[...] = jnp.where(same, jnp.concatenate([wide] * group, axis=0), 0.0).astype(BF)
    bias[0] = jnp.broadcast_to(bias_column(cbias[...]), bias.shape[1:])
    bias[1] = jnp.broadcast_to(bias_column(mbias[...]), bias.shape[1:])
    tap = iota((channels, taps), 1)
    weights = weight[...].astype(F32)
    split = [
        jnp.where((tap >= dt * KS * KS) & (tap < (dt + 1) * KS * KS), weights, 0.0).astype(BF)
        for dt in range(KT)
    ]
    spread = dot(jnp.concatenate(split, axis=0), table[0:taps, :])
    source = iota((channels, patch_cols), 1) % frames
    for f in range(frames):
        total = jnp.zeros((channels, patch_cols), F32)
        for dt in range(KT):
            total = total + jnp.where(source == f + dt - 1, spread[dt * channels : (dt + 1) * channels], 0.0)
        wbig[f * channels : (f + 1) * channels, :] = total.astype(BF)


def core_forward_kernel(
    recv,
    wbig,
    blocks,
    bias,
    pool,
    mask_in,
    wt_in,
    pay,
    target,
    act1,
    slope1,
    slope2,
    xcol,
    mask,
    wt,
    pre0,
    pre1,
    mid0,
    mid1,
    feats,
    sems,
):
    copies = [pltpu.make_async_copy(mask_in, mask, sems.at[0]), pltpu.make_async_copy(wt_in, wt, sems.at[1])]
    for copy in copies:
        copy.start()
    frames, _, width = recv.shape
    rows, pix = act1.shape
    channels = bias.shape[1]
    neurons = target.shape[1]
    span = blocks.shape[0]
    packet = recv[...].astype(F32)
    lines = [packet[:, j, :] for j in range((neurons + pix + width - 1) // width)]
    held = neurons // width
    for j in range(held):
        target[:, j * width : (j + 1) * width] = lines[j]
    video = jnp.concatenate(lines[held:], axis=1)[:, 0:pix]
    lane = iota((frames, pix), 1)
    col = lane % WW
    row = lane // WW
    per_store = max(1, 16 // frames)
    for dx0 in range(0, DX, per_store):
        shifted = []
        for dx in range(dx0, dx0 + per_store):
            s = dx - KS // 2
            if dx == KS:
                shifted.append(None)
            elif s == 0:
                shifted.append(video)
            else:
                rolled = pltpu.roll(video, (-s) % pix, 1)
                shifted.append(jnp.where((col + s >= 0) & (col + s < WW), rolled, 0.0))
        for dy in range(KS):
            t = dy - KS // 2
            parts = []
            for item in shifted:
                if item is None:
                    parts.append(jnp.ones((frames, pix), F32))
                elif t == 0:
                    parts.append(item)
                else:
                    moved = pltpu.roll(item, (-t * WW) % pix, 1)
                    parts.append(jnp.where((row + t >= 0) & (row + t < HH), moved, 0.0))
            base = (dy * DX + dx0) * frames
            block = parts[0] if len(parts) == 1 else jnp.concatenate(parts, axis=0)
            xcol[base : base + per_store * frames, :] = block.astype(BF)
    half = 2 * WW
    pre = (pre0, pre1)
    mid = (mid0, mid1)
    count = pix // CHUNK
    wide = wbig[...]

    def activate(source, which, act, slope, at):
        add = jnp.concatenate([bias[which]] * (CHUNK // 128), axis=1)
        for r in range(0, rows, channels):
            x = source[r : r + channels, :] + add
            e = jnp.exp(jnp.minimum(x, 0.0))
            act[r : r + channels, at] = (jnp.maximum(x, 0.0) + (e - 1.0)).astype(BF)
            slope[r : r + channels, at] = e.astype(BF)

    for t in range(count + 2):
        if t < count:
            pre[t % 2][...] = dot(wide, xcol[:, t * CHUNK : (t + 1) * CHUNK])
        if 1 <= t <= count:
            at = slice((t - 1) * CHUNK, t * CHUNK)
            activate(pre[(t - 1) % 2], 0, act1, slope1, at)
            for r in range(0, rows, span):
                mid[(t - 1) % 2][r : r + span, :] = dot(blocks[...], act1[r : r + span, at])
        if t >= 2:
            at = slice((t - 2) * CHUNK, (t - 1) * CHUNK)
            activate(mid[t % 2], 1, feats, slope2, at)
            if t % 2 == 1:
                first = (t - 3) * CHUNK
                pooled = dot(feats[:, first : first + 2 * CHUNK], pool[...])
                pay[:, first // 4 : first // 4 + half] = pooled.astype(BF)
    p = pix - CHUNK
    tail = dot(feats[:, p:pix], pool[0:CHUNK, :])
    pieces = []
    for t in range(neurons // half):
        at = t * half
        tile = lines[at // width][:, at % width : at % width + half]
        pieces += [pltpu.roll(tile, SEG, 1), tile]
    packed = jnp.concatenate(pieces, axis=0)
    pay[:, p // 4 : p // 4 + half] = jnp.where(iota((rows, half), 1) < SEG, tail, packed).astype(BF)
    for copy in copies:
        copy.wait()


def drive_terms(projected, target, w, rbias, alive, scale, channels):
    frames = target.shape[0]
    sums = [
        jnp.sum(projected[f * channels : (f + 1) * channels, :] * w, axis=0, keepdims=True)
        for f in range(frames)
    ]
    drive = jnp.concatenate(sums, axis=0) + rbias
    e = jnp.exp(-jnp.abs(drive))
    rate = jnp.maximum(drive, 0.0) + jnp.log(1.0 + e) + 0.1
    sig = jnp.where(drive >= 0, 1.0, e) / (1.0 + e)
    grad = jnp.where(alive, (1.0 - target / rate) * sig, 0.0) * scale
    return rate, grad


def mixed_rows(grad, w):
    frames = grad.shape[0]
    return jnp.concatenate([grad[f : f + 1] * w for f in range(frames)], axis=0).astype(BF)


def readout_kernel(
    scale, count, target, pay, mask, wt, rbias, pooled_grad, loss, proj0, proj1, mixed, acc
):
    pooled_n, neurons = mask.shape
    channels = wt.shape[0]
    frames = target.shape[0]
    proj = (proj0, proj1)
    block = proj0.shape[1]
    steps = neurons // block
    pooled = pay[:, 0:pooled_n]
    loss_sum = jnp.zeros((frames, block), F32)
    begun = False
    for t in range(steps + 2):
        if t < steps:
            proj[t % 2][...] = dot(pooled, mask[:, t * block : (t + 1) * block])
        if 1 <= t <= steps:
            at = slice((t - 1) * block, t * block)
            w = wt[:, at].astype(F32)
            goal = target[:, at]
            alive = ((t - 1) * block + iota((frames, block), 1)) < count[0]
            rate, grad = drive_terms(proj[(t - 1) % 2], goal, w, rbias[:, at], alive, scale, channels)
            loss_sum = loss_sum + jnp.where(alive, rate - goal * jnp.log(rate), 0.0)
            for f in range(frames):
                mixed[f * channels : (f + 1) * channels, at] = (grad[f : f + 1] * w).astype(BF)
        if t >= 2 and (t % 2 == 1 or t == steps + 1):
            low = ((t - 2) // 2) * 2 * block
            at = slice(low, (t - 1) * block)
            part = dot(mask[:, at], mixed[:, at], NT)
            acc[...] = acc[...] + part if begun else part
            begun = True
    pooled_grad[...] = acc[...].T.astype(BF)
    loss[...] = jnp.broadcast_to(jnp.sum(loss_sum, keepdims=True) * scale, loss.shape)


def core_backward_kernel(
    channels, pooled_grad, loss, act1, slope1, slope2, xcol, blocks_t, table, unpool, out, up0, up1, down0, down1, g2, g1
):
    rows, pix = act1.shape
    frames = rows // channels
    span = blocks_t.shape[0]
    group = span // channels
    patch_cols = xcol.shape[0]
    up = (up0, up1)
    down = (down0, down1)
    count = pix // CHUNK
    half = 2 * WW
    bias_sum = jnp.zeros((channels, 128), F32)
    for t in range(count + 2):
        if t < count:
            first = (t // 2) * half
            wide = min(half, pooled_grad.shape[1] - first)
            side = (t % 2) * CHUNK
            up[t % 2][...] = dot(pooled_grad[:, first : first + wide], unpool[0:wide, side : side + CHUNK])
        if 1 <= t <= count:
            at = slice((t - 1) * CHUNK, t * CHUNK)
            for r in range(0, rows, channels):
                g = (up[(t - 1) % 2][r : r + channels, :] * slope2[r : r + channels, at].astype(F32)).astype(BF)
                g2[r : r + channels, at] = g
                g = g.astype(F32)
                for c in range(0, CHUNK, 128):
                    bias_sum = bias_sum + g[:, c : c + 128]
            for r in range(0, rows, span):
                down[(t - 1) % 2][r : r + span, :] = dot(blocks_t[...], g2[r : r + span, at])
        if t >= 2:
            at = slice((t - 2) * CHUNK, (t - 1) * CHUNK)
            for r in range(0, rows, channels):
                g = down[t % 2][r : r + channels, :] * slope1[r : r + channels, at].astype(F32)
                g1[r : r + channels, at] = g.astype(BF)
    mix_bias_grad = jnp.sum(bias_sum, axis=1, keepdims=True)
    mix_grad = jnp.zeros((channels, span), F32)
    same = (iota((span, span), 0) // channels) == (iota((span, span), 1) // channels)
    for r in range(0, rows, span):
        full = jnp.where(same, dot(g2[r : r + span, :], act1[r : r + span, :], NT), 0.0)
        for a in range(group):
            mix_grad = mix_grad + full[a * channels : (a + 1) * channels]
    fold = 2 * channels
    folded = mix_grad[:, 0:fold]
    for k in range(fold, span, fold):
        folded = folded + mix_grad[:, k : k + fold]
    folded = folded + pltpu.roll(folded, channels, 1)
    full = dot(g1[...], xcol[...], NT)
    source = iota((channels, patch_cols), 1) % frames
    parts = [jnp.zeros((channels, patch_cols), F32) for _ in range(KT + 1)]
    for f in range(frames):
        piece = full[f * channels : (f + 1) * channels]
        for dt in range(KT):
            parts[dt] = parts[dt] + jnp.where(source == f + dt - 1, piece, 0.0)
        parts[KT] = parts[KT] + piece
    left = jnp.concatenate(parts, axis=0)
    taps = jnp.zeros((left.shape[0], PACK), F32)
    for _ in range(3):
        term = left.astype(BF)
        left = left - term.astype(F32)
        taps = taps + dot(term, table[...], NT)
    lane = iota((channels, PACK), 1)
    conv = jnp.zeros((channels, PACK), F32)
    for dt in range(KT + 1):
        inside = (lane >= dt * KS * KS) & (lane < (dt + 1) * KS * KS)
        conv = conv + jnp.where(inside, taps[dt * channels : (dt + 1) * channels], 0.0)
    used = KT * KS * KS + 1
    low = lane[:, 0:128]
    upper = jnp.where(low < used - 128, conv[:, 128:256], 0.0)
    upper = jnp.where(low == used - 128, mix_bias_grad, upper)
    upper = jnp.where((low == used - 127) & (iota((channels, 128), 0) == 0), loss[0:1, 0:1], upper)
    upper = jnp.where(low >= channels, folded, upper)
    pieces, lines, _ = out.shape
    both = jnp.concatenate([conv[:, 0:128], upper], axis=0)
    for k in range(pieces):
        out[k] = both[k * lines : (k + 1) * lines, :]


def share_kernel(parts, out):
    total = parts.shape[0]
    tile = parts[0]
    for d in range(1, total):
        tile = tile + parts[d]
    for d in range(total):
        out[d] = tile


def unpack_kernel(parts, conv, conv_bias, mix, mix_bias, loss):
    channels, taps = conv.shape
    both = jnp.concatenate([parts[k] for k in range(parts.shape[0])], axis=0)
    low = both[0:channels]
    high = both[channels:]
    rest = taps - 128
    conv[...] = jnp.concatenate([low, high], axis=1)[:, 0:taps]
    mix[...] = pltpu.roll(high, 128 - channels, 1)[:, 0:channels]
    same = iota((channels, channels), 0) == iota((channels, channels), 1)
    conv_bias[...] = jnp.sum(jnp.where(same, high[:, rest : rest + 1], 0.0), axis=0, keepdims=True)
    mix_bias[...] = jnp.sum(jnp.where(same, high[:, rest + 1 : rest + 2], 0.0), axis=0, keepdims=True)
    loss[...] = high[0:1, rest + 2 : rest + 3]


def owned_rows_kernel(scale, clips, begin, own, where, count, *refs):
    pays = refs[:clips]
    wt, rbias, mask = refs[clips : clips + 3]
    outs = refs[-8:-5]
    stage = refs[-5:-2]
    mask_part, sems = refs[-2:]
    pooled_n, block = stage[0].shape
    channels = wt.shape[0]
    frames = pays[0].shape[0] // channels
    first = pl.multiple_of(where[0] * own + begin, block)
    fetch = pltpu.make_async_copy(mask.at[:, pl.ds(first, block)], mask_part, sems.at[3])
    fetch.start()
    w = wt[:, pl.ds(first, block)].astype(F32)
    add = rbias[:, pl.ds(first, block)]
    alive = (first + iota((frames, block), 1)) < count[0]
    total = None
    feat = jnp.zeros((channels, block), F32)
    bias = jnp.zeros((frames, block), F32)
    segs = block // SEG
    base = pl.multiple_of(first // SEG * frames, segs * frames)
    low = iota((frames, 128), 1) < SEG
    fetch.wait()
    m = mask_part[...]
    for pay in pays:
        pooled = pay[:, 0:pooled_n]
        held = pay[pl.ds(base, segs * frames), pooled_n - SEG : pooled_n + SEG].astype(F32)
        tiles = []
        for j in range(0, segs, 2):
            even = held[j * frames : (j + 1) * frames]
            odd = held[(j + 1) * frames : (j + 2) * frames]
            tiles.append(jnp.where(low, pltpu.roll(even, SEG, 1), odd))
        target = jnp.concatenate(tiles, axis=1)
        projected = dot(pooled, m)
        _, grad = drive_terms(projected, target, w, add, alive, scale, channels)
        for f in range(frames):
            feat = feat + grad[f : f + 1] * projected[f * channels : (f + 1) * channels]
        bias = bias + grad
        part = dot(pooled, mixed_rows(grad, w), TN)
        total = part if total is None else total + part
    stage[0][...] = total
    stage[1][...] = feat
    stage[2][...] = jnp.sum(bias, axis=0, keepdims=True)
    copies = [
        pltpu.make_async_copy(src, dst.at[:, begin : begin + block], sems.at[k])
        for k, (src, dst) in enumerate(zip(stage, outs))
    ]
    for copy in copies:
        copy.start()
    for copy in copies:
        copy.wait()


def params(limit=20):
    return pltpu.CompilerParams(vmem_limit_bytes=limit << 20)


def cost(flops, moved=1 << 20):
    return pl.CostEstimate(flops=int(flops), transcendentals=0, bytes_accessed=int(moved))


def in_hbm(*arrays):
    return [pltpu.with_memory_space_constraint(a, pltpu.HBM) for a in arrays]


def xor_pairs(size, mask):
    return [(i, i ^ mask) for i in range(size)]


def per_device(
    video, responses, assignment, counts, conv_weight, conv_bias, mix_weight, mix_bias, masks, feat_w, readout_bias
):
    sess_total = lax.axis_size("sess")
    clip_total = lax.axis_size("clip")
    total = sess_total * clip_total
    clip_block, frame_block, pix = video.shape
    neurons = responses.shape[2]
    pooled_n = masks.shape[2]
    channels, taps = conv_weight.shape
    frames = frame_block * sess_total
    rows = frames * channels
    own = neurons // clip_total
    block = min(512, own)
    assert clip_block == sess_total and frame_block == 1 and masks.shape[0] == 1
    assert neurons == channels * SEG and pooled_n % 128 == SEG and pix == HH * WW
    scale = 1.0 / (clip_block * clip_total * frames)

    group = max(1, 256 // channels)
    lines = 16
    packet = 512
    assert neurons + pix <= lines * packet
    send = pl.pallas_call(
        select_kernel,
        out_shape=jax.ShapeDtypeStruct((sess_total, lines, packet), BF),
        compiler_params=params(),
        name="select",
    )(*in_hbm(assignment[None, :], video.reshape(clip_block, pix), responses.reshape(clip_block, neurons)))
    recv = lax.all_to_all(send, "sess", split_axis=0, concat_axis=0, tiled=True)

    patch_cols = KS * DX * frames
    span = channels * group
    half = 2 * WW
    wbig, blocks, blocks_t, bias, table, pool, unpool = pl.pallas_call(
        functools.partial(prep_kernel, frames),
        out_shape=(
            jax.ShapeDtypeStruct((rows, patch_cols), BF),
            jax.ShapeDtypeStruct((span, span), BF),
            jax.ShapeDtypeStruct((span, span), BF),
            jax.ShapeDtypeStruct((2, channels, 128), F32),
            jax.ShapeDtypeStruct((PACK, patch_cols), BF),
            jax.ShapeDtypeStruct((4 * half, half), BF),
            jax.ShapeDtypeStruct((half, 4 * half), BF),
        ),
        compiler_params=params(),
        cost_estimate=cost(1 << 27),
        name="prep",
    )(*in_hbm(conv_weight, conv_bias[None, :], mix_weight, mix_bias[None, :]))

    wt = jnp.swapaxes(feat_w, 1, 2).reshape(channels, neurons)
    mask_t = jnp.swapaxes(masks, 1, 2).reshape(pooled_n, neurons)
    mask_t, wt, rbias = in_hbm(mask_t, wt, readout_bias)
    width = pooled_n + SEG
    vmem = pl.BlockSpec(memory_space=pltpu.VMEM)
    anywhere = pl.BlockSpec(memory_space=pl.ANY)
    smem = pl.BlockSpec(memory_space=pltpu.SMEM)
    pay, target, act1, slope1, slope2, xcol, mask_v, wt_v = pl.pallas_call(
        core_forward_kernel,
        out_shape=(
            jax.ShapeDtypeStruct((rows, width), BF),
            jax.ShapeDtypeStruct((frames, neurons), F32),
            jax.ShapeDtypeStruct((rows, pix), BF),
            jax.ShapeDtypeStruct((rows, pix), BF),
            jax.ShapeDtypeStruct((rows, pix), BF),
            jax.ShapeDtypeStruct((patch_cols, pix), BF),
            jax.ShapeDtypeStruct((pooled_n, neurons), BF),
            jax.ShapeDtypeStruct((channels, neurons), BF),
        ),
        in_specs=[vmem] * 5 + [anywhere] * 2,
        scratch_shapes=[pltpu.VMEM((rows, CHUNK), F32)] * 4
        + [pltpu.VMEM((rows, pix), BF), pltpu.SemaphoreType.DMA((2,))],
        compiler_params=params(),
        cost_estimate=cost(2 * rows * pix * patch_cols, 8 * rows * pix),
        name="core_forward",
    )(recv, wbig, blocks, bias, pool, mask_t, wt)

    near = {0: pay}
    for mask in range(1, clip_total):
        if mask % 2 == 0 or mask == 1:
            near[mask] = lax.ppermute(pay, "clip", xor_pairs(clip_total, mask))

    big = min(512, neurons)
    work = 2 * rows * neurons * pooled_n
    where = lax.axis_index("clip").astype(jnp.int32)[None]
    pooled_grad, loss = pl.pallas_call(
        functools.partial(readout_kernel, scale),
        in_specs=[smem] + [vmem] * 5,
        out_shape=(jax.ShapeDtypeStruct((rows, pooled_n), BF), jax.ShapeDtypeStruct((8, 128), F32)),
        scratch_shapes=[pltpu.VMEM((rows, big), F32)] * 2
        + [pltpu.VMEM((rows, neurons), BF), pltpu.VMEM((pooled_n, rows), F32)],
        compiler_params=params(),
        cost_estimate=cost(2 * work, 2 * neurons * pooled_n),
        name="readout",
    )(counts, target, pay, mask_v, wt_v, rbias)

    assert 2 * channels % total == 0
    pieces = (total, 2 * channels // total, 128)
    core = pl.pallas_call(
        functools.partial(core_backward_kernel, channels),
        out_shape=jax.ShapeDtypeStruct(pieces, F32),
        scratch_shapes=[pltpu.VMEM((rows, CHUNK), F32)] * 4 + [pltpu.VMEM((rows, pix), BF)] * 2,
        compiler_params=params(),
        cost_estimate=cost(2 * work, 8 * rows * pix),
        name="core_backward",
    )(pooled_grad, loss, act1, slope1, slope2, xcol, blocks_t, table, unpool)

    far = [mask for mask in near if mask > 1]
    held, core = lax.optimization_barrier(([near[mask] for mask in far], core))
    pays = [near[0], near[1]]
    for mask, value in zip(far, held):
        pays += [value, lax.ppermute(value, "clip", xor_pairs(clip_total, 1))]

    axes = ("clip", "sess")
    parts = lax.all_to_all(core, axes, split_axis=0, concat_axis=0, tiled=True)

    def owned_rows(begin, held):
        return pl.pallas_call(
            functools.partial(owned_rows_kernel, scale, clip_total, begin, own),
            in_specs=[smem, smem] + [vmem] * (clip_total + 2) + [anywhere] * (1 + len(held)),
            out_specs=[anywhere] * 3,
            out_shape=[
                jax.ShapeDtypeStruct((pooled_n, own), F32),
                jax.ShapeDtypeStruct((channels, own), F32),
                jax.ShapeDtypeStruct((1, own), F32),
            ],
            input_output_aliases={5 + clip_total + k: k for k in range(len(held))},
            scratch_shapes=[
                pltpu.VMEM((pooled_n, block), F32),
                pltpu.VMEM((channels, block), F32),
                pltpu.VMEM((1, block), F32),
                pltpu.VMEM((pooled_n, block), BF),
                pltpu.SemaphoreType.DMA((4,)),
            ],
            compiler_params=params(),
            cost_estimate=cost(2 * work * block // own, 4 * block * pooled_n),
            name="owned_rows",
        )(where, counts, *pays, wt_v, rbias, mask_t, *held)

    readout_grads = ()
    early = max(block, own // 2)
    for begin in range(0, early, block):
        readout_grads = owned_rows(begin, readout_grads)
    parts, readout_grads = lax.optimization_barrier((parts, readout_grads))
    copies = pl.pallas_call(
        share_kernel,
        out_shape=jax.ShapeDtypeStruct(pieces, F32),
        compiler_params=params(),
        name="share",
    )(parts)
    summed = lax.all_to_all(copies, axes, split_axis=0, concat_axis=0, tiled=True)
    if early < own:
        for begin in range(early, own, block):
            readout_grads = owned_rows(begin, readout_grads)
        summed, readout_grads = lax.optimization_barrier((summed, readout_grads))
    mask_grad, feat_grad, grad_rbias = readout_grads
    grad_conv, grad_cb, grad_mix, grad_mb, loss = pl.pallas_call(
        unpack_kernel,
        out_shape=(
            jax.ShapeDtypeStruct((channels, taps), F32),
            jax.ShapeDtypeStruct((1, channels), F32),
            jax.ShapeDtypeStruct((channels, channels), F32),
            jax.ShapeDtypeStruct((1, channels), F32),
            jax.ShapeDtypeStruct((1, 1), F32),
        ),
        compiler_params=params(),
        name="unpack",
    )(summed)
    return (
        loss.reshape(()),
        grad_conv,
        grad_cb.reshape(channels),
        grad_mix,
        grad_mb.reshape(channels),
        jnp.swapaxes(mask_grad[None], 1, 2),
        jnp.swapaxes(feat_grad[None], 1, 2),
        grad_rbias,
    )


def solution(mesh):
    return jax.shard_map(
        per_device,
        mesh=mesh,
        in_specs=(
            P("clip", "sess", None),
            P("clip", "sess", None),
            P("clip"),
            P("sess"),
            P(),
            P(),
            P(),
            P(),
            P("sess", None, None),
            P("sess", None, None),
            P("sess", None),
        ),
        out_specs=(
            P(),
            P(),
            P(),
            P(),
            P(),
            P("sess", "clip", None),
            P("sess", "clip", None),
            P("sess", "clip"),
        ),
        check_vma=False,
    )
```

```python
import functools

import jax
import jax.numpy as jnp
from jax import lax
from jax.experimental import pallas as pl
from jax.experimental.pallas import tpu as pltpu
from jax.sharding import PartitionSpec as P

HH = 36
WW = 64
KS = 7
KT = 3
DX = 8
PACK = 256
SEG = 64
CHUNK = 4 * WW
BF = jnp.bfloat16
F32 = jnp.float32
NT = (((1,), (1,)), ((), ()))
TN = (((0,), (0,)), ((), ()))


def dot(a, b, dims=(((1,), (0,)), ((), ())), precision=None):
    return lax.dot_general(a, b, dims, precision=precision, preferred_element_type=F32)


def iota(shape, axis):
    return lax.broadcasted_iota(jnp.int32, shape, axis)


def bias_column(row):
    size = row.shape[1]
    return jnp.sum(jnp.where(iota((size, size), 0) == iota((size, size), 1), row, 0.0), axis=1, keepdims=True)


def select_kernel(assign, video, responses, out):
    owners, lines, width = out.shape
    clips, pix = video.shape
    neurons = responses.shape[1]
    pick = (iota((owners, clips), 0) == assign[...]).astype(BF)
    first = dot(pick, responses[...])
    second = dot(pick, video[...])
    rows = [first[:, p : p + width] for p in range(0, neurons, width)]
    for p in range(0, pix, width):
        piece = second[:, p : p + width]
        if piece.shape[1] < width:
            piece = jnp.concatenate([piece, jnp.zeros((owners, width - piece.shape[1]), F32)], axis=1)
        rows.append(piece)
    while len(rows) < lines:
        rows.append(jnp.zeros((owners, width), F32))
    out[...] = jnp.stack(rows, axis=1).astype(BF)


def prep_kernel(frames, weight, cbias, mix, mbias, wbig, blocks, blocks_t, bias, table, pool, unpool):
    channels, taps = weight.shape
    patch_cols = wbig.shape[1]
    group = blocks.shape[0] // channels
    t = iota(table.shape, 0)
    l = iota(table.shape, 1)
    dy = l // (DX * frames)
    dx = (l // frames) % DX
    place = dy * KS + dx
    hit = (t == place) | (t == place + KS * KS) | (t == place + 2 * KS * KS)
    last = (t == KT * KS * KS) & (l == KS * frames)
    table[...] = jnp.where(((dx < KS) & hit & (t < KT * KS * KS)) | last, 1.0, 0.0).astype(BF)
    r = iota(pool.shape, 0)
    c = iota(pool.shape, 1)
    target = (r // (2 * WW)) * (WW // 2) + (r % WW) // 2
    pool[...] = jnp.where(target == c, 0.25, 0.0).astype(BF)
    r = iota(unpool.shape, 1)
    c = iota(unpool.shape, 0)
    target = (r // (2 * WW)) * (WW // 2) + (r % WW) // 2
    unpool[...] = jnp.where(target == c, 0.25, 0.0).astype(BF)
    size = channels * group
    same = (iota((size, size), 0) // channels) == (iota((size, size), 1) // channels)
    square = mix[...].astype(F32)
    for ref, base in ((blocks, square), (blocks_t, square.T)):
        wide = jnp.concatenate([base] * group, axis=1)
        ref[...] = jnp.where(same, jnp.concatenate([wide] * group, axis=0), 0.0).astype(BF)
    bias[0] = jnp.broadcast_to(bias_column(cbias[...]), bias.shape[1:])
    bias[1] = jnp.broadcast_to(bias_column(mbias[...]), bias.shape[1:])
    tap = iota((channels, taps), 1)
    weights = weight[...].astype(F32)
    split = [
        jnp.where((tap >= dt * KS * KS) & (tap < (dt + 1) * KS * KS), weights, 0.0).astype(BF)
        for dt in range(KT)
    ]
    spread = dot(jnp.concatenate(split, axis=0), table[0:taps, :])
    source = iota((channels, patch_cols), 1) % frames
    for f in range(frames):
        total = jnp.zeros((channels, patch_cols), F32)
        for dt in range(KT):
            total = total + jnp.where(source == f + dt - 1, spread[dt * channels : (dt + 1) * channels], 0.0)
        wbig[f * channels : (f + 1) * channels, :] = total.astype(BF)


def core_forward_kernel(
    recv,
    wbig,
    blocks,
    bias,
    pool,
    mask_in,
    wt_in,
    pay,
    target,
    act1,
    slope1,
    slope2,
    xcol,
    mask,
    wt,
    pre0,
    pre1,
    mid0,
    mid1,
    feats,
    sems,
):
    copies = [pltpu.make_async_copy(wt_in, wt, sems.at[0])]
    for k, r in enumerate(range(0, mask.shape[0], SEG)):
        copies.append(pltpu.make_async_copy(mask_in.at[r : r + SEG, :], mask.at[r : r + SEG, :], sems.at[k + 1]))
    for copy in copies:
        copy.start()
    frames, _, width = recv.shape
    rows, pix = act1.shape
    channels = bias.shape[1]
    neurons = target.shape[1]
    span = blocks.shape[0]
    packet = recv[...].astype(F32)
    lines = [packet[:, j, :] for j in range((neurons + pix + width - 1) // width)]
    held = neurons // width
    for j in range(held):
        target[:, j * width : (j + 1) * width] = lines[j]
    video = jnp.concatenate(lines[held:], axis=1)[:, 0:pix]
    lane = iota((frames, pix), 1)
    col = lane % WW
    row = lane // WW
    per_store = max(1, 16 // frames)
    for dx0 in range(0, DX, per_store):
        shifted = []
        for dx in range(dx0, dx0 + per_store):
            s = dx - KS // 2
            if dx == KS:
                shifted.append(None)
            elif s == 0:
                shifted.append(video)
            else:
                rolled = pltpu.roll(video, (-s) % pix, 1)
                shifted.append(jnp.where((col + s >= 0) & (col + s < WW), rolled, 0.0))
        for dy in range(KS):
            t = dy - KS // 2
            parts = []
            for item in shifted:
                if item is None:
                    parts.append(jnp.ones((frames, pix), F32))
                elif t == 0:
                    parts.append(item)
                else:
                    moved = pltpu.roll(item, (-t * WW) % pix, 1)
                    parts.append(jnp.where((row + t >= 0) & (row + t < HH), moved, 0.0))
            base = (dy * DX + dx0) * frames
            block = parts[0] if len(parts) == 1 else jnp.concatenate(parts, axis=0)
            xcol[base : base + per_store * frames, :] = block.astype(BF)
    half = 2 * WW
    pre = (pre0, pre1)
    mid = (mid0, mid1)
    count = pix // CHUNK
    wide = wbig[...]

    def activate(source, which, act, slope, at):
        add = jnp.concatenate([bias[which]] * (CHUNK // 128), axis=1)
        for r in range(0, rows, channels):
            x = source[r : r + channels, :] + add
            e = jnp.exp(jnp.minimum(x, 0.0))
            act[r : r + channels, at] = (jnp.maximum(x, 0.0) + (e - 1.0)).astype(BF)
            slope[r : r + channels, at] = e.astype(BF)

    for t in range(count + 2):
        if t < count:
            pre[t % 2][...] = dot(wide, xcol[:, t * CHUNK : (t + 1) * CHUNK])
        if 1 <= t <= count:
            at = slice((t - 1) * CHUNK, t * CHUNK)
            activate(pre[(t - 1) % 2], 0, act1, slope1, at)
            for r in range(0, rows, span):
                mid[(t - 1) % 2][r : r + span, :] = dot(blocks[...], act1[r : r + span, at])
        if t >= 2:
            at = slice((t - 2) * CHUNK, (t - 1) * CHUNK)
            activate(mid[t % 2], 1, feats, slope2, at)
            if t % 2 == 1:
                first = (t - 3) * CHUNK
                pooled = dot(feats[:, first : first + 2 * CHUNK], pool[...])
                pay[:, first // 4 : first // 4 + half] = pooled.astype(BF)
    p = pix - CHUNK
    tail = dot(feats[:, p:pix], pool[0:CHUNK, :])
    pieces = []
    for t in range(neurons // half):
        at = t * half
        tile = lines[at // width][:, at % width : at % width + half]
        pieces += [pltpu.roll(tile, SEG, 1), tile]
    packed = jnp.concatenate(pieces, axis=0)
    pay[:, p // 4 : p // 4 + half] = jnp.where(iota((rows, half), 1) < SEG, tail, packed).astype(BF)
    for copy in copies:
        copy.wait()


def drive_terms(projected, target, w, rbias, alive, scale, channels):
    frames = target.shape[0]
    sums = [
        jnp.sum(projected[f * channels : (f + 1) * channels, :] * w, axis=0, keepdims=True)
        for f in range(frames)
    ]
    drive = jnp.concatenate(sums, axis=0) + rbias
    e = jnp.exp(-jnp.abs(drive))
    rate = jnp.maximum(drive, 0.0) + jnp.log(1.0 + e) + 0.1
    sig = jnp.where(drive >= 0, 1.0, e) / (1.0 + e)
    grad = jnp.where(alive, (1.0 - target / rate) * sig, 0.0) * scale
    return rate, grad


def mixed_rows(grad, w):
    frames = grad.shape[0]
    return jnp.concatenate([grad[f : f + 1] * w for f in range(frames)], axis=0).astype(BF)


def readout_kernel(
    scale, count, target, pay, mask, wt, rbias, pooled_grad, loss, proj0, proj1, mixed, acc
):
    pooled_n, neurons = mask.shape
    channels = wt.shape[0]
    frames = target.shape[0]
    proj = (proj0, proj1)
    block = proj0.shape[1]
    steps = neurons // block
    pooled = pay[:, 0:pooled_n]
    loss_sum = jnp.zeros((frames, block), F32)
    begun = False
    for t in range(steps + 2):
        if t < steps:
            proj[t % 2][...] = dot(pooled, mask[:, t * block : (t + 1) * block])
        if 1 <= t <= steps:
            at = slice((t - 1) * block, t * block)
            w = wt[:, at].astype(F32)
            goal = target[:, at]
            alive = ((t - 1) * block + iota((frames, block), 1)) < count[0]
            rate, grad = drive_terms(proj[(t - 1) % 2], goal, w, rbias[:, at], alive, scale, channels)
            loss_sum = loss_sum + jnp.where(alive, rate - goal * jnp.log(rate), 0.0)
            for f in range(frames):
                mixed[f * channels : (f + 1) * channels, at] = (grad[f : f + 1] * w).astype(BF)
        if t >= 2 and (t % 2 == 1 or t == steps + 1):
            low = ((t - 2) // 2) * 2 * block
            at = slice(low, (t - 1) * block)
            part = dot(mask[:, at], mixed[:, at], NT)
            acc[...] = acc[...] + part if begun else part
            begun = True
    pooled_grad[...] = acc[...].T.astype(BF)
    loss[...] = jnp.broadcast_to(jnp.sum(loss_sum, keepdims=True) * scale, loss.shape)


def core_backward_kernel(
    channels, pooled_grad, loss, act1, slope1, slope2, xcol, blocks_t, table, unpool, out, up0, up1, down0, down1, g2, g1
):
    rows, pix = act1.shape
    frames = rows // channels
    span = blocks_t.shape[0]
    group = span // channels
    patch_cols = xcol.shape[0]
    up = (up0, up1)
    down = (down0, down1)
    count = pix // CHUNK
    half = 2 * WW
    bias_sum = jnp.zeros((channels, 128), F32)
    for t in range(count + 2):
        if t < count:
            first = (t // 2) * half
            wide = min(half, pooled_grad.shape[1] - first)
            side = (t % 2) * CHUNK
            up[t % 2][...] = dot(pooled_grad[:, first : first + wide], unpool[0:wide, side : side + CHUNK])
        if 1 <= t <= count:
            at = slice((t - 1) * CHUNK, t * CHUNK)
            for r in range(0, rows, channels):
                g = (up[(t - 1) % 2][r : r + channels, :] * slope2[r : r + channels, at].astype(F32)).astype(BF)
                g2[r : r + channels, at] = g
                g = g.astype(F32)
                for c in range(0, CHUNK, 128):
                    bias_sum = bias_sum + g[:, c : c + 128]
            for r in range(0, rows, span):
                down[(t - 1) % 2][r : r + span, :] = dot(blocks_t[...], g2[r : r + span, at])
        if t >= 2:
            at = slice((t - 2) * CHUNK, (t - 1) * CHUNK)
            for r in range(0, rows, channels):
                g = down[t % 2][r : r + channels, :] * slope1[r : r + channels, at].astype(F32)
                g1[r : r + channels, at] = g.astype(BF)
    mix_bias_grad = jnp.sum(bias_sum, axis=1, keepdims=True)
    mix_grad = jnp.zeros((channels, span), F32)
    same = (iota((span, span), 0) // channels) == (iota((span, span), 1) // channels)
    for r in range(0, rows, span):
        full = jnp.where(same, dot(g2[r : r + span, :], act1[r : r + span, :], NT), 0.0)
        for a in range(group):
            mix_grad = mix_grad + full[a * channels : (a + 1) * channels]
    fold = 2 * channels
    folded = mix_grad[:, 0:fold]
    for k in range(fold, span, fold):
        folded = folded + mix_grad[:, k : k + fold]
    folded = folded + pltpu.roll(folded, channels, 1)
    full = dot(g1[...], xcol[...], NT)
    source = iota((channels, patch_cols), 1) % frames
    parts = [jnp.zeros((channels, patch_cols), F32) for _ in range(KT + 1)]
    for f in range(frames):
        piece = full[f * channels : (f + 1) * channels]
        for dt in range(KT):
            parts[dt] = parts[dt] + jnp.where(source == f + dt - 1, piece, 0.0)
        parts[KT] = parts[KT] + piece
    left = jnp.concatenate(parts, axis=0)
    taps = jnp.zeros((left.shape[0], PACK), F32)
    for _ in range(3):
        term = left.astype(BF)
        left = left - term.astype(F32)
        taps = taps + dot(term, table[...], NT)
    lane = iota((channels, PACK), 1)
    conv = jnp.zeros((channels, PACK), F32)
    for dt in range(KT + 1):
        inside = (lane >= dt * KS * KS) & (lane < (dt + 1) * KS * KS)
        conv = conv + jnp.where(inside, taps[dt * channels : (dt + 1) * channels], 0.0)
    used = KT * KS * KS + 1
    low = lane[:, 0:128]
    upper = jnp.where(low < used - 128, conv[:, 128:256], 0.0)
    upper = jnp.where(low == used - 128, mix_bias_grad, upper)
    upper = jnp.where((low == used - 127) & (iota((channels, 128), 0) == 0), loss[0:1, 0:1], upper)
    upper = jnp.where(low >= channels, folded, upper)
    pieces, lines, _ = out.shape
    both = jnp.concatenate([conv[:, 0:128], upper], axis=0)
    for k in range(pieces):
        out[k] = both[k * lines : (k + 1) * lines, :]


def share_kernel(parts, out):
    total = parts.shape[0]
    tile = parts[0]
    for d in range(1, total):
        tile = tile + parts[d]
    for d in range(total):
        out[d] = tile


def unpack_kernel(parts, conv, conv_bias, mix, mix_bias, loss):
    channels, taps = conv.shape
    both = jnp.concatenate([parts[k] for k in range(parts.shape[0])], axis=0)
    low = both[0:channels]
    high = both[channels:]
    rest = taps - 128
    conv[...] = jnp.concatenate([low, high], axis=1)[:, 0:taps]
    mix[...] = pltpu.roll(high, 128 - channels, 1)[:, 0:channels]
    same = iota((channels, channels), 0) == iota((channels, channels), 1)
    conv_bias[...] = jnp.sum(jnp.where(same, high[:, rest : rest + 1], 0.0), axis=0, keepdims=True)
    mix_bias[...] = jnp.sum(jnp.where(same, high[:, rest + 1 : rest + 2], 0.0), axis=0, keepdims=True)
    loss[...] = high[0:1, rest + 2 : rest + 3]


def owned_rows_kernel(scale, clips, own, block, held, where, count, *refs):
    pays = refs[:clips]
    wt, rbias, mask_in = refs[clips : clips + 3]
    channels = refs[clips].shape[0]
    before = refs[clips + 3 : clips + 3 + held]
    outs = refs[clips + 3 + held : -8]
    proj0, proj1, mixed0, mixed1, turned, mask, stage, sems = refs[-8:]
    proj = (proj0, proj1)
    mixed = (mixed0, mixed1)
    pooled_n = mask.shape[0]
    low_rows = pooled_n + channels
    rows = pays[0].shape[0]
    frames = rows // channels
    steps = own // block
    first = pl.multiple_of(where[0] * own, own)
    fetches = []
    for k in range(steps):
        lanes = pl.ds(pl.multiple_of(first + k * block, block), block)
        fetches.append(pltpu.make_async_copy(mask_in.at[:, lanes], mask.at[:, k * block : (k + 1) * block], sems.at[k]))
        fetches[k].start()
    for c in range(clips):
        turned[:, c * rows : (c + 1) * rows] = pays[c][:, 0:pooled_n].T
    segs = block // SEG
    low = iota((frames, 128), 1) < SEG
    items = [(k, c) for k in range(steps) for c in range(clips)]
    feats = [jnp.zeros((channels, block), F32) for _ in range(steps)]
    biases = [jnp.zeros((frames, block), F32) for _ in range(steps)]
    stores = []
    for t in range(len(items) + 2):
        if t < len(items):
            k, c = items[t]
            if c == 0:
                fetches[k].wait()
            proj[t % 2][...] = dot(pays[c][:, 0:pooled_n], mask[:, k * block : (k + 1) * block])
        if 1 <= t <= len(items):
            k, c = items[t - 1]
            start = pl.multiple_of(first + k * block, block)
            base = pl.multiple_of(start // SEG * frames, segs * frames)
            packed = pays[c][pl.ds(base, segs * frames), pooled_n - SEG : pooled_n + SEG].astype(F32)
            tiles = []
            for j in range(0, segs, 2):
                even = packed[j * frames : (j + 1) * frames]
                odd = packed[(j + 1) * frames : (j + 2) * frames]
                tiles.append(jnp.where(low, pltpu.roll(even, SEG, 1), odd))
            target = jnp.concatenate(tiles, axis=1)
            w = wt[:, pl.ds(start, block)].astype(F32)
            alive = (start + iota((frames, block), 1)) < count[0]
            now = proj[(t - 1) % 2]
            _, grad = drive_terms(now, target, w, rbias[:, pl.ds(start, block)], alive, scale, channels)
            for f in range(frames):
                feats[k] = feats[k] + grad[f : f + 1] * now[f * channels : (f + 1) * channels, :]
                at = c * rows + f * channels
                mixed[k % 2][at : at + channels, :] = (grad[f : f + 1] * w).astype(BF)
            biases[k] = biases[k] + grad
        if t >= 2 and items[t - 2][1] == clips - 1:
            k = items[t - 2][0]
            at = slice(k * block, (k + 1) * block)
            total = dot(turned[...], mixed[k % 2][...])
            bias = jnp.sum(biases[k], axis=0, keepdims=True)
            if held:
                stage[:, at] = total + before[0][0:pooled_n, at]
                outs[1][:, at] = feats[k] + before[0][pooled_n:low_rows, at]
                outs[2][:, at] = bias + before[0][low_rows : low_rows + 1, at]
                stores.append(pltpu.make_async_copy(stage.at[:, at], outs[0].at[:, at], sems.at[steps + k]))
                stores[-1].start()
            else:
                outs[0][0:pooled_n, at] = total
                outs[0][pooled_n:low_rows, at] = feats[k]
                outs[0][low_rows:, at] = jnp.broadcast_to(bias, (8, block))
    for store in stores:
        store.wait()


def params(limit=20):
    return pltpu.CompilerParams(vmem_limit_bytes=limit << 20)


def cost(flops, moved=1 << 20):
    return pl.CostEstimate(flops=int(flops), transcendentals=0, bytes_accessed=int(moved))


def in_hbm(*arrays):
    return [pltpu.with_memory_space_constraint(a, pltpu.HBM) for a in arrays]


def xor_pairs(size, mask):
    return [(i, i ^ mask) for i in range(size)]


def per_device(
    video, responses, assignment, counts, conv_weight, conv_bias, mix_weight, mix_bias, masks, feat_w, readout_bias
):
    sess_total = lax.axis_size("sess")
    clip_total = lax.axis_size("clip")
    total = sess_total * clip_total
    clip_block, frame_block, pix = video.shape
    neurons = responses.shape[2]
    pooled_n = masks.shape[2]
    channels, taps = conv_weight.shape
    frames = frame_block * sess_total
    rows = frames * channels
    own = neurons // clip_total
    block = min(512, own)
    assert clip_block == sess_total and frame_block == 1 and masks.shape[0] == 1
    assert neurons == channels * SEG and pooled_n % 128 == SEG and pix == HH * WW
    scale = 1.0 / (clip_block * clip_total * frames)

    group = max(1, 256 // channels)
    lines = 16
    packet = 512
    assert neurons + pix <= lines * packet
    send = pl.pallas_call(
        select_kernel,
        out_shape=jax.ShapeDtypeStruct((sess_total, lines, packet), BF),
        compiler_params=params(),
        name="select",
    )(*in_hbm(assignment[None, :], video.reshape(clip_block, pix), responses.reshape(clip_block, neurons)))
    recv = lax.all_to_all(send, "sess", split_axis=0, concat_axis=0, tiled=True)

    patch_cols = KS * DX * frames
    span = channels * group
    half = 2 * WW
    wbig, blocks, blocks_t, bias, table, pool, unpool = pl.pallas_call(
        functools.partial(prep_kernel, frames),
        out_shape=(
            jax.ShapeDtypeStruct((rows, patch_cols), BF),
            jax.ShapeDtypeStruct((span, span), BF),
            jax.ShapeDtypeStruct((span, span), BF),
            jax.ShapeDtypeStruct((2, channels, 128), F32),
            jax.ShapeDtypeStruct((PACK, patch_cols), BF),
            jax.ShapeDtypeStruct((4 * half, half), BF),
            jax.ShapeDtypeStruct((half, 4 * half), BF),
        ),
        compiler_params=params(),
        cost_estimate=cost(1 << 27),
        name="prep",
    )(*in_hbm(conv_weight, conv_bias[None, :], mix_weight, mix_bias[None, :]))

    wt = jnp.swapaxes(feat_w, 1, 2).reshape(channels, neurons)
    mask_t = jnp.swapaxes(masks, 1, 2).reshape(pooled_n, neurons)
    mask_t, wt, rbias = in_hbm(mask_t, wt, readout_bias)
    width = pooled_n + SEG
    vmem = pl.BlockSpec(memory_space=pltpu.VMEM)
    anywhere = pl.BlockSpec(memory_space=pl.ANY)
    smem = pl.BlockSpec(memory_space=pltpu.SMEM)
    pay, target, act1, slope1, slope2, xcol, mask_v, wt_v = pl.pallas_call(
        core_forward_kernel,
        out_shape=(
            jax.ShapeDtypeStruct((rows, width), BF),
            jax.ShapeDtypeStruct((frames, neurons), F32),
            jax.ShapeDtypeStruct((rows, pix), BF),
            jax.ShapeDtypeStruct((rows, pix), BF),
            jax.ShapeDtypeStruct((rows, pix), BF),
            jax.ShapeDtypeStruct((patch_cols, pix), BF),
            jax.ShapeDtypeStruct((pooled_n, neurons), BF),
            jax.ShapeDtypeStruct((channels, neurons), BF),
        ),
        in_specs=[vmem] * 5 + [anywhere] * 2,
        scratch_shapes=[pltpu.VMEM((rows, CHUNK), F32)] * 4
        + [pltpu.VMEM((rows, pix), BF), pltpu.SemaphoreType.DMA((1 + pooled_n // SEG,))],
        compiler_params=params(),
        cost_estimate=cost(2 * rows * pix * patch_cols, 8 * rows * pix),
        name="core_forward",
    )(recv, wbig, blocks, bias, pool, mask_t, wt)

    near = {0: pay}
    for mask in range(1, clip_total):
        if mask % 2 == 0 or mask == 1:
            near[mask] = lax.ppermute(pay, "clip", xor_pairs(clip_total, mask))

    big = min(512, neurons)
    work = 2 * rows * neurons * pooled_n
    where = lax.axis_index("clip").astype(jnp.int32)[None]
    pooled_grad, loss = pl.pallas_call(
        functools.partial(readout_kernel, scale),
        in_specs=[smem] + [vmem] * 5,
        out_shape=(jax.ShapeDtypeStruct((rows, pooled_n), BF), jax.ShapeDtypeStruct((8, 128), F32)),
        scratch_shapes=[pltpu.VMEM((rows, big), F32)] * 2
        + [pltpu.VMEM((rows, neurons), BF), pltpu.VMEM((pooled_n, rows), F32)],
        compiler_params=params(),
        cost_estimate=cost(2 * work, 2 * neurons * pooled_n),
        name="readout",
    )(counts, target, pay, mask_v, wt_v, rbias)

    assert 2 * channels % total == 0
    pieces = (total, 2 * channels // total, 128)
    core = pl.pallas_call(
        functools.partial(core_backward_kernel, channels),
        out_shape=jax.ShapeDtypeStruct(pieces, F32),
        scratch_shapes=[pltpu.VMEM((rows, CHUNK), F32)] * 4 + [pltpu.VMEM((rows, pix), BF)] * 2,
        compiler_params=params(),
        cost_estimate=cost(2 * work, 8 * rows * pix),
        name="core_backward",
    )(pooled_grad, loss, act1, slope1, slope2, xcol, blocks_t, table, unpool)

    axes = ("clip", "sess")
    parts = lax.all_to_all(core, axes, split_axis=0, concat_axis=0, tiled=True)

    def owned_rows(clips, held):
        last = len(held) > 0
        return pl.pallas_call(
            functools.partial(owned_rows_kernel, scale, len(clips), own, block, len(held)),
            in_specs=[smem, smem] + [vmem] * (len(clips) + 2) + [anywhere] + [vmem] * len(held),
            out_specs=[anywhere, vmem, vmem] if last else [vmem],
            out_shape=[
                jax.ShapeDtypeStruct((pooled_n, own), F32),
                jax.ShapeDtypeStruct((channels, own), F32),
                jax.ShapeDtypeStruct((1, own), F32),
            ]
            if last
            else [jax.ShapeDtypeStruct((pooled_n + channels + 8, own), F32)],
            scratch_shapes=[pltpu.VMEM((rows, block), F32)] * 2
            + [pltpu.VMEM((len(clips) * rows, block), BF)] * 2
            + [
                pltpu.VMEM((pooled_n, len(clips) * rows), BF),
                pltpu.VMEM((pooled_n, own), BF),
                pltpu.VMEM((pooled_n, own) if last else (8, 128), F32),
                pltpu.SemaphoreType.DMA((2 * (own // block),)),
            ],
            compiler_params=params(),
            cost_estimate=cost(2 * work * len(clips) // clip_total, 4 * own * pooled_n),
            name="owned_rows",
        )(where, counts, *clips, wt_v, rbias, mask_t, *held)

    readout_grads = owned_rows([near[0], near[1]], ())
    far = [mask for mask in near if mask > 1]
    parts, readout_grads, reached = lax.optimization_barrier((parts, readout_grads, [near[mask] for mask in far]))
    others = []
    for value in reached:
        others += [value, lax.ppermute(value, "clip", xor_pairs(clip_total, 1))]
    copies = pl.pallas_call(
        share_kernel,
        out_shape=jax.ShapeDtypeStruct(pieces, F32),
        compiler_params=params(),
        name="share",
    )(parts)
    summed = lax.all_to_all(copies, axes, split_axis=0, concat_axis=0, tiled=True)
    readout_grads = owned_rows(others, readout_grads)
    summed, readout_grads = lax.optimization_barrier((summed, readout_grads))
    mask_grad, feat_grad, grad_rbias = readout_grads
    grad_conv, grad_cb, grad_mix, grad_mb, loss = pl.pallas_call(
        unpack_kernel,
        out_shape=(
            jax.ShapeDtypeStruct((channels, taps), F32),
            jax.ShapeDtypeStruct((1, channels), F32),
            jax.ShapeDtypeStruct((channels, channels), F32),
            jax.ShapeDtypeStruct((1, channels), F32),
            jax.ShapeDtypeStruct((1, 1), F32),
        ),
        compiler_params=params(),
        name="unpack",
    )(summed)
    return (
        loss.reshape(()),
        grad_conv,
        grad_cb.reshape(channels),
        grad_mix,
        grad_mb.reshape(channels),
        jnp.swapaxes(mask_grad[None], 1, 2),
        jnp.swapaxes(feat_grad[None], 1, 2),
        grad_rbias,
    )


def solution(mesh):
    return jax.shard_map(
        per_device,
        mesh=mesh,
        in_specs=(
            P("clip", "sess", None),
            P("clip", "sess", None),
            P("clip"),
            P("sess"),
            P(),
            P(),
            P(),
            P(),
            P("sess", None, None),
            P("sess", None, None),
            P("sess", None),
        ),
        out_specs=(
            P(),
            P(),
            P(),
            P(),
            P(),
            P("sess", "clip", None),
            P("sess", "clip", None),
            P("sess", "clip"),
        ),
        check_vma=False,
    )
```

```python
import functools

import jax
import jax.numpy as jnp
from jax import lax
from jax.experimental import pallas as pl
from jax.experimental.pallas import tpu as pltpu
from jax.sharding import PartitionSpec as P

HH = 36
WW = 64
KS = 7
KT = 3
DX = 8
PACK = 256
SEG = 64
CHUNK = 4 * WW
BF = jnp.bfloat16
F32 = jnp.float32
NT = (((1,), (1,)), ((), ()))


def dot(a, b, dims=(((1,), (0,)), ((), ())), precision=None):
    return lax.dot_general(a, b, dims, precision=precision, preferred_element_type=F32)


def iota(shape, axis):
    return lax.broadcasted_iota(jnp.int32, shape, axis)


def bias_column(row):
    size = row.shape[1]
    return jnp.sum(jnp.where(iota((size, size), 0) == iota((size, size), 1), row, 0.0), axis=1, keepdims=True)


def select_kernel(assign, video, responses, out):
    owners, lines, width = out.shape
    clips, pix = video.shape
    neurons = responses.shape[1]
    pick = (iota((owners, clips), 0) == assign[...]).astype(BF)
    first = dot(pick, responses[...])
    second = dot(pick, video[...])
    rows = [first[:, p : p + width] for p in range(0, neurons, width)]
    for p in range(0, pix, width):
        piece = second[:, p : p + width]
        if piece.shape[1] < width:
            piece = jnp.concatenate([piece, jnp.zeros((owners, width - piece.shape[1]), F32)], axis=1)
        rows.append(piece)
    while len(rows) < lines:
        rows.append(jnp.zeros((owners, width), F32))
    out[...] = jnp.stack(rows, axis=1).astype(BF)


def fill_table(table, frames):
    t = iota(table.shape, 0)
    l = iota(table.shape, 1)
    dy = l // (DX * frames)
    dx = (l // frames) % DX
    place = dy * KS + dx
    hit = (t == place) | (t == place + KS * KS) | (t == place + 2 * KS * KS)
    last = (t == KT * KS * KS) & (l == KS * frames)
    table[...] = jnp.where(((dx < KS) & hit & (t < KT * KS * KS)) | last, 1.0, 0.0).astype(BF)


def pool_weights(shape, pixel_axis):
    pixel = iota(shape, pixel_axis)
    target = (pixel // (2 * WW)) * (WW // 2) + (pixel % WW) // 2
    return jnp.where(target == iota(shape, 1 - pixel_axis), 0.25, 0.0).astype(BF)


def prep_kernel(frames, weight, cbias, mix, mbias, wbig, blocks, blocks_t, bias, pool, table):
    channels, taps = weight.shape
    patch_cols = wbig.shape[1]
    group = blocks.shape[0] // channels
    fill_table(table, frames)
    pool[...] = pool_weights(pool.shape, 0)
    size = channels * group
    same = (iota((size, size), 0) // channels) == (iota((size, size), 1) // channels)
    square = mix[...].astype(F32)
    for ref, base in ((blocks, square), (blocks_t, square.T)):
        wide = jnp.concatenate([base] * group, axis=1)
        ref[...] = jnp.where(same, jnp.concatenate([wide] * group, axis=0), 0.0).astype(BF)
    bias[0] = jnp.broadcast_to(bias_column(cbias[...]), bias.shape[1:])
    bias[1] = jnp.broadcast_to(bias_column(mbias[...]), bias.shape[1:])
    tap = iota((channels, taps), 1)
    weights = weight[...].astype(F32)
    split = [
        jnp.where((tap >= dt * KS * KS) & (tap < (dt + 1) * KS * KS), weights, 0.0).astype(BF)
        for dt in range(KT)
    ]
    spread = dot(jnp.concatenate(split, axis=0), table[0:taps, :])
    source = iota((channels, patch_cols), 1) % frames
    for f in range(frames):
        total = jnp.zeros((channels, patch_cols), F32)
        for dt in range(KT):
            total = total + jnp.where(source == f + dt - 1, spread[dt * channels : (dt + 1) * channels], 0.0)
        wbig[f * channels : (f + 1) * channels, :] = total.astype(BF)


def core_forward_kernel(
    recv,
    wbig,
    blocks,
    bias,
    pool,
    mask_in,
    pay,
    pay_send,
    target,
    act1,
    slope1,
    slope2,
    xcol,
    mask,
    pre0,
    pre1,
    mid0,
    mid1,
    feats,
    sems,
):
    copies = []
    for k, at in enumerate(range(0, mask.shape[1], 512)):
        copies.append(pltpu.make_async_copy(mask_in.at[:, at : at + 512], mask.at[:, at : at + 512], sems.at[k]))
        copies[k].start()
    frames, _, width = recv.shape
    rows, pix = act1.shape
    channels = bias.shape[1]
    neurons = target.shape[1]
    span = blocks.shape[0]
    packet = recv[...].astype(F32)
    lines = [packet[:, j, :] for j in range((neurons + pix + width - 1) // width)]
    held = neurons // width
    for j in range(held):
        target[:, j * width : (j + 1) * width] = lines[j]
    video = jnp.concatenate(lines[held:], axis=1)[:, 0:pix]
    lane = iota((frames, pix), 1)
    col = lane % WW
    row = lane // WW
    per_store = max(1, 16 // frames)
    for dx0 in range(0, DX, per_store):
        shifted = []
        for dx in range(dx0, dx0 + per_store):
            s = dx - KS // 2
            if dx == KS:
                shifted.append(None)
            elif s == 0:
                shifted.append(video)
            else:
                rolled = pltpu.roll(video, (-s) % pix, 1)
                shifted.append(jnp.where((col + s >= 0) & (col + s < WW), rolled, 0.0))
        for dy in range(KS):
            t = dy - KS // 2
            parts = []
            for item in shifted:
                if item is None:
                    parts.append(jnp.ones((frames, pix), F32))
                elif t == 0:
                    parts.append(item)
                else:
                    moved = pltpu.roll(item, (-t * WW) % pix, 1)
                    parts.append(jnp.where((row + t >= 0) & (row + t < HH), moved, 0.0))
            base = (dy * DX + dx0) * frames
            block = parts[0] if len(parts) == 1 else jnp.concatenate(parts, axis=0)
            xcol[base : base + per_store * frames, :] = block.astype(BF)
    half = 2 * WW
    pre = (pre0, pre1)
    mid = (mid0, mid1)

    def send(at):
        lanes = slice(at, at + half)
        copies.append(pltpu.make_async_copy(pay.at[:, lanes], pay_send.at[:, lanes], sems.at[len(copies)]))
        copies[-1].start()

    count = pix // CHUNK
    wide = wbig[...]

    def activate(source, which, act, slope, at):
        add = jnp.concatenate([bias[which]] * (CHUNK // 128), axis=1)
        for r in range(0, rows, channels):
            x = source[r : r + channels, :] + add
            e = jnp.exp(jnp.minimum(x, 0.0))
            act[r : r + channels, at] = (jnp.maximum(x, 0.0) + (e - 1.0)).astype(BF)
            slope[r : r + channels, at] = e.astype(BF)

    for t in range(count + 2):
        if t < count:
            pre[t % 2][...] = dot(wide, xcol[:, t * CHUNK : (t + 1) * CHUNK])
        if 1 <= t <= count:
            at = slice((t - 1) * CHUNK, t * CHUNK)
            activate(pre[(t - 1) % 2], 0, act1, slope1, at)
            for r in range(0, rows, span):
                mid[(t - 1) % 2][r : r + span, :] = dot(blocks[...], act1[r : r + span, at])
        if t >= 2:
            at = slice((t - 2) * CHUNK, (t - 1) * CHUNK)
            activate(mid[t % 2], 1, feats, slope2, at)
            if t % 2 == 1:
                first = (t - 3) * CHUNK
                pooled = dot(feats[:, first : first + 2 * CHUNK], pool[...])
                pay[:, first // 4 : first // 4 + half] = pooled.astype(BF)
                send(first // 4)
    p = pix - CHUNK
    tail = dot(feats[:, p:pix], pool[0:CHUNK, :])
    pieces = []
    for t in range(neurons // half):
        at = t * half
        tile = lines[at // width][:, at % width : at % width + half]
        pieces += [pltpu.roll(tile, SEG, 1), tile]
    packed = jnp.concatenate(pieces, axis=0)
    pay[:, p // 4 : p // 4 + half] = jnp.where(iota((rows, half), 1) < SEG, tail, packed).astype(BF)
    send(p // 4)
    for copy in copies:
        copy.wait()


def drive_terms(projected, target, w, rbias, alive, scale, channels):
    frames = target.shape[0]
    sums = [
        jnp.sum(projected[f * channels : (f + 1) * channels, :] * w, axis=0, keepdims=True)
        for f in range(frames)
    ]
    drive = jnp.concatenate(sums, axis=0) + rbias
    e = jnp.exp(-jnp.abs(drive))
    rate = jnp.maximum(drive, 0.0) + jnp.log(1.0 + e) + 0.1
    sig = jnp.where(drive >= 0, 1.0, e) / (1.0 + e)
    grad = jnp.where(alive, (1.0 - target / rate) * sig, 0.0) * scale
    return rate, grad


def readout_kernel(
    scale, count, target, pay, mask_near, mask_in, wt, rbias, pooled_grad, loss, mask_late, proj0, proj1, mixed, acc, sems
):
    pooled_n, early = mask_near.shape
    neurons = early + mask_late.shape[1]
    channels = wt.shape[0]
    frames = target.shape[0]
    proj = (proj0, proj1)
    block = proj0.shape[1]
    steps = neurons // block
    copies = {}
    for at in range(early, neurons, block):
        lanes = slice(at - early, at - early + block)
        copies[at] = pltpu.make_async_copy(
            mask_in.at[:, at : at + block], mask_late.at[:, lanes], sems.at[(at - early) // block]
        )
        copies[at].start()

    def mask_part(at, size):
        if at < early:
            return mask_near[:, at : at + size]
        return mask_late[:, at - early : at - early + size]

    pooled = pay[:, 0:pooled_n]
    loss_sum = jnp.zeros((frames, block), F32)
    begun = False
    for t in range(steps + 2):
        if t < steps:
            if t * block in copies:
                copies[t * block].wait()
            proj[t % 2][...] = dot(pooled, mask_part(t * block, block))
        if 1 <= t <= steps:
            at = slice((t - 1) * block, t * block)
            w = wt[:, at].astype(F32)
            goal = target[:, at]
            alive = ((t - 1) * block + iota((frames, block), 1)) < count[0]
            rate, grad = drive_terms(proj[(t - 1) % 2], goal, w, rbias[:, at], alive, scale, channels)
            loss_sum = loss_sum + jnp.where(alive, rate - goal * jnp.log(rate), 0.0)
            for f in range(frames):
                mixed[f * channels : (f + 1) * channels, at] = (grad[f : f + 1] * w).astype(BF)
        if t >= 2 and (t % 2 == 1 or t == steps + 1):
            low = ((t - 2) // 2) * 2 * block
            at = slice(low, (t - 1) * block)
            part = dot(mask_part(low, (t - 1) * block - low), mixed[:, at], NT)
            acc[...] = acc[...] + part if begun else part
            begun = True
    pooled_grad[...] = acc[...].T.astype(BF)
    loss[...] = jnp.broadcast_to(jnp.sum(loss_sum, keepdims=True) * scale, loss.shape)


def core_backward_kernel(
    channels, pooled_grad, loss, act1, slope1, slope2, xcol, blocks_t, out, up0, up1, down0, down1, g2, g1, table
):
    rows, pix = act1.shape
    frames = rows // channels
    span = blocks_t.shape[0]
    group = span // channels
    patch_cols = xcol.shape[0]
    up = (up0, up1)
    down = (down0, down1)
    count = pix // CHUNK
    half = 2 * WW
    unpool = pool_weights((half, 4 * half), 1)
    fill_table(table, frames)
    bias_sum = jnp.zeros((channels, 128), F32)
    for t in range(count + 2):
        if t < count:
            first = (t // 2) * half
            wide = min(half, pooled_grad.shape[1] - first)
            side = (t % 2) * CHUNK
            up[t % 2][...] = dot(pooled_grad[:, first : first + wide], unpool[0:wide, side : side + CHUNK])
        if 1 <= t <= count:
            at = slice((t - 1) * CHUNK, t * CHUNK)
            for r in range(0, rows, channels):
                g = (up[(t - 1) % 2][r : r + channels, :] * slope2[r : r + channels, at].astype(F32)).astype(BF)
                g2[r : r + channels, at] = g
                g = g.astype(F32)
                for c in range(0, CHUNK, 128):
                    bias_sum = bias_sum + g[:, c : c + 128]
            for r in range(0, rows, span):
                down[(t - 1) % 2][r : r + span, :] = dot(blocks_t[...], g2[r : r + span, at])
        if t >= 2:
            at = slice((t - 2) * CHUNK, (t - 1) * CHUNK)
            for r in range(0, rows, channels):
                g = down[t % 2][r : r + channels, :] * slope1[r : r + channels, at].astype(F32)
                g1[r : r + channels, at] = g.astype(BF)
    mix_bias_grad = jnp.sum(bias_sum, axis=1, keepdims=True)
    mix_grad = jnp.zeros((channels, span), F32)
    same = (iota((span, span), 0) // channels) == (iota((span, span), 1) // channels)
    for r in range(0, rows, span):
        full = jnp.where(same, dot(g2[r : r + span, :], act1[r : r + span, :], NT), 0.0)
        for a in range(group):
            mix_grad = mix_grad + full[a * channels : (a + 1) * channels]
    fold = 2 * channels
    folded = mix_grad[:, 0:fold]
    for k in range(fold, span, fold):
        folded = folded + mix_grad[:, k : k + fold]
    folded = folded + pltpu.roll(folded, channels, 1)
    full = dot(g1[...], xcol[...], NT)
    source = iota((channels, patch_cols), 1) % frames
    parts = [jnp.zeros((channels, patch_cols), F32) for _ in range(KT + 1)]
    for f in range(frames):
        piece = full[f * channels : (f + 1) * channels]
        for dt in range(KT):
            parts[dt] = parts[dt] + jnp.where(source == f + dt - 1, piece, 0.0)
        parts[KT] = parts[KT] + piece
    left = jnp.concatenate(parts, axis=0)
    taps = jnp.zeros((left.shape[0], PACK), F32)
    for _ in range(3):
        term = left.astype(BF)
        left = left - term.astype(F32)
        taps = taps + dot(term, table[...], NT)
    lane = iota((channels, PACK), 1)
    conv = jnp.zeros((channels, PACK), F32)
    for dt in range(KT + 1):
        inside = (lane >= dt * KS * KS) & (lane < (dt + 1) * KS * KS)
        conv = conv + jnp.where(inside, taps[dt * channels : (dt + 1) * channels], 0.0)
    used = KT * KS * KS + 1
    low = lane[:, 0:128]
    upper = jnp.where(low < used - 128, conv[:, 128:256], 0.0)
    upper = jnp.where(low == used - 128, mix_bias_grad, upper)
    upper = jnp.where((low == used - 127) & (iota((channels, 128), 0) == 0), loss[0:1, 0:1], upper)
    upper = jnp.where(low >= channels, folded, upper)
    pieces, lines, _ = out.shape
    both = jnp.concatenate([conv[:, 0:128], upper], axis=0)
    for k in range(pieces):
        out[k] = both[k * lines : (k + 1) * lines, :]


def share_kernel(parts, out):
    total = parts.shape[0]
    tile = parts[0]
    for d in range(1, total):
        tile = tile + parts[d]
    for d in range(total):
        out[d] = tile


def unpack_kernel(parts, conv, conv_bias, mix, mix_bias, loss):
    channels, taps = conv.shape
    both = jnp.concatenate([parts[k] for k in range(parts.shape[0])], axis=0)
    low = both[0:channels]
    high = both[channels:]
    rest = taps - 128
    conv[...] = jnp.concatenate([low, high], axis=1)[:, 0:taps]
    mix[...] = pltpu.roll(high, 128 - channels, 1)[:, 0:channels]
    same = iota((channels, channels), 0) == iota((channels, channels), 1)
    conv_bias[...] = jnp.sum(jnp.where(same, high[:, rest : rest + 1], 0.0), axis=0, keepdims=True)
    mix_bias[...] = jnp.sum(jnp.where(same, high[:, rest + 1 : rest + 2], 0.0), axis=0, keepdims=True)
    loss[...] = high[0:1, rest + 2 : rest + 3]


def owned_rows_kernel(scale, clips, own, block, held, where, count, *refs):
    sent = refs[:clips]
    wt_in, mask_in, rbias = refs[clips : clips + 3]
    before = refs[clips + 3 : clips + 3 + held]
    outs = refs[clips + 3 + held : -10]
    pays, wt, proj0, proj1, mixed0, mixed1, turned, mask, stage, sems = refs[-10:]
    proj = (proj0, proj1)
    mixed = (mixed0, mixed1)
    pooled_n = mask.shape[0]
    channels = wt.shape[0]
    low_rows = pooled_n + channels
    rows = pays.shape[1]
    frames = rows // channels
    steps = own // block
    first = pl.multiple_of(where[0] * own, own)
    fetches = []
    for k in range(steps):
        lanes = pl.ds(pl.multiple_of(first + k * block, block), block)
        fetches.append(pltpu.make_async_copy(mask_in.at[:, lanes], mask.at[:, k * block : (k + 1) * block], sems.at[k]))
    arrive = [pltpu.make_async_copy(sent[c], pays.at[c], sems.at[2 * steps + c]) for c in range(clips)]
    weights = pltpu.make_async_copy(wt_in.at[:, pl.ds(first, own)], wt, sems.at[2 * steps + clips])
    arrive[0].start()
    fetches[0].start()
    weights.start()
    for copy in arrive[1:] + fetches[1:]:
        copy.start()
    segs = block // SEG
    low = iota((frames, 128), 1) < SEG
    items = [(k, c) for k in range(steps) for c in range(clips)]
    feats = [jnp.zeros((channels, block), F32) for _ in range(steps)]
    biases = [jnp.zeros((frames, block), F32) for _ in range(steps)]
    stores = []
    for t in range(len(items) + 2):
        if t < len(items):
            k, c = items[t]
            if k == 0:
                arrive[c].wait()
                turned[:, c * rows : (c + 1) * rows] = pays[c, :, 0:pooled_n].T
            if c == 0:
                fetches[k].wait()
            if t == 0:
                weights.wait()
            proj[t % 2][...] = dot(pays[c, :, 0:pooled_n], mask[:, k * block : (k + 1) * block])
        if 1 <= t <= len(items):
            k, c = items[t - 1]
            start = pl.multiple_of(first + k * block, block)
            base = pl.multiple_of(start // SEG * frames, segs * frames)
            packed = pays[c, pl.ds(base, segs * frames), pooled_n - SEG : pooled_n + SEG].astype(F32)
            tiles = []
            for j in range(0, segs, 2):
                even = packed[j * frames : (j + 1) * frames]
                odd = packed[(j + 1) * frames : (j + 2) * frames]
                tiles.append(jnp.where(low, pltpu.roll(even, SEG, 1), odd))
            target = jnp.concatenate(tiles, axis=1)
            w = wt[:, k * block : (k + 1) * block].astype(F32)
            alive = (start + iota((frames, block), 1)) < count[0]
            now = proj[(t - 1) % 2]
            _, grad = drive_terms(now, target, w, rbias[:, pl.ds(start, block)], alive, scale, channels)
            for f in range(frames):
                feats[k] = feats[k] + grad[f : f + 1] * now[f * channels : (f + 1) * channels, :]
                at = c * rows + f * channels
                mixed[k % 2][at : at + channels, :] = (grad[f : f + 1] * w).astype(BF)
            biases[k] = biases[k] + grad
        if t >= 2 and items[t - 2][1] == clips - 1:
            k = items[t - 2][0]
            at = slice(k * block, (k + 1) * block)
            total = dot(turned[...], mixed[k % 2][...])
            bias = jnp.sum(biases[k], axis=0, keepdims=True)
            if held:
                stage[:, at] = total + before[0][0:pooled_n, at]
                outs[1][:, at] = feats[k] + before[0][pooled_n:low_rows, at]
                outs[2][:, at] = bias + before[0][low_rows : low_rows + 1, at]
                stores.append(pltpu.make_async_copy(stage.at[:, at], outs[0].at[:, at], sems.at[steps + k]))
                stores[-1].start()
            else:
                outs[0][0:pooled_n, at] = total
                outs[0][pooled_n:low_rows, at] = feats[k]
                outs[0][low_rows:, at] = jnp.broadcast_to(bias, (8, block))
    for store in stores:
        store.wait()


def params(rows=512):
    return pltpu.CompilerParams(vmem_limit_bytes=min(56, 20 * max(1, rows // 512)) << 20)


def cost(flops, moved=1 << 20):
    return pl.CostEstimate(flops=int(flops), transcendentals=0, bytes_accessed=int(moved))


def in_hbm(*arrays):
    return [pltpu.with_memory_space_constraint(a, pltpu.HBM) for a in arrays]


def xor_pairs(size, mask):
    return [(i, i ^ mask) for i in range(size)]


def per_device(
    video, responses, assignment, counts, conv_weight, conv_bias, mix_weight, mix_bias, masks, feat_w, readout_bias
):
    sess_total = lax.axis_size("sess")
    clip_total = lax.axis_size("clip")
    total = sess_total * clip_total
    clip_block, frame_block, pix = video.shape
    neurons = responses.shape[2]
    pooled_n = masks.shape[2]
    channels, taps = conv_weight.shape
    frames = frame_block * sess_total
    rows = frames * channels
    own = neurons // clip_total
    block = min(512, own)
    assert clip_block == sess_total and frame_block == 1 and masks.shape[0] == 1
    assert neurons == channels * SEG and pooled_n % 128 == SEG and pix == HH * WW
    scale = 1.0 / (clip_block * clip_total * frames)

    group = max(1, 256 // channels)
    lines = 16
    packet = 512
    assert neurons + pix <= lines * packet
    send = pl.pallas_call(
        select_kernel,
        out_shape=jax.ShapeDtypeStruct((sess_total, lines, packet), BF),
        compiler_params=params(),
        name="select",
    )(*in_hbm(assignment[None, :], video.reshape(clip_block, pix), responses.reshape(clip_block, neurons)))
    where = lax.axis_index("clip").astype(jnp.int32)[None]
    send, where = lax.optimization_barrier((send, where))
    recv = lax.all_to_all(send, "sess", split_axis=0, concat_axis=0, tiled=True)

    patch_cols = KS * DX * frames
    span = channels * group
    half = 2 * WW
    wbig, blocks, blocks_t, bias, pool = pl.pallas_call(
        functools.partial(prep_kernel, frames),
        out_shape=(
            jax.ShapeDtypeStruct((rows, patch_cols), BF),
            jax.ShapeDtypeStruct((span, span), BF),
            jax.ShapeDtypeStruct((span, span), BF),
            jax.ShapeDtypeStruct((2, channels, 128), F32),
            jax.ShapeDtypeStruct((4 * half, half), BF),
        ),
        scratch_shapes=[pltpu.VMEM((PACK, patch_cols), BF)],
        compiler_params=params(),
        cost_estimate=cost(1 << 27),
        name="prep",
    )(*in_hbm(conv_weight, conv_bias[None, :], mix_weight, mix_bias[None, :]))

    wt = jnp.swapaxes(feat_w, 1, 2).reshape(channels, neurons)
    mask_t = jnp.swapaxes(masks, 1, 2).reshape(pooled_n, neurons)
    rbias = readout_bias
    mask_far, wt_far = in_hbm(mask_t, wt)
    width = pooled_n + SEG
    early = neurons // 2
    vmem = pl.BlockSpec(memory_space=pltpu.VMEM)
    anywhere = pl.BlockSpec(memory_space=pl.ANY)
    smem = pl.BlockSpec(memory_space=pltpu.SMEM)
    pay, pay_send, target, act1, slope1, slope2, xcol, mask_near = pl.pallas_call(
        core_forward_kernel,
        out_shape=(
            jax.ShapeDtypeStruct((rows, width), BF),
            jax.ShapeDtypeStruct((rows, width), BF),
            jax.ShapeDtypeStruct((frames, neurons), F32),
            jax.ShapeDtypeStruct((rows, pix), BF),
            jax.ShapeDtypeStruct((rows, pix), BF),
            jax.ShapeDtypeStruct((rows, pix), BF),
            jax.ShapeDtypeStruct((patch_cols, pix), BF),
            jax.ShapeDtypeStruct((pooled_n, early), BF),
        ),
        in_specs=[vmem] * 5 + [anywhere],
        out_specs=(vmem, anywhere) + (vmem,) * 6,
        scratch_shapes=[pltpu.VMEM((rows, CHUNK), F32)] * 4
        + [pltpu.VMEM((rows, pix), BF), pltpu.SemaphoreType.DMA((early // 512 + width // half,))],
        compiler_params=params(),
        cost_estimate=cost(2 * rows * pix * patch_cols, 8 * rows * pix),
        name="core_forward",
    )(recv, wbig, blocks, bias, pool, mask_far)

    (pay_send,) = in_hbm(pay_send)
    near = {0: pay_send}
    for mask in range(1, clip_total):
        if mask % 2 == 0 or mask == 1:
            near[mask] = lax.ppermute(pay_send, "clip", xor_pairs(clip_total, mask))

    big = min(512, neurons)
    work = 2 * rows * neurons * pooled_n
    pooled_grad, loss = pl.pallas_call(
        functools.partial(readout_kernel, scale),
        in_specs=[smem] + [vmem] * 3 + [anywhere] + [vmem] * 2,
        out_shape=(jax.ShapeDtypeStruct((rows, pooled_n), BF), jax.ShapeDtypeStruct((8, 128), F32)),
        scratch_shapes=[pltpu.VMEM((pooled_n, neurons - early), BF)]
        + [pltpu.VMEM((rows, big), F32)] * 2
        + [
            pltpu.VMEM((rows, neurons), BF),
            pltpu.VMEM((pooled_n, rows), F32),
            pltpu.SemaphoreType.DMA(((neurons - early) // big,)),
        ],
        compiler_params=params(),
        cost_estimate=cost(2 * work, 2 * neurons * pooled_n),
        name="readout",
    )(counts, target, pay, mask_near, mask_far, wt, rbias)

    assert 2 * channels % total == 0
    pieces = (total, 2 * channels // total, 128)
    core = pl.pallas_call(
        functools.partial(core_backward_kernel, channels),
        out_shape=jax.ShapeDtypeStruct(pieces, F32),
        scratch_shapes=[pltpu.VMEM((rows, CHUNK), F32)] * 4
        + [pltpu.VMEM((rows, pix), BF)] * 2
        + [pltpu.VMEM((PACK, patch_cols), BF)],
        compiler_params=params(),
        cost_estimate=cost(2 * work, 8 * rows * pix),
        name="core_backward",
    )(pooled_grad, loss, act1, slope1, slope2, xcol, blocks_t)

    axes = ("clip", "sess")
    parts = lax.all_to_all(core, axes, split_axis=0, concat_axis=0, tiled=True)

    def owned_rows(clips, held, block):
        last = len(held) > 0
        return pl.pallas_call(
            functools.partial(owned_rows_kernel, scale, len(clips), own, block, len(held)),
            in_specs=[smem, smem] + [anywhere] * (len(clips) + 2) + [vmem] * (1 + len(held)),
            out_specs=[anywhere, vmem, vmem] if last else [vmem],
            out_shape=[
                jax.ShapeDtypeStruct((pooled_n, own), F32),
                jax.ShapeDtypeStruct((channels, own), F32),
                jax.ShapeDtypeStruct((1, own), F32),
            ]
            if last
            else [jax.ShapeDtypeStruct((pooled_n + channels + 8, own), F32)],
            scratch_shapes=[pltpu.VMEM((len(clips), rows, width), BF), pltpu.VMEM((channels, own), BF)]
            + [pltpu.VMEM((rows, block), F32)] * 2
            + [pltpu.VMEM((len(clips) * rows, block), BF)] * 2
            + [
                pltpu.VMEM((pooled_n, len(clips) * rows), BF),
                pltpu.VMEM((pooled_n, own), BF),
                pltpu.VMEM((pooled_n, own) if last else (8, 128), F32),
                pltpu.SemaphoreType.DMA((2 * (own // block) + len(clips) + 1,)),
            ],
            compiler_params=params(rows),
            cost_estimate=cost(2 * work * len(clips) // clip_total, 4 * own * pooled_n),
            name="owned_rows",
        )(where, counts, *in_hbm(*clips), wt_far, mask_far, rbias, *held)

    far = [mask for mask in near if mask > 1]
    reached, _ = lax.optimization_barrier(([near[mask] for mask in far], core))
    others = [lax.ppermute(value, "clip", xor_pairs(clip_total, 1)) for value in reached]
    (partial,) = owned_rows([near[0], near[1]] + reached, (), block)
    parts, partial = lax.optimization_barrier((parts, partial))
    copies = pl.pallas_call(
        share_kernel,
        out_shape=jax.ShapeDtypeStruct(pieces, F32),
        compiler_params=params(),
        name="share",
    )(parts)
    summed = lax.all_to_all(copies, axes, split_axis=0, concat_axis=0, tiled=True)
    readout_grads = owned_rows(others, (partial,), max(128, block // 2))
    summed, readout_grads = lax.optimization_barrier((summed, readout_grads))
    mask_grad, feat_grad, grad_rbias = readout_grads
    grad_conv, grad_cb, grad_mix, grad_mb, loss = pl.pallas_call(
        unpack_kernel,
        out_shape=(
            jax.ShapeDtypeStruct((channels, taps), F32),
            jax.ShapeDtypeStruct((1, channels), F32),
            jax.ShapeDtypeStruct((channels, channels), F32),
            jax.ShapeDtypeStruct((1, channels), F32),
            jax.ShapeDtypeStruct((1, 1), F32),
        ),
        compiler_params=params(),
        name="unpack",
    )(summed)
    return (
        loss.reshape(()),
        grad_conv,
        grad_cb.reshape(channels),
        grad_mix,
        grad_mb.reshape(channels),
        jnp.swapaxes(mask_grad[None], 1, 2),
        jnp.swapaxes(feat_grad[None], 1, 2),
        grad_rbias,
    )


def solution(mesh):
    return jax.shard_map(
        per_device,
        mesh=mesh,
        in_specs=(
            P("clip", "sess", None),
            P("clip", "sess", None),
            P("clip"),
            P("sess"),
            P(),
            P(),
            P(),
            P(),
            P("sess", None, None),
            P("sess", None, None),
            P("sess", None),
        ),
        out_specs=(
            P(),
            P(),
            P(),
            P(),
            P(),
            P("sess", "clip", None),
            P("sess", "clip", None),
            P("sess", "clip"),
        ),
        check_vma=False,
    )
```

```python
import functools

import jax
import jax.numpy as jnp
from jax import lax
from jax.experimental import pallas as pl
from jax.experimental.pallas import tpu as pltpu
from jax.sharding import PartitionSpec as P

HH = 36
WW = 64
KS = 7
KT = 3
DX = 8
PACK = 256
SEG = 64
CHUNK = 4 * WW
BF = jnp.bfloat16
F32 = jnp.float32
NT = (((1,), (1,)), ((), ()))


def dot(a, b, dims=(((1,), (0,)), ((), ())), precision=None):
    return lax.dot_general(a, b, dims, precision=precision, preferred_element_type=F32)


def iota(shape, axis):
    return lax.broadcasted_iota(jnp.int32, shape, axis)


def bias_column(row):
    size = row.shape[1]
    return jnp.sum(jnp.where(iota((size, size), 0) == iota((size, size), 1), row, 0.0), axis=1, keepdims=True)


def select_kernel(assign, video, responses, out):
    owners, lines, width = out.shape
    clips, pix = video.shape
    neurons = responses.shape[1]
    pick = (iota((owners, clips), 0) == assign[...]).astype(BF)
    first = dot(pick, responses[...])
    second = dot(pick, video[...])
    rows = [first[:, p : p + width] for p in range(0, neurons, width)]
    for p in range(0, pix, width):
        piece = second[:, p : p + width]
        if piece.shape[1] < width:
            piece = jnp.concatenate([piece, jnp.zeros((owners, width - piece.shape[1]), F32)], axis=1)
        rows.append(piece)
    while len(rows) < lines:
        rows.append(jnp.zeros((owners, width), F32))
    out[...] = jnp.stack(rows, axis=1).astype(BF)


def fill_table(table, frames):
    t = iota(table.shape, 0)
    l = iota(table.shape, 1)
    dy = l // (DX * frames)
    dx = (l // frames) % DX
    place = dy * KS + dx
    hit = (t == place) | (t == place + KS * KS) | (t == place + 2 * KS * KS)
    last = (t == KT * KS * KS) & (l == KS * frames)
    table[...] = jnp.where(((dx < KS) & hit & (t < KT * KS * KS)) | last, 1.0, 0.0).astype(BF)


def pool_weights(shape, pixel_axis):
    pixel = iota(shape, pixel_axis)
    target = (pixel // (2 * WW)) * (WW // 2) + (pixel % WW) // 2
    return jnp.where(target == iota(shape, 1 - pixel_axis), 0.25, 0.0).astype(BF)


def prep_kernel(frames, weight, cbias, mix, mbias, wbig, blocks, blocks_t, bias, pool, table):
    channels, taps = weight.shape
    patch_cols = wbig.shape[1]
    group = blocks.shape[0] // channels
    fill_table(table, frames)
    pool[...] = pool_weights(pool.shape, 0)
    size = channels * group
    same = (iota((size, size), 0) // channels) == (iota((size, size), 1) // channels)
    square = mix[...].astype(F32)
    for ref, base in ((blocks, square), (blocks_t, square.T)):
        wide = jnp.concatenate([base] * group, axis=1)
        ref[...] = jnp.where(same, jnp.concatenate([wide] * group, axis=0), 0.0).astype(BF)
    bias[0] = jnp.broadcast_to(bias_column(cbias[...]), bias.shape[1:])
    bias[1] = jnp.broadcast_to(bias_column(mbias[...]), bias.shape[1:])
    tap = iota((channels, taps), 1)
    weights = weight[...].astype(F32)
    split = [
        jnp.where((tap >= dt * KS * KS) & (tap < (dt + 1) * KS * KS), weights, 0.0).astype(BF)
        for dt in range(KT)
    ]
    spread = dot(jnp.concatenate(split, axis=0), table[0:taps, :])
    source = iota((channels, patch_cols), 1) % frames
    for f in range(frames):
        total = jnp.zeros((channels, patch_cols), F32)
        for dt in range(KT):
            total = total + jnp.where(source == f + dt - 1, spread[dt * channels : (dt + 1) * channels], 0.0)
        wbig[f * channels : (f + 1) * channels, :] = total.astype(BF)


def core_forward_kernel(
    recv,
    wbig,
    blocks,
    bias,
    pool,
    mask_in,
    pay,
    target,
    act1,
    slope1,
    slope2,
    xcol,
    mask,
    pre0,
    pre1,
    mid0,
    mid1,
    feats,
    sems,
):
    copies = []
    for k, r in enumerate(range(0, mask.shape[0], SEG)):
        copies.append(pltpu.make_async_copy(mask_in.at[r : r + SEG, :], mask.at[r : r + SEG, :], sems.at[k]))
    frames, _, width = recv.shape
    rows, pix = act1.shape
    channels = bias.shape[1]
    neurons = target.shape[1]
    span = blocks.shape[0]
    packet = recv[...].astype(F32)
    lines = [packet[:, j, :] for j in range((neurons + pix + width - 1) // width)]
    held = neurons // width
    for j in range(held):
        target[:, j * width : (j + 1) * width] = lines[j]
    video = jnp.concatenate(lines[held:], axis=1)[:, 0:pix]
    lane = iota((frames, pix), 1)
    col = lane % WW
    row = lane // WW
    per_store = max(1, 16 // frames)
    for dx0 in range(0, DX, per_store):
        shifted = []
        for dx in range(dx0, dx0 + per_store):
            s = dx - KS // 2
            if dx == KS:
                shifted.append(None)
            elif s == 0:
                shifted.append(video)
            else:
                rolled = pltpu.roll(video, (-s) % pix, 1)
                shifted.append(jnp.where((col + s >= 0) & (col + s < WW), rolled, 0.0))
        for dy in range(KS):
            t = dy - KS // 2
            parts = []
            for item in shifted:
                if item is None:
                    parts.append(jnp.ones((frames, pix), F32))
                elif t == 0:
                    parts.append(item)
                else:
                    moved = pltpu.roll(item, (-t * WW) % pix, 1)
                    parts.append(jnp.where((row + t >= 0) & (row + t < HH), moved, 0.0))
            base = (dy * DX + dx0) * frames
            block = parts[0] if len(parts) == 1 else jnp.concatenate(parts, axis=0)
            xcol[base : base + per_store * frames, :] = block.astype(BF)
    half = 2 * WW
    pre = (pre0, pre1)
    mid = (mid0, mid1)
    count = pix // CHUNK
    wide = wbig[...]

    def activate(source, which, act, slope, at):
        add = jnp.concatenate([bias[which]] * (CHUNK // 128), axis=1)
        for r in range(0, rows, channels):
            x = source[r : r + channels, :] + add
            e = jnp.exp(jnp.minimum(x, 0.0))
            act[r : r + channels, at] = (jnp.maximum(x, 0.0) + (e - 1.0)).astype(BF)
            slope[r : r + channels, at] = e.astype(BF)

    for t in range(count + 2):
        if t < len(copies):
            copies[t].start()
        if t < count:
            pre[t % 2][...] = dot(wide, xcol[:, t * CHUNK : (t + 1) * CHUNK])
        if 1 <= t <= count:
            at = slice((t - 1) * CHUNK, t * CHUNK)
            activate(pre[(t - 1) % 2], 0, act1, slope1, at)
            for r in range(0, rows, span):
                mid[(t - 1) % 2][r : r + span, :] = dot(blocks[...], act1[r : r + span, at])
        if t >= 2:
            at = slice((t - 2) * CHUNK, (t - 1) * CHUNK)
            activate(mid[t % 2], 1, feats, slope2, at)
            if t % 2 == 1:
                first = (t - 3) * CHUNK
                pooled = dot(feats[:, first : first + 2 * CHUNK], pool[...])
                pay[:, first // 4 : first // 4 + half] = pooled.astype(BF)
    p = pix - CHUNK
    tail = dot(feats[:, p:pix], pool[0:CHUNK, :])
    pieces = []
    for t in range(neurons // half):
        at = t * half
        tile = lines[at // width][:, at % width : at % width + half]
        pieces += [pltpu.roll(tile, SEG, 1), tile]
    packed = jnp.concatenate(pieces, axis=0)
    pay[:, p // 4 : p // 4 + half] = jnp.where(iota((rows, half), 1) < SEG, tail, packed).astype(BF)
    for copy in copies:
        copy.wait()


def drive_terms(projected, target, w, rbias, alive, scale, channels):
    frames = target.shape[0]
    sums = [
        jnp.sum(projected[f * channels : (f + 1) * channels, :] * w, axis=0, keepdims=True)
        for f in range(frames)
    ]
    drive = jnp.concatenate(sums, axis=0) + rbias
    e = jnp.exp(-jnp.abs(drive))
    rate = jnp.maximum(drive, 0.0) + jnp.log(1.0 + e) + 0.1
    sig = jnp.where(drive >= 0, 1.0, e) / (1.0 + e)
    grad = jnp.where(alive, (1.0 - target / rate) * sig, 0.0) * scale
    return rate, grad


def readout_kernel(
    scale,
    where,
    count,
    target,
    pay,
    mask,
    wt,
    rbias,
    pooled_grad,
    loss,
    mask_own,
    wt_own,
    proj0,
    proj1,
    mixed,
    acc,
):
    pooled_n, neurons = mask.shape
    own = mask_own.shape[1]
    channels = wt.shape[0]
    frames = target.shape[0]
    proj = (proj0, proj1)
    block = proj0.shape[1]
    steps = neurons // block
    first = pl.multiple_of(where[0] * own, own)
    mask_own[...] = mask[:, pl.ds(first, own)]
    wt_own[...] = wt[:, pl.ds(first, own)]
    pooled = pay[:, 0:pooled_n]
    loss_sum = jnp.zeros((frames, block), F32)
    begun = False
    for t in range(steps + 2):
        if t < steps:
            proj[t % 2][...] = dot(pooled, mask[:, t * block : (t + 1) * block])
        if 1 <= t <= steps:
            at = slice((t - 1) * block, t * block)
            w = wt[:, at].astype(F32)
            goal = target[:, at]
            alive = ((t - 1) * block + iota((frames, block), 1)) < count[0]
            rate, grad = drive_terms(proj[(t - 1) % 2], goal, w, rbias[:, at], alive, scale, channels)
            loss_sum = loss_sum + jnp.where(alive, rate - goal * jnp.log(rate), 0.0)
            for f in range(frames):
                mixed[f * channels : (f + 1) * channels, at] = (grad[f : f + 1] * w).astype(BF)
        last = t - 2
        if last >= 0 and (last % 2 == 0 or last == steps - 1):
            low = (last - 1 if last > 0 and last % 2 == 0 else last) * block
            at = slice(low, (last + 1) * block)
            part = dot(mask[:, at], mixed[:, at], NT)
            acc[...] = acc[...] + part if begun else part
            begun = True
    pooled_grad[...] = acc[...].T.astype(BF)
    loss[...] = jnp.broadcast_to(jnp.sum(loss_sum, keepdims=True) * scale, loss.shape)


def core_backward_kernel(
    channels, pooled_grad, loss, act1, slope1, slope2, xcol, blocks_t, out, up0, up1, down0, down1, g2, g1, table
):
    rows, pix = act1.shape
    frames = rows // channels
    span = blocks_t.shape[0]
    group = span // channels
    patch_cols = xcol.shape[0]
    up = (up0, up1)
    down = (down0, down1)
    count = pix // CHUNK
    half = 2 * WW
    unpool = pool_weights((half, 4 * half), 1)
    fill_table(table, frames)
    bias_sum = jnp.zeros((channels, 128), F32)
    for t in range(count + 2):
        if t < count:
            first = (t // 2) * half
            wide = min(half, pooled_grad.shape[1] - first)
            side = (t % 2) * CHUNK
            up[t % 2][...] = dot(pooled_grad[:, first : first + wide], unpool[0:wide, side : side + CHUNK])
        if 1 <= t <= count:
            at = slice((t - 1) * CHUNK, t * CHUNK)
            for r in range(0, rows, channels):
                g = (up[(t - 1) % 2][r : r + channels, :] * slope2[r : r + channels, at].astype(F32)).astype(BF)
                g2[r : r + channels, at] = g
                g = g.astype(F32)
                for c in range(0, CHUNK, 128):
                    bias_sum = bias_sum + g[:, c : c + 128]
            for r in range(0, rows, span):
                down[(t - 1) % 2][r : r + span, :] = dot(blocks_t[...], g2[r : r + span, at])
        if t >= 2:
            at = slice((t - 2) * CHUNK, (t - 1) * CHUNK)
            for r in range(0, rows, channels):
                g = down[t % 2][r : r + channels, :] * slope1[r : r + channels, at].astype(F32)
                g1[r : r + channels, at] = g.astype(BF)
    mix_bias_grad = jnp.sum(bias_sum, axis=1, keepdims=True)
    mix_grad = jnp.zeros((channels, span), F32)
    same = (iota((span, span), 0) // channels) == (iota((span, span), 1) // channels)
    for r in range(0, rows, span):
        full = jnp.where(same, dot(g2[r : r + span, :], act1[r : r + span, :], NT), 0.0)
        for a in range(group):
            mix_grad = mix_grad + full[a * channels : (a + 1) * channels]
    fold = 2 * channels
    folded = mix_grad[:, 0:fold]
    for k in range(fold, span, fold):
        folded = folded + mix_grad[:, k : k + fold]
    folded = folded + pltpu.roll(folded, channels, 1)
    full = dot(g1[...], xcol[...], NT)
    source = iota((channels, patch_cols), 1) % frames
    parts = [jnp.zeros((channels, patch_cols), F32) for _ in range(KT + 1)]
    for f in range(frames):
        piece = full[f * channels : (f + 1) * channels]
        for dt in range(KT):
            parts[dt] = parts[dt] + jnp.where(source == f + dt - 1, piece, 0.0)
        parts[KT] = parts[KT] + piece
    left = jnp.concatenate(parts, axis=0)
    taps = jnp.zeros((left.shape[0], PACK), F32)
    for _ in range(3):
        term = left.astype(BF)
        left = left - term.astype(F32)
        taps = taps + dot(term, table[...], NT)
    lane = iota((channels, PACK), 1)
    conv = jnp.zeros((channels, PACK), F32)
    for dt in range(KT + 1):
        inside = (lane >= dt * KS * KS) & (lane < (dt + 1) * KS * KS)
        conv = conv + jnp.where(inside, taps[dt * channels : (dt + 1) * channels], 0.0)
    used = KT * KS * KS + 1
    low = lane[:, 0:128]
    upper = jnp.where(low < used - 128, conv[:, 128:256], 0.0)
    upper = jnp.where(low == used - 128, mix_bias_grad, upper)
    upper = jnp.where((low == used - 127) & (iota((channels, 128), 0) == 0), loss[0:1, 0:1], upper)
    upper = jnp.where(low >= channels, folded, upper)
    out[0:channels, :] = conv[:, 0:128]
    out[channels:, :] = upper


def pair_sum(values):
    while len(values) > 1:
        values = [values[k] + values[k + 1] for k in range(0, len(values), 2)]
    return values[0]


def add_kernel(*refs):
    refs[-1][...] = pair_sum([ref[...] for ref in refs[:-1]])


def unpack_kernel(*refs):
    conv, conv_bias, mix, mix_bias, loss = refs[-5:]
    channels, taps = conv.shape
    both = pair_sum([ref[...] for ref in refs[:-5]])
    low = both[0:channels]
    high = both[channels:]
    rest = taps - 128
    conv[...] = jnp.concatenate([low, high], axis=1)[:, 0:taps]
    mix[...] = pltpu.roll(high, 128 - channels, 1)[:, 0:channels]
    same = iota((channels, channels), 0) == iota((channels, channels), 1)
    conv_bias[...] = jnp.sum(jnp.where(same, high[:, rest : rest + 1], 0.0), axis=0, keepdims=True)
    mix_bias[...] = jnp.sum(jnp.where(same, high[:, rest + 1 : rest + 2], 0.0), axis=0, keepdims=True)
    loss[...] = high[0:1, rest + 2 : rest + 3]


def owned_rows_kernel(scale, clips, own, block, held, last, where, count, *refs):
    pays = refs[:clips]
    wt, rbias, mask = refs[clips : clips + 3]
    before = refs[clips + 3 : clips + 3 + held]
    outs = refs[clips + 3 + held : -7]
    proj0, proj1, mixed0, mixed1, turned, stage, sems = refs[-7:]
    proj = (proj0, proj1)
    mixed = (mixed0, mixed1)
    pooled_n = mask.shape[0]
    channels = wt.shape[0]
    low_rows = pooled_n + channels
    rows = pays[0].shape[0]
    frames = rows // channels
    steps = own // block
    first = pl.multiple_of(where[0] * own, own)
    segs = block // SEG
    low = iota((frames, 128), 1) < SEG
    items = [(k, c) for k in range(steps) for c in range(clips)]
    feats = [jnp.zeros((channels, block), F32) for _ in range(steps)]
    biases = [jnp.zeros((frames, block), F32) for _ in range(steps)]
    stores = []
    for t in range(len(items) + 2):
        if t < len(items):
            k, c = items[t]
            if k == 0:
                turned[:, c * rows : (c + 1) * rows] = pays[c][:, 0:pooled_n].T
            proj[t % 2][...] = dot(pays[c][:, 0:pooled_n], mask[:, k * block : (k + 1) * block])
        if 1 <= t <= len(items):
            k, c = items[t - 1]
            start = pl.multiple_of(first + k * block, block)
            base = pl.multiple_of(start // SEG * frames, segs * frames)
            packed = pays[c][pl.ds(base, segs * frames), pooled_n - SEG : pooled_n + SEG].astype(F32)
            tiles = []
            for j in range(0, segs, 2):
                even = packed[j * frames : (j + 1) * frames]
                odd = packed[(j + 1) * frames : (j + 2) * frames]
                tiles.append(jnp.where(low, pltpu.roll(even, SEG, 1), odd))
            target = jnp.concatenate(tiles, axis=1)
            w = wt[:, k * block : (k + 1) * block].astype(F32)
            alive = (start + iota((frames, block), 1)) < count[0]
            now = proj[(t - 1) % 2]
            _, grad = drive_terms(now, target, w, rbias[:, pl.ds(start, block)], alive, scale, channels)
            for f in range(frames):
                feats[k] = feats[k] + grad[f : f + 1] * now[f * channels : (f + 1) * channels, :]
                at = c * rows + f * channels
                mixed[k % 2][at : at + channels, :] = (grad[f : f + 1] * w).astype(BF)
            biases[k] = biases[k] + grad
        if t >= 2 and items[t - 2][1] == clips - 1:
            k = items[t - 2][0]
            at = slice(k * block, (k + 1) * block)
            total = dot(turned[...], mixed[k % 2][...])
            feat = feats[k]
            bias = jnp.sum(biases[k], axis=0, keepdims=True)
            if held:
                total = total + before[0][0:pooled_n, at]
                feat = feat + before[0][pooled_n:low_rows, at]
                bias = bias + before[0][low_rows : low_rows + 1, at]
            if last:
                stage[:, at] = total
                outs[1][:, at] = feat
                outs[2][:, at] = bias
                stores.append(pltpu.make_async_copy(stage.at[:, at], outs[0].at[:, at], sems.at[k]))
                stores[-1].start()
            else:
                outs[0][0:pooled_n, at] = total
                outs[0][pooled_n:low_rows, at] = feat
                outs[0][low_rows:, at] = jnp.broadcast_to(bias, (8, block))
    for store in stores:
        store.wait()


def params(rows=512):
    return pltpu.CompilerParams(vmem_limit_bytes=min(56, 20 * max(1, rows // 512)) << 20)


def cost(flops, moved=1 << 20):
    return pl.CostEstimate(flops=int(flops), transcendentals=0, bytes_accessed=int(moved))


def in_hbm(*arrays):
    return [pltpu.with_memory_space_constraint(a, pltpu.HBM) for a in arrays]


def rounds_of(size):
    assert size & (size - 1) == 0
    bits = [1 << k for k in range(size.bit_length() - 1)]
    groups = [bits[:1]] if len(bits) % 2 else []
    bits = bits[len(bits) % 2 :]
    groups += [[low, low * 2, low * 3] for low in bits[::2]]
    return groups


def xor_pairs(size, mask):
    return [(i, i ^ mask) for i in range(size)]


def per_device(
    video, responses, assignment, counts, conv_weight, conv_bias, mix_weight, mix_bias, masks, feat_w, readout_bias
):
    sess_total = lax.axis_size("sess")
    clip_total = lax.axis_size("clip")
    clip_block, frame_block, pix = video.shape
    neurons = responses.shape[2]
    pooled_n = masks.shape[2]
    channels, taps = conv_weight.shape
    frames = frame_block * sess_total
    rows = frames * channels
    own = neurons // clip_total
    block = min(512, own)
    assert clip_block == sess_total and frame_block == 1 and masks.shape[0] == 1
    assert neurons == channels * SEG and pooled_n % 128 == SEG and pix == HH * WW
    scale = 1.0 / (clip_block * clip_total * frames)

    group = max(1, 256 // channels)
    lines = 16
    packet = 512
    assert neurons + pix <= lines * packet
    send = pl.pallas_call(
        select_kernel,
        out_shape=jax.ShapeDtypeStruct((sess_total, lines, packet), BF),
        compiler_params=params(),
        name="select",
    )(*in_hbm(assignment[None, :], video.reshape(clip_block, pix), responses.reshape(clip_block, neurons)))
    where = lax.axis_index("clip").astype(jnp.int32)[None]
    send, where = lax.optimization_barrier((send, where))
    recv = lax.all_to_all(send, "sess", split_axis=0, concat_axis=0, tiled=True)

    patch_cols = KS * DX * frames
    span = channels * group
    half = 2 * WW
    wbig, blocks, blocks_t, bias, pool = pl.pallas_call(
        functools.partial(prep_kernel, frames),
        out_shape=(
            jax.ShapeDtypeStruct((rows, patch_cols), BF),
            jax.ShapeDtypeStruct((span, span), BF),
            jax.ShapeDtypeStruct((span, span), BF),
            jax.ShapeDtypeStruct((2, channels, 128), F32),
            jax.ShapeDtypeStruct((4 * half, half), BF),
        ),
        scratch_shapes=[pltpu.VMEM((PACK, patch_cols), BF)],
        compiler_params=params(),
        cost_estimate=cost(1 << 27),
        name="prep",
    )(*in_hbm(conv_weight, conv_bias[None, :], mix_weight, mix_bias[None, :]))

    wt = jnp.swapaxes(feat_w, 1, 2).reshape(channels, neurons)
    mask_t = jnp.swapaxes(masks, 1, 2).reshape(pooled_n, neurons)
    rbias = readout_bias
    (mask_far,) = in_hbm(mask_t)
    width = pooled_n + SEG
    vmem = pl.BlockSpec(memory_space=pltpu.VMEM)
    anywhere = pl.BlockSpec(memory_space=pl.ANY)
    smem = pl.BlockSpec(memory_space=pltpu.SMEM)
    pay, target, act1, slope1, slope2, xcol, mask_near = pl.pallas_call(
        core_forward_kernel,
        out_shape=(
            jax.ShapeDtypeStruct((rows, width), BF),
            jax.ShapeDtypeStruct((frames, neurons), F32),
            jax.ShapeDtypeStruct((rows, pix), BF),
            jax.ShapeDtypeStruct((rows, pix), BF),
            jax.ShapeDtypeStruct((rows, pix), BF),
            jax.ShapeDtypeStruct((patch_cols, pix), BF),
            jax.ShapeDtypeStruct((pooled_n, neurons), BF),
        ),
        in_specs=[vmem] * 5 + [anywhere],
        scratch_shapes=[pltpu.VMEM((rows, CHUNK), F32)] * 4
        + [pltpu.VMEM((rows, pix), BF), pltpu.SemaphoreType.DMA((pooled_n // SEG,))],
        compiler_params=params(),
        cost_estimate=cost(2 * rows * pix * patch_cols, 8 * rows * pix),
        name="core_forward",
    )(recv, wbig, blocks, bias, pool, mask_far)

    near = {0: pay}
    for mask in range(1, clip_total):
        if mask % 2 == 0 or mask == 1:
            near[mask] = lax.ppermute(pay, "clip", xor_pairs(clip_total, mask))

    big = min(512, neurons)
    work = 2 * rows * neurons * pooled_n
    pooled_grad, loss, mask_own, wt_own = pl.pallas_call(
        functools.partial(readout_kernel, scale),
        in_specs=[smem, smem] + [vmem] * 5,
        out_shape=(
            jax.ShapeDtypeStruct((rows, pooled_n), BF),
            jax.ShapeDtypeStruct((8, 128), F32),
            jax.ShapeDtypeStruct((pooled_n, own), BF),
            jax.ShapeDtypeStruct((channels, own), BF),
        ),
        scratch_shapes=[pltpu.VMEM((rows, big), F32)] * 2
        + [pltpu.VMEM((rows, neurons), BF), pltpu.VMEM((pooled_n, rows), F32)],
        compiler_params=params(),
        cost_estimate=cost(2 * work, 2 * neurons * pooled_n),
        name="readout",
    )(where, counts, target, pay, mask_near, wt, rbias)

    core = pl.pallas_call(
        functools.partial(core_backward_kernel, channels),
        out_shape=jax.ShapeDtypeStruct((2 * channels, 128), F32),
        scratch_shapes=[pltpu.VMEM((rows, CHUNK), F32)] * 4
        + [pltpu.VMEM((rows, pix), BF)] * 2
        + [pltpu.VMEM((PACK, patch_cols), BF)],
        compiler_params=params(),
        cost_estimate=cost(2 * work, 8 * rows * pix),
        name="core_backward",
    )(pooled_grad, loss, act1, slope1, slope2, xcol, blocks_t)

    def owned_rows(clips, held, last):
        return pl.pallas_call(
            functools.partial(owned_rows_kernel, scale, len(clips), own, block, len(held), last),
            in_specs=[smem, smem] + [vmem] * (len(clips) + 3 + len(held)),
            out_specs=[anywhere, vmem, vmem] if last else [vmem],
            out_shape=[
                jax.ShapeDtypeStruct((pooled_n, own), F32),
                jax.ShapeDtypeStruct((channels, own), F32),
                jax.ShapeDtypeStruct((1, own), F32),
            ]
            if last
            else [jax.ShapeDtypeStruct((pooled_n + channels + 8, own), F32)],
            scratch_shapes=[pltpu.VMEM((rows, block), F32)] * 2
            + [pltpu.VMEM((len(clips) * rows, block), BF)] * 2
            + [
                pltpu.VMEM((pooled_n, len(clips) * rows), BF),
                pltpu.VMEM((pooled_n, own) if last else (8, 128), F32),
                pltpu.SemaphoreType.DMA((own // block,)),
            ],
            compiler_params=params(rows),
            cost_estimate=cost(2 * work * len(clips) // clip_total, 4 * own * pooled_n),
            name="owned_rows",
        )(where, counts, *clips, wt_own, rbias, mask_own, *held)

    far = [mask for mask in near if mask > 1]
    reached, _ = lax.optimization_barrier(([near[mask] for mask in far], core))
    others = [lax.ppermute(value, "clip", xor_pairs(clip_total, 1)) for value in reached]
    work_of = [[near[0], near[1]], reached, others]
    rounds = [("clip", masks) for masks in rounds_of(clip_total)] + [("sess", masks) for masks in rounds_of(sess_total)]
    held = ()
    for step, (axis, masks) in enumerate(rounds):
        got = [core] + [lax.ppermute(core, axis, xor_pairs(lax.axis_size(axis), mask)) for mask in masks]
        if step < len(work_of):
            held = owned_rows(work_of[step], held, step == len(work_of) - 1)
            got, held = lax.optimization_barrier((got, held))
        if step < len(rounds) - 1:
            core = pl.pallas_call(
                add_kernel,
                out_shape=jax.ShapeDtypeStruct(core.shape, F32),
                compiler_params=params(),
                name="add",
            )(*got)
            core, held = lax.optimization_barrier((core, held))
    mask_grad, feat_grad, grad_rbias = held
    grad_conv, grad_cb, grad_mix, grad_mb, loss = pl.pallas_call(
        unpack_kernel,
        out_shape=(
            jax.ShapeDtypeStruct((channels, taps), F32),
            jax.ShapeDtypeStruct((1, channels), F32),
            jax.ShapeDtypeStruct((channels, channels), F32),
            jax.ShapeDtypeStruct((1, channels), F32),
            jax.ShapeDtypeStruct((1, 1), F32),
        ),
        compiler_params=params(),
        name="unpack",
    )(*got)
    return (
        loss.reshape(()),
        grad_conv,
        grad_cb.reshape(channels),
        grad_mix,
        grad_mb.reshape(channels),
        jnp.swapaxes(mask_grad[None], 1, 2),
        jnp.swapaxes(feat_grad[None], 1, 2),
        grad_rbias,
    )


def solution(mesh):
    return jax.shard_map(
        per_device,
        mesh=mesh,
        in_specs=(
            P("clip", "sess", None),
            P("clip", "sess", None),
            P("clip"),
            P("sess"),
            P(),
            P(),
            P(),
            P(),
            P("sess", None, None),
            P("sess", None, None),
            P("sess", None),
        ),
        out_specs=(
            P(),
            P(),
            P(),
            P(),
            P(),
            P("sess", "clip", None),
            P("sess", "clip", None),
            P("sess", "clip"),
        ),
        check_vma=False,
    )
```

```python
import functools

import jax
import jax.numpy as jnp
from jax import lax
from jax.experimental import pallas as pl
from jax.experimental.pallas import tpu as pltpu
from jax.sharding import PartitionSpec as P

HH = 36
WW = 64
KS = 7
KT = 3
DX = 8
PACK = 256
SEG = 64
CHUNK = 4 * WW
BF = jnp.bfloat16
F32 = jnp.float32
NT = (((1,), (1,)), ((), ()))


def dot(a, b, dims=(((1,), (0,)), ((), ())), precision=None):
    return lax.dot_general(a, b, dims, precision=precision, preferred_element_type=F32)


def iota(shape, axis):
    return lax.broadcasted_iota(jnp.int32, shape, axis)


def bias_column(row):
    size = row.shape[1]
    return jnp.sum(jnp.where(iota((size, size), 0) == iota((size, size), 1), row, 0.0), axis=1, keepdims=True)


def select_kernel(assign, video, responses, out):
    owners, lines, width = out.shape
    clips, pix = video.shape
    neurons = responses.shape[1]
    pick = (iota((owners, clips), 0) == assign[...]).astype(BF)
    first = dot(pick, responses[...])
    second = dot(pick, video[...])
    rows = [first[:, p : p + width] for p in range(0, neurons, width)]
    for p in range(0, pix, width):
        piece = second[:, p : p + width]
        if piece.shape[1] < width:
            piece = jnp.concatenate([piece, jnp.zeros((owners, width - piece.shape[1]), F32)], axis=1)
        rows.append(piece)
    while len(rows) < lines:
        rows.append(jnp.zeros((owners, width), F32))
    out[...] = jnp.stack(rows, axis=1).astype(BF)


def fill_table(table, frames):
    t = iota(table.shape, 0)
    l = iota(table.shape, 1)
    dy = l // (DX * frames)
    dx = (l // frames) % DX
    place = dy * KS + dx
    hit = (t == place) | (t == place + KS * KS) | (t == place + 2 * KS * KS)
    last = (t == KT * KS * KS) & (l == KS * frames)
    table[...] = jnp.where(((dx < KS) & hit & (t < KT * KS * KS)) | last, 1.0, 0.0).astype(BF)


def pool_weights(shape, pixel_axis):
    pixel = iota(shape, pixel_axis)
    target = (pixel // (2 * WW)) * (WW // 2) + (pixel % WW) // 2
    return jnp.where(target == iota(shape, 1 - pixel_axis), 0.25, 0.0).astype(BF)


def fetch_rows(source, first, target, sems):
    copies = []
    for k, r in enumerate(range(0, target.shape[0], SEG)):
        part = source.at[r : r + SEG, first : first + target.shape[1]]
        copies.append(pltpu.make_async_copy(part, target.at[r : r + SEG, :], sems.at[k]))
        copies[k].start()
    return copies


def prep_kernel(frames, weight, cbias, mix, mbias, mask_in, wbig, blocks, blocks_t, bias, pool, mask, table, sems):
    copies = fetch_rows(mask_in, 0, mask, sems)
    channels, taps = weight.shape
    patch_cols = wbig.shape[1]
    group = blocks.shape[0] // channels
    fill_table(table, frames)
    pool[...] = pool_weights(pool.shape, 0)
    size = channels * group
    same = (iota((size, size), 0) // channels) == (iota((size, size), 1) // channels)
    square = mix[...].astype(F32)
    for ref, base in ((blocks, square), (blocks_t, square.T)):
        wide = jnp.concatenate([base] * group, axis=1)
        ref[...] = jnp.where(same, jnp.concatenate([wide] * group, axis=0), 0.0).astype(BF)
    bias[0] = jnp.broadcast_to(bias_column(cbias[...]), bias.shape[1:])
    bias[1] = jnp.broadcast_to(bias_column(mbias[...]), bias.shape[1:])
    tap = iota((channels, taps), 1)
    weights = weight[...].astype(F32)
    split = [
        jnp.where((tap >= dt * KS * KS) & (tap < (dt + 1) * KS * KS), weights, 0.0).astype(BF)
        for dt in range(KT)
    ]
    spread = dot(jnp.concatenate(split, axis=0), table[0:taps, :])
    source = iota((channels, patch_cols), 1) % frames
    for f in range(frames):
        total = jnp.zeros((channels, patch_cols), F32)
        for dt in range(KT):
            total = total + jnp.where(source == f + dt - 1, spread[dt * channels : (dt + 1) * channels], 0.0)
        wbig[f * channels : (f + 1) * channels, :] = total.astype(BF)
    for copy in copies:
        copy.wait()


def core_forward_kernel(
    recv,
    wbig,
    blocks,
    bias,
    pool,
    mask_in,
    pay,
    target,
    act1,
    slope1,
    slope2,
    xcol,
    mask,
    pre0,
    pre1,
    mid0,
    mid1,
    feats,
    sems,
):
    copies = fetch_rows(mask_in, mask_in.shape[1] - mask.shape[1], mask, sems)
    frames, _, width = recv.shape
    rows, pix = act1.shape
    channels = bias.shape[1]
    neurons = target.shape[1]
    span = blocks.shape[0]
    packet = recv[...].astype(F32)
    lines = [packet[:, j, :] for j in range((neurons + pix + width - 1) // width)]
    held = neurons // width
    for j in range(held):
        target[:, j * width : (j + 1) * width] = lines[j]
    video = jnp.concatenate(lines[held:], axis=1)[:, 0:pix]
    lane = iota((frames, pix), 1)
    col = lane % WW
    row = lane // WW
    per_store = max(1, 16 // frames)
    for dx0 in range(0, DX, per_store):
        shifted = []
        for dx in range(dx0, dx0 + per_store):
            s = dx - KS // 2
            if dx == KS:
                shifted.append(None)
            elif s == 0:
                shifted.append(video)
            else:
                rolled = pltpu.roll(video, (-s) % pix, 1)
                shifted.append(jnp.where((col + s >= 0) & (col + s < WW), rolled, 0.0))
        for dy in range(KS):
            t = dy - KS // 2
            parts = []
            for item in shifted:
                if item is None:
                    parts.append(jnp.ones((frames, pix), F32))
                elif t == 0:
                    parts.append(item)
                else:
                    moved = pltpu.roll(item, (-t * WW) % pix, 1)
                    parts.append(jnp.where((row + t >= 0) & (row + t < HH), moved, 0.0))
            base = (dy * DX + dx0) * frames
            block = parts[0] if len(parts) == 1 else jnp.concatenate(parts, axis=0)
            xcol[base : base + per_store * frames, :] = block.astype(BF)
    half = 2 * WW
    pre = (pre0, pre1)
    mid = (mid0, mid1)
    count = pix // CHUNK
    wide = wbig[...]

    def activate(source, which, act, slope, at):
        add = jnp.concatenate([bias[which]] * (CHUNK // 128), axis=1)
        for r in range(0, rows, channels):
            x = source[r : r + channels, :] + add
            e = jnp.exp(jnp.minimum(x, 0.0))
            act[r : r + channels, at] = (jnp.maximum(x, 0.0) + (e - 1.0)).astype(BF)
            slope[r : r + channels, at] = e.astype(BF)

    for t in range(count + 2):
        if t < count:
            pre[t % 2][...] = dot(wide, xcol[:, t * CHUNK : (t + 1) * CHUNK])
        if 1 <= t <= count:
            at = slice((t - 1) * CHUNK, t * CHUNK)
            activate(pre[(t - 1) % 2], 0, act1, slope1, at)
            for r in range(0, rows, span):
                mid[(t - 1) % 2][r : r + span, :] = dot(blocks[...], act1[r : r + span, at])
        if t >= 2:
            at = slice((t - 2) * CHUNK, (t - 1) * CHUNK)
            activate(mid[t % 2], 1, feats, slope2, at)
            if t % 2 == 1:
                first = (t - 3) * CHUNK
                pooled = dot(feats[:, first : first + 2 * CHUNK], pool[...])
                pay[:, first // 4 : first // 4 + half] = pooled.astype(BF)
    p = pix - CHUNK
    tail = dot(feats[:, p:pix], pool[0:CHUNK, :])
    pieces = []
    for t in range(neurons // half):
        at = t * half
        tile = lines[at // width][:, at % width : at % width + half]
        pieces += [pltpu.roll(tile, SEG, 1), tile]
    packed = jnp.concatenate(pieces, axis=0)
    pay[:, p // 4 : p // 4 + half] = jnp.where(iota((rows, half), 1) < SEG, tail, packed).astype(BF)
    for copy in copies:
        copy.wait()


def drive_terms(projected, target, w, rbias, alive, scale, channels):
    frames = target.shape[0]
    sums = [
        jnp.sum(projected[f * channels : (f + 1) * channels, :] * w, axis=0, keepdims=True)
        for f in range(frames)
    ]
    drive = jnp.concatenate(sums, axis=0) + rbias
    e = jnp.exp(-jnp.abs(drive))
    rate = jnp.maximum(drive, 0.0) + jnp.log(1.0 + e) + 0.1
    sig = jnp.where(drive >= 0, 1.0, e) / (1.0 + e)
    grad = jnp.where(alive, (1.0 - target / rate) * sig, 0.0) * scale
    return rate, grad


def readout_kernel(
    scale,
    where,
    count,
    target,
    pay,
    mask_near,
    mask_late,
    wt,
    rbias,
    pooled_grad,
    loss,
    mask_own,
    wt_own,
    proj0,
    proj1,
    mixed,
    acc,
):
    pooled_n, early = mask_near.shape
    neurons = target.shape[1]
    own = mask_own.shape[1]
    channels = wt.shape[0]
    frames = target.shape[0]
    proj = (proj0, proj1)
    block = proj0.shape[1]
    steps = neurons // block
    first = pl.multiple_of(where[0] * own, own)

    @pl.when(first < early)
    def _():
        mask_own[...] = mask_near[:, pl.ds(pl.multiple_of(jnp.minimum(first, early - own), own), own)]

    @pl.when(first >= early)
    def _():
        mask_own[...] = mask_late[:, pl.ds(pl.multiple_of(jnp.maximum(first - early, 0), own), own)]

    def mask_part(low, high):
        return mask_near[:, low:high] if high <= early else mask_late[:, low - early : high - early]

    wt_own[...] = wt[:, pl.ds(first, own)]
    pooled = pay[:, 0:pooled_n]
    loss_sum = jnp.zeros((frames, block), F32)
    begun = False
    for t in range(steps + 2):
        if t < steps:
            proj[t % 2][...] = dot(pooled, mask_part(t * block, (t + 1) * block))
        if 1 <= t <= steps:
            at = slice((t - 1) * block, t * block)
            w = wt[:, at].astype(F32)
            goal = target[:, at]
            alive = ((t - 1) * block + iota((frames, block), 1)) < count[0]
            rate, grad = drive_terms(proj[(t - 1) % 2], goal, w, rbias[:, at], alive, scale, channels)
            loss_sum = loss_sum + jnp.where(alive, rate - goal * jnp.log(rate), 0.0)
            for f in range(frames):
                mixed[f * channels : (f + 1) * channels, at] = (grad[f : f + 1] * w).astype(BF)
        last = t - 2
        if last >= 0 and last % 2 == 1:
            low = (last - 1) * block
            at = slice(low, (last + 1) * block)
            part = dot(mask_part(low, at.stop), mixed[:, at], NT)
            acc[...] = acc[...] + part if begun else part
            begun = True
    pooled_grad[...] = acc[...].T.astype(BF)
    loss[...] = jnp.broadcast_to(jnp.sum(loss_sum, keepdims=True) * scale, loss.shape)


def core_backward_kernel(
    channels, pooled_grad, loss, act1, slope1, slope2, xcol, blocks_t, out, up0, up1, down0, down1, g2, g1, table
):
    rows, pix = act1.shape
    frames = rows // channels
    span = blocks_t.shape[0]
    group = span // channels
    patch_cols = xcol.shape[0]
    up = (up0, up1)
    down = (down0, down1)
    count = pix // CHUNK
    half = 2 * WW
    unpool = pool_weights((half, 4 * half), 1)
    fill_table(table, frames)
    bias_sum = jnp.zeros((channels, 128), F32)
    for t in range(count + 2):
        if t < count:
            first = (t // 2) * half
            wide = min(half, pooled_grad.shape[1] - first)
            side = (t % 2) * CHUNK
            up[t % 2][...] = dot(pooled_grad[:, first : first + wide], unpool[0:wide, side : side + CHUNK])
        if 1 <= t <= count:
            at = slice((t - 1) * CHUNK, t * CHUNK)
            for r in range(0, rows, channels):
                g = (up[(t - 1) % 2][r : r + channels, :] * slope2[r : r + channels, at].astype(F32)).astype(BF)
                g2[r : r + channels, at] = g
                g = g.astype(F32)
                for c in range(0, CHUNK, 128):
                    bias_sum = bias_sum + g[:, c : c + 128]
            for r in range(0, rows, span):
                down[(t - 1) % 2][r : r + span, :] = dot(blocks_t[...], g2[r : r + span, at])
        if t >= 2:
            at = slice((t - 2) * CHUNK, (t - 1) * CHUNK)
            for r in range(0, rows, channels):
                g = down[t % 2][r : r + channels, :] * slope1[r : r + channels, at].astype(F32)
                g1[r : r + channels, at] = g.astype(BF)
    mix_bias_grad = jnp.sum(bias_sum, axis=1, keepdims=True)
    mix_grad = jnp.zeros((channels, span), F32)
    same = (iota((span, span), 0) // channels) == (iota((span, span), 1) // channels)
    for r in range(0, rows, span):
        full = jnp.where(same, dot(g2[r : r + span, :], act1[r : r + span, :], NT), 0.0)
        for a in range(group):
            mix_grad = mix_grad + full[a * channels : (a + 1) * channels]
    fold = 2 * channels
    folded = mix_grad[:, 0:fold]
    for k in range(fold, span, fold):
        folded = folded + mix_grad[:, k : k + fold]
    folded = folded + pltpu.roll(folded, channels, 1)
    full = dot(g1[...], xcol[...], NT)
    source = iota((channels, patch_cols), 1) % frames
    parts = [jnp.zeros((channels, patch_cols), F32) for _ in range(KT + 1)]
    for f in range(frames):
        piece = full[f * channels : (f + 1) * channels]
        for dt in range(KT):
            parts[dt] = parts[dt] + jnp.where(source == f + dt - 1, piece, 0.0)
        parts[KT] = parts[KT] + piece
    left = jnp.concatenate(parts, axis=0)
    taps = jnp.zeros((left.shape[0], PACK), F32)
    for _ in range(3):
        term = left.astype(BF)
        left = left - term.astype(F32)
        taps = taps + dot(term, table[...], NT)
    lane = iota((channels, PACK), 1)
    conv = jnp.zeros((channels, PACK), F32)
    for dt in range(KT + 1):
        inside = (lane >= dt * KS * KS) & (lane < (dt + 1) * KS * KS)
        conv = conv + jnp.where(inside, taps[dt * channels : (dt + 1) * channels], 0.0)
    used = KT * KS * KS + 1
    low = lane[:, 0:128]
    upper = jnp.where(low < used - 128, conv[:, 128:256], 0.0)
    upper = jnp.where(low == used - 128, mix_bias_grad, upper)
    upper = jnp.where((low == used - 127) & (iota((channels, 128), 0) == 0), loss[0:1, 0:1], upper)
    upper = jnp.where(low >= channels, folded, upper)
    out[0:channels, :] = conv[:, 0:128]
    out[channels:, :] = upper


def pair_sum(values):
    while len(values) > 1:
        values = [values[k] + values[k + 1] for k in range(0, len(values), 2)]
    return values[0]


def add_kernel(*refs):
    refs[-1][...] = pair_sum([ref[...] for ref in refs[:-1]])


def unpack_kernel(*refs):
    conv, conv_bias, mix, mix_bias, loss = refs[-5:]
    channels, taps = conv.shape
    both = pair_sum([ref[...] for ref in refs[:-5]])
    low = both[0:channels]
    high = both[channels:]
    rest = taps - 128
    conv[...] = jnp.concatenate([low, high], axis=1)[:, 0:taps]
    mix[...] = pltpu.roll(high, 128 - channels, 1)[:, 0:channels]
    same = iota((channels, channels), 0) == iota((channels, channels), 1)
    conv_bias[...] = jnp.sum(jnp.where(same, high[:, rest : rest + 1], 0.0), axis=0, keepdims=True)
    mix_bias[...] = jnp.sum(jnp.where(same, high[:, rest + 1 : rest + 2], 0.0), axis=0, keepdims=True)
    loss[...] = high[0:1, rest + 2 : rest + 3]


def owned_rows_kernel(scale, clips, own, block, held, last, where, count, *refs):
    pays = refs[:clips]
    wt, rbias, mask = refs[clips : clips + 3]
    before = refs[clips + 3 : clips + 3 + held]
    outs = refs[clips + 3 + held : -7]
    proj0, proj1, mixed0, mixed1, turned, stage, sems = refs[-7:]
    proj = (proj0, proj1)
    mixed = (mixed0, mixed1)
    pooled_n = mask.shape[0]
    channels = wt.shape[0]
    low_rows = pooled_n + channels
    rows = pays[0].shape[0]
    frames = rows // channels
    steps = own // block
    first = pl.multiple_of(where[0] * own, own)
    segs = block // SEG
    low = iota((frames, 128), 1) < SEG
    items = [(k, c) for k in range(steps) for c in range(clips)]
    feats = [jnp.zeros((channels, block), F32) for _ in range(steps)]
    biases = [jnp.zeros((frames, block), F32) for _ in range(steps)]
    stores = []
    for t in range(len(items) + 2):
        if t < len(items):
            k, c = items[t]
            if k == 0:
                turned[:, c * rows : (c + 1) * rows] = pays[c][:, 0:pooled_n].T
            proj[t % 2][...] = dot(pays[c][:, 0:pooled_n], mask[:, k * block : (k + 1) * block])
        if 1 <= t <= len(items):
            k, c = items[t - 1]
            start = pl.multiple_of(first + k * block, block)
            base = pl.multiple_of(start // SEG * frames, segs * frames)
            packed = pays[c][pl.ds(base, segs * frames), pooled_n - SEG : pooled_n + SEG].astype(F32)
            tiles = []
            for j in range(0, segs, 2):
                even = packed[j * frames : (j + 1) * frames]
                odd = packed[(j + 1) * frames : (j + 2) * frames]
                tiles.append(jnp.where(low, pltpu.roll(even, SEG, 1), odd))
            target = jnp.concatenate(tiles, axis=1)
            w = wt[:, k * block : (k + 1) * block].astype(F32)
            alive = (start + iota((frames, block), 1)) < count[0]
            now = proj[(t - 1) % 2]
            _, grad = drive_terms(now, target, w, rbias[:, pl.ds(start, block)], alive, scale, channels)
            for f in range(frames):
                feats[k] = feats[k] + grad[f : f + 1] * now[f * channels : (f + 1) * channels, :]
                at = c * rows + f * channels
                mixed[k % 2][at : at + channels, :] = (grad[f : f + 1] * w).astype(BF)
            biases[k] = biases[k] + grad
        if t >= 2 and items[t - 2][1] == clips - 1:
            k = items[t - 2][0]
            at = slice(k * block, (k + 1) * block)
            total = dot(turned[...], mixed[k % 2][...])
            feat = feats[k]
            bias = jnp.sum(biases[k], axis=0, keepdims=True)
            if held:
                total = total + before[0][0:pooled_n, at]
                feat = feat + before[0][pooled_n:low_rows, at]
                bias = bias + before[0][low_rows : low_rows + 1, at]
            if last:
                stage[:, at] = total
                outs[1][:, at] = feat
                outs[2][:, at] = bias
                stores.append(pltpu.make_async_copy(stage.at[:, at], outs[0].at[:, at], sems.at[k]))
                stores[-1].start()
            else:
                outs[0][0:pooled_n, at] = total
                outs[0][pooled_n:low_rows, at] = feat
                outs[0][low_rows:, at] = jnp.broadcast_to(bias, (8, block))
    for store in stores:
        store.wait()


def params(rows=512):
    return pltpu.CompilerParams(vmem_limit_bytes=min(56, 20 * max(1, rows // 512)) << 20)


def cost(flops, moved=1 << 20):
    return pl.CostEstimate(flops=int(flops), transcendentals=0, bytes_accessed=int(moved))


def in_hbm(*arrays):
    return [pltpu.with_memory_space_constraint(a, pltpu.HBM) for a in arrays]


def rounds_of(size):
    assert size & (size - 1) == 0
    bits = [1 << k for k in range(size.bit_length() - 1)]
    groups = [bits[:1]] if len(bits) % 2 else []
    bits = bits[len(bits) % 2 :]
    groups += [[low, low * 2, low * 3] for low in bits[::2]]
    return groups


def xor_pairs(size, mask):
    return [(i, i ^ mask) for i in range(size)]


def per_device(
    video, responses, assignment, counts, conv_weight, conv_bias, mix_weight, mix_bias, masks, feat_w, readout_bias
):
    sess_total = lax.axis_size("sess")
    clip_total = lax.axis_size("clip")
    clip_block, frame_block, pix = video.shape
    neurons = responses.shape[2]
    pooled_n = masks.shape[2]
    channels, taps = conv_weight.shape
    frames = frame_block * sess_total
    rows = frames * channels
    own = neurons // clip_total
    block = min(512, own)
    assert clip_block == sess_total and frame_block == 1 and masks.shape[0] == 1
    assert neurons == channels * SEG and pooled_n % 128 == SEG and pix == HH * WW
    scale = 1.0 / (clip_block * clip_total * frames)

    group = max(1, 256 // channels)
    lines = 16
    packet = 512
    assert neurons + pix <= lines * packet
    send = pl.pallas_call(
        select_kernel,
        out_shape=jax.ShapeDtypeStruct((sess_total, lines, packet), BF),
        compiler_params=params(),
        name="select",
    )(*in_hbm(assignment[None, :], video.reshape(clip_block, pix), responses.reshape(clip_block, neurons)))
    where = lax.axis_index("clip").astype(jnp.int32)[None]
    send, where = lax.optimization_barrier((send, where))
    recv = lax.all_to_all(send, "sess", split_axis=0, concat_axis=0, tiled=True)

    wt = jnp.swapaxes(feat_w, 1, 2).reshape(channels, neurons)
    mask_t = jnp.swapaxes(masks, 1, 2).reshape(pooled_n, neurons)
    rbias = readout_bias
    (mask_far,) = in_hbm(mask_t)
    width = pooled_n + SEG
    vmem = pl.BlockSpec(memory_space=pltpu.VMEM)
    anywhere = pl.BlockSpec(memory_space=pl.ANY)
    smem = pl.BlockSpec(memory_space=pltpu.SMEM)
    early = neurons // 2
    patch_cols = KS * DX * frames
    span = channels * group
    half = 2 * WW
    wbig, blocks, blocks_t, bias, pool, mask_near = pl.pallas_call(
        functools.partial(prep_kernel, frames),
        out_shape=(
            jax.ShapeDtypeStruct((rows, patch_cols), BF),
            jax.ShapeDtypeStruct((span, span), BF),
            jax.ShapeDtypeStruct((span, span), BF),
            jax.ShapeDtypeStruct((2, channels, 128), F32),
            jax.ShapeDtypeStruct((4 * half, half), BF),
            jax.ShapeDtypeStruct((pooled_n, early), BF),
        ),
        in_specs=[vmem] * 4 + [anywhere],
        scratch_shapes=[pltpu.VMEM((PACK, patch_cols), BF), pltpu.SemaphoreType.DMA((pooled_n // SEG,))],
        compiler_params=params(),
        cost_estimate=cost(1 << 27),
        name="prep",
    )(*in_hbm(conv_weight, conv_bias[None, :], mix_weight, mix_bias[None, :]), mask_far)

    pay, target, act1, slope1, slope2, xcol, mask_late = pl.pallas_call(
        core_forward_kernel,
        out_shape=(
            jax.ShapeDtypeStruct((rows, width), BF),
            jax.ShapeDtypeStruct((frames, neurons), F32),
            jax.ShapeDtypeStruct((rows, pix), BF),
            jax.ShapeDtypeStruct((rows, pix), BF),
            jax.ShapeDtypeStruct((rows, pix), BF),
            jax.ShapeDtypeStruct((patch_cols, pix), BF),
            jax.ShapeDtypeStruct((pooled_n, neurons - early), BF),
        ),
        in_specs=[vmem] * 5 + [anywhere],
        scratch_shapes=[pltpu.VMEM((rows, CHUNK), F32)] * 4
        + [pltpu.VMEM((rows, pix), BF), pltpu.SemaphoreType.DMA((pooled_n // SEG,))],
        compiler_params=params(),
        cost_estimate=cost(2 * rows * pix * patch_cols, 8 * rows * pix),
        name="core_forward",
    )(recv, wbig, blocks, bias, pool, mask_far)

    near = {0: pay}
    for mask in range(1, clip_total):
        if mask % 2 == 0 or mask == 1:
            near[mask] = lax.ppermute(pay, "clip", xor_pairs(clip_total, mask))

    big = min(512, neurons)
    work = 2 * rows * neurons * pooled_n
    pooled_grad, loss, mask_own, wt_own = pl.pallas_call(
        functools.partial(readout_kernel, scale),
        in_specs=[smem, smem] + [vmem] * 6,
        out_shape=(
            jax.ShapeDtypeStruct((rows, pooled_n), BF),
            jax.ShapeDtypeStruct((8, 128), F32),
            jax.ShapeDtypeStruct((pooled_n, own), BF),
            jax.ShapeDtypeStruct((channels, own), BF),
        ),
        scratch_shapes=[pltpu.VMEM((rows, big), F32)] * 2
        + [pltpu.VMEM((rows, neurons), BF), pltpu.VMEM((pooled_n, rows), F32)],
        compiler_params=params(),
        cost_estimate=cost(2 * work, 2 * neurons * pooled_n),
        name="readout",
    )(where, counts, target, pay, mask_near, mask_late, wt, rbias)

    core = pl.pallas_call(
        functools.partial(core_backward_kernel, channels),
        out_shape=jax.ShapeDtypeStruct((2 * channels, 128), F32),
        scratch_shapes=[pltpu.VMEM((rows, CHUNK), F32)] * 4
        + [pltpu.VMEM((rows, pix), BF)] * 2
        + [pltpu.VMEM((PACK, patch_cols), BF)],
        compiler_params=params(),
        cost_estimate=cost(2 * work, 8 * rows * pix),
        name="core_backward",
    )(pooled_grad, loss, act1, slope1, slope2, xcol, blocks_t)

    def owned_rows(clips, held, last):
        return pl.pallas_call(
            functools.partial(owned_rows_kernel, scale, len(clips), own, block, len(held), last),
            in_specs=[smem, smem] + [vmem] * (len(clips) + 3 + len(held)),
            out_specs=[anywhere, vmem, vmem] if last else [vmem],
            out_shape=[
                jax.ShapeDtypeStruct((pooled_n, own), F32),
                jax.ShapeDtypeStruct((channels, own), F32),
                jax.ShapeDtypeStruct((1, own), F32),
            ]
            if last
            else [jax.ShapeDtypeStruct((pooled_n + channels + 8, own), F32)],
            scratch_shapes=[pltpu.VMEM((rows, block), F32)] * 2
            + [pltpu.VMEM((len(clips) * rows, block), BF)] * 2
            + [
                pltpu.VMEM((pooled_n, len(clips) * rows), BF),
                pltpu.VMEM((pooled_n, own) if last else (8, 128), F32),
                pltpu.SemaphoreType.DMA((own // block,)),
            ],
            compiler_params=params(rows),
            cost_estimate=cost(2 * work * len(clips) // clip_total, 4 * own * pooled_n),
            name="owned_rows",
        )(where, counts, *clips, wt_own, rbias, mask_own, *held)

    far = [mask for mask in near if mask > 1]
    reached, _ = lax.optimization_barrier(([near[mask] for mask in far], core))
    others = [lax.ppermute(value, "clip", xor_pairs(clip_total, 1)) for value in reached]
    work_of = [[near[0], near[1]], reached, others]
    rounds = [("clip", masks) for masks in rounds_of(clip_total)] + [("sess", masks) for masks in rounds_of(sess_total)]
    held = ()
    for step, (axis, masks) in enumerate(rounds):
        got = [core] + [lax.ppermute(core, axis, xor_pairs(lax.axis_size(axis), mask)) for mask in masks]
        if step < len(work_of):
            held = owned_rows(work_of[step], held, step == len(work_of) - 1)
            got, held = lax.optimization_barrier((got, held))
        if step < len(rounds) - 1:
            core = pl.pallas_call(
                add_kernel,
                out_shape=jax.ShapeDtypeStruct(core.shape, F32),
                compiler_params=params(),
                name="add",
            )(*got)
            core, held = lax.optimization_barrier((core, held))
    mask_grad, feat_grad, grad_rbias = held
    grad_conv, grad_cb, grad_mix, grad_mb, loss = pl.pallas_call(
        unpack_kernel,
        out_shape=(
            jax.ShapeDtypeStruct((channels, taps), F32),
            jax.ShapeDtypeStruct((1, channels), F32),
            jax.ShapeDtypeStruct((channels, channels), F32),
            jax.ShapeDtypeStruct((1, channels), F32),
            jax.ShapeDtypeStruct((1, 1), F32),
        ),
        compiler_params=params(),
        name="unpack",
    )(*got)
    return (
        loss.reshape(()),
        grad_conv,
        grad_cb.reshape(channels),
        grad_mix,
        grad_mb.reshape(channels),
        jnp.swapaxes(mask_grad[None], 1, 2),
        jnp.swapaxes(feat_grad[None], 1, 2),
        grad_rbias,
    )


def solution(mesh):
    return jax.shard_map(
        per_device,
        mesh=mesh,
        in_specs=(
            P("clip", "sess", None),
            P("clip", "sess", None),
            P("clip"),
            P("sess"),
            P(),
            P(),
            P(),
            P(),
            P("sess", None, None),
            P("sess", None, None),
            P("sess", None),
        ),
        out_specs=(
            P(),
            P(),
            P(),
            P(),
            P(),
            P("sess", "clip", None),
            P("sess", "clip", None),
            P("sess", "clip"),
        ),
        check_vma=False,
    )
```

```python
import functools

import jax
import jax.numpy as jnp
from jax import lax
from jax.experimental import pallas as pl
from jax.experimental.pallas import tpu as pltpu
from jax.sharding import PartitionSpec as P

HH = 36
WW = 64
KS = 7
KT = 3
DX = 8
PACK = 256
SEG = 64
CHUNK = 4 * WW
BF = jnp.bfloat16
F32 = jnp.float32
NT = (((1,), (1,)), ((), ()))


def dot(a, b, dims=(((1,), (0,)), ((), ())), precision=None):
    return lax.dot_general(a, b, dims, precision=precision, preferred_element_type=F32)


def iota(shape, axis):
    return lax.broadcasted_iota(jnp.int32, shape, axis)


def bias_column(row):
    size = row.shape[1]
    return jnp.sum(jnp.where(iota((size, size), 0) == iota((size, size), 1), row, 0.0), axis=1, keepdims=True)


def select_kernel(assign, video, responses, out):
    owners, lines, width = out.shape
    clips, pix = video.shape
    neurons = responses.shape[1]
    pick = (iota((owners, clips), 0) == assign[...]).astype(BF)
    first = dot(pick, responses[...])
    second = dot(pick, video[...])
    rows = [first[:, p : p + width] for p in range(0, neurons, width)]
    for p in range(0, pix, width):
        piece = second[:, p : p + width]
        if piece.shape[1] < width:
            piece = jnp.concatenate([piece, jnp.zeros((owners, width - piece.shape[1]), F32)], axis=1)
        rows.append(piece)
    while len(rows) < lines:
        rows.append(jnp.zeros((owners, width), F32))
    out[...] = jnp.stack(rows, axis=1).astype(BF)


def fill_table(table, frames):
    t = iota(table.shape, 0)
    l = iota(table.shape, 1)
    dy = l // (DX * frames)
    dx = (l // frames) % DX
    place = dy * KS + dx
    hit = (t == place) | (t == place + KS * KS) | (t == place + 2 * KS * KS)
    last = (t == KT * KS * KS) & (l == KS * frames)
    table[...] = jnp.where(((dx < KS) & hit & (t < KT * KS * KS)) | last, 1.0, 0.0).astype(BF)


def pool_weights(shape, pixel_axis):
    pixel = iota(shape, pixel_axis)
    target = (pixel // (2 * WW)) * (WW // 2) + (pixel % WW) // 2
    return jnp.where(target == iota(shape, 1 - pixel_axis), 0.25, 0.0).astype(BF)


def prep_kernel(frames, weight, cbias, mix, mbias, wbig, blocks, blocks_t, bias, pool, table):
    channels, taps = weight.shape
    patch_cols = wbig.shape[1]
    group = blocks.shape[0] // channels
    fill_table(table, frames)
    pool[...] = pool_weights(pool.shape, 0)
    size = channels * group
    same = (iota((size, size), 0) // channels) == (iota((size, size), 1) // channels)
    square = mix[...].astype(F32)
    for ref, base in ((blocks, square), (blocks_t, square.T)):
        wide = jnp.concatenate([base] * group, axis=1)
        ref[...] = jnp.where(same, jnp.concatenate([wide] * group, axis=0), 0.0).astype(BF)
    bias[0] = jnp.broadcast_to(bias_column(cbias[...]), bias.shape[1:])
    bias[1] = jnp.broadcast_to(bias_column(mbias[...]), bias.shape[1:])
    tap = iota((channels, taps), 1)
    weights = weight[...].astype(F32)
    split = [
        jnp.where((tap >= dt * KS * KS) & (tap < (dt + 1) * KS * KS), weights, 0.0).astype(BF)
        for dt in range(KT)
    ]
    spread = dot(jnp.concatenate(split, axis=0), table[0:taps, :])
    source = iota((channels, patch_cols), 1) % frames
    for f in range(frames):
        total = jnp.zeros((channels, patch_cols), F32)
        for dt in range(KT):
            total = total + jnp.where(source == f + dt - 1, spread[dt * channels : (dt + 1) * channels], 0.0)
        wbig[f * channels : (f + 1) * channels, :] = total.astype(BF)


def core_forward_kernel(
    recv,
    wbig,
    blocks,
    bias,
    pool,
    mask_in,
    pay,
    target,
    act1,
    slope1,
    slope2,
    xcol,
    mask,
    pre0,
    pre1,
    mid0,
    mid1,
    feats,
    sems,
):
    copy_count = mask.shape[0] // SEG

    def mask_copy(k):
        rows_at = pl.ds(pl.multiple_of(k * SEG, SEG), SEG)
        return pltpu.make_async_copy(mask_in.at[rows_at, :], mask.at[rows_at, :], sems.at[k])

    @pl.loop(0, copy_count)
    def _(k):
        mask_copy(k).start()

    frames, _, width = recv.shape
    rows, pix = act1.shape
    channels = bias.shape[1]
    neurons = target.shape[1]
    span = blocks.shape[0]
    packet = recv[...].astype(F32)
    lines = [packet[:, j, :] for j in range((neurons + pix + width - 1) // width)]
    held = neurons // width
    for j in range(held):
        target[:, j * width : (j + 1) * width] = lines[j]
    video = jnp.concatenate(lines[held:], axis=1)[:, 0:pix]
    lane = iota((frames, pix), 1)
    col = lane % WW
    row = lane // WW
    per_store = max(1, 16 // frames)
    for dx0 in range(0, DX, per_store):
        shifted = []
        for dx in range(dx0, dx0 + per_store):
            s = dx - KS // 2
            if dx == KS:
                shifted.append(None)
            elif s == 0:
                shifted.append(video)
            else:
                rolled = pltpu.roll(video, (-s) % pix, 1)
                shifted.append(jnp.where((col + s >= 0) & (col + s < WW), rolled, 0.0))
        for dy in range(KS):
            t = dy - KS // 2
            parts = []
            for item in shifted:
                if item is None:
                    parts.append(jnp.ones((frames, pix), F32))
                elif t == 0:
                    parts.append(item)
                else:
                    moved = pltpu.roll(item, (-t * WW) % pix, 1)
                    parts.append(jnp.where((row + t >= 0) & (row + t < HH), moved, 0.0))
            base = (dy * DX + dx0) * frames
            block = parts[0] if len(parts) == 1 else jnp.concatenate(parts, axis=0)
            xcol[base : base + per_store * frames, :] = block.astype(BF)
    half = 2 * WW
    pre = (pre0, pre1)
    mid = (mid0, mid1)
    count = pix // CHUNK
    wide = wbig[...]

    def activate(source, which, act, slope, at):
        add = jnp.concatenate([bias[which]] * (CHUNK // 128), axis=1)
        for r in range(0, rows, channels):
            x = source[r : r + channels, :] + add
            e = jnp.exp(jnp.minimum(x, 0.0))
            act[r : r + channels, at] = (jnp.maximum(x, 0.0) + (e - 1.0)).astype(BF)
            slope[r : r + channels, at] = e.astype(BF)

    for t in range(count + 2):
        if t < count:
            pre[t % 2][...] = dot(wide, xcol[:, t * CHUNK : (t + 1) * CHUNK])
        if 1 <= t <= count:
            at = slice((t - 1) * CHUNK, t * CHUNK)
            activate(pre[(t - 1) % 2], 0, act1, slope1, at)
            for r in range(0, rows, span):
                mid[(t - 1) % 2][r : r + span, :] = dot(blocks[...], act1[r : r + span, at])
        if t >= 2:
            at = slice((t - 2) * CHUNK, (t - 1) * CHUNK)
            activate(mid[t % 2], 1, feats, slope2, at)
            if t % 2 == 1:
                first = (t - 3) * CHUNK
                pooled = dot(feats[:, first : first + 2 * CHUNK], pool[...])
                pay[:, first // 4 : first // 4 + half] = pooled.astype(BF)
    p = pix - CHUNK
    tail = dot(feats[:, p:pix], pool[0:CHUNK, :])
    pieces = []
    for t in range(neurons // half):
        at = t * half
        tile = lines[at // width][:, at % width : at % width + half]
        pieces += [pltpu.roll(tile, SEG, 1), tile]
    packed = jnp.concatenate(pieces, axis=0)
    pay[:, p // 4 : p // 4 + half] = jnp.where(iota((rows, half), 1) < SEG, tail, packed).astype(BF)

    @pl.loop(0, copy_count)
    def _(k):
        mask_copy(k).wait()


def drive_terms(projected, target, w, rbias, alive, scale, channels):
    frames = target.shape[0]
    sums = [
        jnp.sum(projected[f * channels : (f + 1) * channels, :] * w, axis=0, keepdims=True)
        for f in range(frames)
    ]
    drive = jnp.concatenate(sums, axis=0) + rbias
    e = jnp.exp(-jnp.abs(drive))
    rate = jnp.maximum(drive, 0.0) + jnp.log(1.0 + e) + 0.1
    sig = jnp.where(drive >= 0, 1.0, e) / (1.0 + e)
    grad = jnp.where(alive, (1.0 - target / rate) * sig, 0.0) * scale
    return rate, grad


def readout_kernel(
    scale,
    where,
    count,
    target,
    pay,
    mask,
    wt,
    rbias,
    pooled_grad,
    loss,
    mask_own,
    wt_own,
    proj0,
    proj1,
    mixed,
    acc,
):
    pooled_n, neurons = mask.shape
    own = mask_own.shape[1]
    channels = wt.shape[0]
    frames = target.shape[0]
    proj = (proj0, proj1)
    block = proj0.shape[1]
    steps = neurons // block
    first = pl.multiple_of(where[0] * own, own)
    mask_own[...] = mask[:, pl.ds(first, own)]
    wt_own[...] = wt[:, pl.ds(first, own)]
    pooled = pay[:, 0:pooled_n]
    loss_sum = jnp.zeros((frames, block), F32)
    begun = False
    for t in range(steps + 2):
        if t < steps:
            proj[t % 2][...] = dot(pooled, mask[:, t * block : (t + 1) * block])
        if 1 <= t <= steps:
            at = slice((t - 1) * block, t * block)
            w = wt[:, at].astype(F32)
            goal = target[:, at]
            alive = ((t - 1) * block + iota((frames, block), 1)) < count[0]
            rate, grad = drive_terms(proj[(t - 1) % 2], goal, w, rbias[:, at], alive, scale, channels)
            loss_sum = loss_sum + jnp.where(alive, rate - goal * jnp.log(rate), 0.0)
            for f in range(frames):
                mixed[f * channels : (f + 1) * channels, at] = (grad[f : f + 1] * w).astype(BF)
        last = t - 2
        if last >= 0 and (last % 2 == 0 or last == steps - 1):
            low = (last - 1 if last > 0 and last % 2 == 0 else last) * block
            at = slice(low, (last + 1) * block)
            part = dot(mask[:, at], mixed[:, at], NT)
            acc[...] = acc[...] + part if begun else part
            begun = True
    pooled_grad[...] = acc[...].T.astype(BF)
    loss[...] = jnp.broadcast_to(jnp.sum(loss_sum, keepdims=True) * scale, loss.shape)


def core_backward_kernel(
    channels, pooled_grad, loss, act1, slope1, slope2, xcol, blocks_t, out, up0, up1, down0, down1, g2, g1, table
):
    rows, pix = act1.shape
    frames = rows // channels
    span = blocks_t.shape[0]
    group = span // channels
    patch_cols = xcol.shape[0]
    up = (up0, up1)
    down = (down0, down1)
    count = pix // CHUNK
    half = 2 * WW
    unpool = pool_weights((half, 4 * half), 1)
    fill_table(table, frames)
    bias_sum = jnp.zeros((channels, 128), F32)
    for t in range(count + 2):
        if t < count:
            first = (t // 2) * half
            wide = min(half, pooled_grad.shape[1] - first)
            side = (t % 2) * CHUNK
            up[t % 2][...] = dot(pooled_grad[:, first : first + wide], unpool[0:wide, side : side + CHUNK])
        if 1 <= t <= count:
            at = slice((t - 1) * CHUNK, t * CHUNK)
            for r in range(0, rows, channels):
                g = (up[(t - 1) % 2][r : r + channels, :] * slope2[r : r + channels, at].astype(F32)).astype(BF)
                g2[r : r + channels, at] = g
                g = g.astype(F32)
                for c in range(0, CHUNK, 128):
                    bias_sum = bias_sum + g[:, c : c + 128]
            for r in range(0, rows, span):
                down[(t - 1) % 2][r : r + span, :] = dot(blocks_t[...], g2[r : r + span, at])
        if t >= 2:
            at = slice((t - 2) * CHUNK, (t - 1) * CHUNK)
            for r in range(0, rows, channels):
                g = down[t % 2][r : r + channels, :] * slope1[r : r + channels, at].astype(F32)
                g1[r : r + channels, at] = g.astype(BF)
    mix_bias_grad = jnp.sum(bias_sum, axis=1, keepdims=True)
    mix_grad = jnp.zeros((channels, span), F32)
    same = (iota((span, span), 0) // channels) == (iota((span, span), 1) // channels)
    for r in range(0, rows, span):
        full = jnp.where(same, dot(g2[r : r + span, :], act1[r : r + span, :], NT), 0.0)
        for a in range(group):
            mix_grad = mix_grad + full[a * channels : (a + 1) * channels]
    fold = 2 * channels
    folded = mix_grad[:, 0:fold]
    for k in range(fold, span, fold):
        folded = folded + mix_grad[:, k : k + fold]
    folded = folded + pltpu.roll(folded, channels, 1)
    full = dot(g1[...], xcol[...], NT)
    source = iota((channels, patch_cols), 1) % frames
    parts = [jnp.zeros((channels, patch_cols), F32) for _ in range(KT + 1)]
    for f in range(frames):
        piece = full[f * channels : (f + 1) * channels]
        for dt in range(KT):
            parts[dt] = parts[dt] + jnp.where(source == f + dt - 1, piece, 0.0)
        parts[KT] = parts[KT] + piece
    left = jnp.concatenate(parts, axis=0)
    taps = jnp.zeros((left.shape[0], PACK), F32)
    for _ in range(3):
        term = left.astype(BF)
        left = left - term.astype(F32)
        taps = taps + dot(term, table[...], NT)
    lane = iota((channels, PACK), 1)
    conv = jnp.zeros((channels, PACK), F32)
    for dt in range(KT + 1):
        inside = (lane >= dt * KS * KS) & (lane < (dt + 1) * KS * KS)
        conv = conv + jnp.where(inside, taps[dt * channels : (dt + 1) * channels], 0.0)
    used = KT * KS * KS + 1
    low = lane[:, 0:128]
    upper = jnp.where(low < used - 128, conv[:, 128:256], 0.0)
    upper = jnp.where(low == used - 128, mix_bias_grad, upper)
    upper = jnp.where((low == used - 127) & (iota((channels, 128), 0) == 0), loss[0:1, 0:1], upper)
    upper = jnp.where(low >= channels, folded, upper)
    out[0:channels, :] = conv[:, 0:128]
    out[channels:, :] = upper


def pair_sum(values):
    while len(values) > 1:
        values = [values[k] + values[k + 1] for k in range(0, len(values), 2)]
    return values[0]


def add_kernel(*refs):
    refs[-1][...] = pair_sum([ref[...] for ref in refs[:-1]])


def unpack_kernel(*refs):
    conv, conv_bias, mix, mix_bias, loss = refs[-5:]
    channels, taps = conv.shape
    both = pair_sum([ref[...] for ref in refs[:-5]])
    low = both[0:channels]
    high = both[channels:]
    rest = taps - 128
    conv[...] = jnp.concatenate([low, high], axis=1)[:, 0:taps]
    mix[...] = pltpu.roll(high, 128 - channels, 1)[:, 0:channels]
    same = iota((channels, channels), 0) == iota((channels, channels), 1)
    conv_bias[...] = jnp.sum(jnp.where(same, high[:, rest : rest + 1], 0.0), axis=0, keepdims=True)
    mix_bias[...] = jnp.sum(jnp.where(same, high[:, rest + 1 : rest + 2], 0.0), axis=0, keepdims=True)
    loss[...] = high[0:1, rest + 2 : rest + 3]


def owned_rows_kernel(scale, clips, each, own, block, held, last, where, count, *refs):
    pays = refs[:clips]
    wt, rbias, mask = refs[clips : clips + 3]
    before = refs[clips + 3 : clips + 3 + held]
    outs = refs[clips + 3 + held : -7]
    proj0, proj1, mixed0, mixed1, turned, stage, sems = refs[-7:]
    proj = (proj0, proj1)
    mixed = (mixed0, mixed1)
    pooled_n = mask.shape[0]
    channels = wt.shape[0]
    low_rows = pooled_n + channels
    rows = pays[0].shape[0]
    frames = rows // channels
    steps = own // block
    first = pl.multiple_of(where[0] * own, own)
    segs = block // SEG
    low = iota((frames, 128), 1) < SEG
    items = [(k, c) for k in range(steps) for c in range(each[k])]
    opening = items[0][0]
    passed = [k for k in range(steps) if each[k] == 0]
    span = pooled_n // 2

    def finished(k, part):
        at = slice(k * block, (k + 1) * block)
        rows_at = pl.ds(pl.multiple_of(part * span, 8), span)
        return pltpu.make_async_copy(before[0].at[rows_at, at], outs[0].at[rows_at, at], sems.at[steps + 2 * k + part])

    for k in passed:
        at = slice(k * block, (k + 1) * block)
        outs[1][:, at] = before[0][pooled_n:low_rows, at]
        outs[2][:, at] = before[0][low_rows : low_rows + 1, at]

        @pl.loop(0, 2)
        def _(part, k=k):
            finished(k, part).start()

    feats = [jnp.zeros((channels, block), F32) for _ in range(steps)]
    biases = [jnp.zeros((frames, block), F32) for _ in range(steps)]
    stores = []
    for t in range(len(items) + 2):
        if t < len(items):
            k, c = items[t]
            if k == opening:
                turned[:, c * rows : (c + 1) * rows] = pays[c][:, 0:pooled_n].T
            proj[t % 2][...] = dot(pays[c][:, 0:pooled_n], mask[:, k * block : (k + 1) * block])
        if 1 <= t <= len(items):
            k, c = items[t - 1]
            start = pl.multiple_of(first + k * block, block)
            base = pl.multiple_of(start // SEG * frames, segs * frames)
            packed = pays[c][pl.ds(base, segs * frames), pooled_n - SEG : pooled_n + SEG].astype(F32)
            tiles = []
            for j in range(0, segs, 2):
                even = packed[j * frames : (j + 1) * frames]
                odd = packed[(j + 1) * frames : (j + 2) * frames]
                tiles.append(jnp.where(low, pltpu.roll(even, SEG, 1), odd))
            target = jnp.concatenate(tiles, axis=1)
            w = wt[:, k * block : (k + 1) * block].astype(F32)
            alive = (start + iota((frames, block), 1)) < count[0]
            now = proj[(t - 1) % 2]
            _, grad = drive_terms(now, target, w, rbias[:, pl.ds(start, block)], alive, scale, channels)
            for f in range(frames):
                feats[k] = feats[k] + grad[f : f + 1] * now[f * channels : (f + 1) * channels, :]
                at = c * rows + f * channels
                mixed[k % 2][at : at + channels, :] = (grad[f : f + 1] * w).astype(BF)
            biases[k] = biases[k] + grad
        if t >= 2 and items[t - 2][1] == each[items[t - 2][0]] - 1:
            k = items[t - 2][0]
            at = slice(k * block, (k + 1) * block)
            used = each[k] * rows
            total = dot(turned[:, 0:used], mixed[k % 2][0:used, :])
            feat = feats[k]
            bias = jnp.sum(biases[k], axis=0, keepdims=True)
            if held:
                total = total + before[0][0:pooled_n, at]
                feat = feat + before[0][pooled_n:low_rows, at]
                bias = bias + before[0][low_rows : low_rows + 1, at]
            if last:
                stage[:, at] = total
                outs[1][:, at] = feat
                outs[2][:, at] = bias
                stores.append(pltpu.make_async_copy(stage.at[:, at], outs[0].at[:, at], sems.at[k]))
                stores[-1].start()
            else:
                outs[0][0:pooled_n, at] = total
                outs[0][pooled_n:low_rows, at] = feat
                outs[0][low_rows:, at] = jnp.broadcast_to(bias, (8, block))
    for store in stores:
        store.wait()
    for k in passed:

        @pl.loop(0, 2)
        def _(part, k=k):
            finished(k, part).wait()


def params(rows=512):
    return pltpu.CompilerParams(vmem_limit_bytes=min(56, 20 * max(1, rows // 512)) << 20)


def cost(flops, moved=1 << 20):
    return pl.CostEstimate(flops=int(flops), transcendentals=0, bytes_accessed=int(moved))


def in_hbm(*arrays):
    return [pltpu.with_memory_space_constraint(a, pltpu.HBM) for a in arrays]


def rounds_of(size):
    assert size & (size - 1) == 0
    bits = [1 << k for k in range(size.bit_length() - 1)]
    groups = [bits[:1]] if len(bits) % 2 else []
    bits = bits[len(bits) % 2 :]
    groups += [[low, low * 2, low * 3] for low in bits[::2]]
    return groups


def xor_pairs(size, mask):
    return [(i, i ^ mask) for i in range(size)]


def per_device(
    video, responses, assignment, counts, conv_weight, conv_bias, mix_weight, mix_bias, masks, feat_w, readout_bias
):
    sess_total = lax.axis_size("sess")
    clip_total = lax.axis_size("clip")
    clip_block, frame_block, pix = video.shape
    neurons = responses.shape[2]
    pooled_n = masks.shape[2]
    channels, taps = conv_weight.shape
    frames = frame_block * sess_total
    rows = frames * channels
    own = neurons // clip_total
    block = min(512, own)
    assert clip_block == sess_total and frame_block == 1 and masks.shape[0] == 1
    assert neurons == channels * SEG and pooled_n % 128 == SEG and pix == HH * WW
    scale = 1.0 / (clip_block * clip_total * frames)

    group = max(1, 256 // channels)
    lines = 16
    packet = 512
    assert neurons + pix <= lines * packet
    send = pl.pallas_call(
        select_kernel,
        out_shape=jax.ShapeDtypeStruct((sess_total, lines, packet), BF),
        compiler_params=params(),
        name="select",
    )(*in_hbm(assignment[None, :], video.reshape(clip_block, pix), responses.reshape(clip_block, neurons)))
    where = lax.axis_index("clip").astype(jnp.int32)[None]
    send, where = lax.optimization_barrier((send, where))
    recv = lax.all_to_all(send, "sess", split_axis=0, concat_axis=0, tiled=True)

    patch_cols = KS * DX * frames
    span = channels * group
    half = 2 * WW
    wbig, blocks, blocks_t, bias, pool = pl.pallas_call(
        functools.partial(prep_kernel, frames),
        out_shape=(
            jax.ShapeDtypeStruct((rows, patch_cols), BF),
            jax.ShapeDtypeStruct((span, span), BF),
            jax.ShapeDtypeStruct((span, span), BF),
            jax.ShapeDtypeStruct((2, channels, 128), F32),
            jax.ShapeDtypeStruct((4 * half, half), BF),
        ),
        scratch_shapes=[pltpu.VMEM((PACK, patch_cols), BF)],
        compiler_params=params(),
        cost_estimate=cost(1 << 27),
        name="prep",
    )(*in_hbm(conv_weight, conv_bias[None, :], mix_weight, mix_bias[None, :]))

    wt = jnp.swapaxes(feat_w, 1, 2).reshape(channels, neurons)
    mask_t = jnp.swapaxes(masks, 1, 2).reshape(pooled_n, neurons)
    rbias = readout_bias
    (mask_far,) = in_hbm(mask_t)
    width = pooled_n + SEG
    vmem = pl.BlockSpec(memory_space=pltpu.VMEM)
    anywhere = pl.BlockSpec(memory_space=pl.ANY)
    smem = pl.BlockSpec(memory_space=pltpu.SMEM)
    pay, target, act1, slope1, slope2, xcol, mask_near = pl.pallas_call(
        core_forward_kernel,
        out_shape=(
            jax.ShapeDtypeStruct((rows, width), BF),
            jax.ShapeDtypeStruct((frames, neurons), F32),
            jax.ShapeDtypeStruct((rows, pix), BF),
            jax.ShapeDtypeStruct((rows, pix), BF),
            jax.ShapeDtypeStruct((rows, pix), BF),
            jax.ShapeDtypeStruct((patch_cols, pix), BF),
            jax.ShapeDtypeStruct((pooled_n, neurons), BF),
        ),
        in_specs=[vmem] * 5 + [anywhere],
        scratch_shapes=[pltpu.VMEM((rows, CHUNK), F32)] * 4
        + [pltpu.VMEM((rows, pix), BF), pltpu.SemaphoreType.DMA((pooled_n // SEG,))],
        compiler_params=params(),
        cost_estimate=cost(2 * rows * pix * patch_cols, 8 * rows * pix),
        name="core_forward",
    )(recv, wbig, blocks, bias, pool, mask_far)

    near = {0: pay}
    for mask in range(1, clip_total):
        if mask % 2 == 0 or mask == 1:
            near[mask] = lax.ppermute(pay, "clip", xor_pairs(clip_total, mask))

    big = min(512, neurons)
    work = 2 * rows * neurons * pooled_n
    pooled_grad, loss, mask_own, wt_own = pl.pallas_call(
        functools.partial(readout_kernel, scale),
        in_specs=[smem, smem] + [vmem] * 5,
        out_shape=(
            jax.ShapeDtypeStruct((rows, pooled_n), BF),
            jax.ShapeDtypeStruct((8, 128), F32),
            jax.ShapeDtypeStruct((pooled_n, own), BF),
            jax.ShapeDtypeStruct((channels, own), BF),
        ),
        scratch_shapes=[pltpu.VMEM((rows, big), F32)] * 2
        + [pltpu.VMEM((rows, neurons), BF), pltpu.VMEM((pooled_n, rows), F32)],
        compiler_params=params(),
        cost_estimate=cost(2 * work, 2 * neurons * pooled_n),
        name="readout",
    )(where, counts, target, pay, mask_near, wt, rbias)

    core = pl.pallas_call(
        functools.partial(core_backward_kernel, channels),
        out_shape=jax.ShapeDtypeStruct((2 * channels, 128), F32),
        scratch_shapes=[pltpu.VMEM((rows, CHUNK), F32)] * 4
        + [pltpu.VMEM((rows, pix), BF)] * 2
        + [pltpu.VMEM((PACK, patch_cols), BF)],
        compiler_params=params(),
        cost_estimate=cost(2 * work, 8 * rows * pix),
        name="core_backward",
    )(pooled_grad, loss, act1, slope1, slope2, xcol, blocks_t)

    def owned_rows(clips, each, held, last):
        return pl.pallas_call(
            functools.partial(owned_rows_kernel, scale, len(clips), each, own, block, len(held), last),
            in_specs=[smem, smem] + [vmem] * (len(clips) + 3 + len(held)),
            out_specs=[anywhere, vmem, vmem] if last else [vmem],
            out_shape=[
                jax.ShapeDtypeStruct((pooled_n, own), F32),
                jax.ShapeDtypeStruct((channels, own), F32),
                jax.ShapeDtypeStruct((1, own), F32),
            ]
            if last
            else [jax.ShapeDtypeStruct((pooled_n + channels + 8, own), F32)],
            scratch_shapes=[pltpu.VMEM((rows, block), F32)] * 2
            + [pltpu.VMEM((len(clips) * rows, block), BF)] * 2
            + [
                pltpu.VMEM((pooled_n, len(clips) * rows), BF),
                pltpu.VMEM((pooled_n, own) if last else (8, 128), F32),
                pltpu.SemaphoreType.DMA((3 * (own // block),)),
            ],
            compiler_params=params(rows),
            cost_estimate=cost(2 * work * len(clips) // clip_total, 4 * own * pooled_n),
            name="owned_rows",
        )(where, counts, *clips, wt_own, rbias, mask_own, *held)

    far = [mask for mask in near if mask > 1]
    reached, _ = lax.optimization_barrier(([near[mask] for mask in far], core))
    others = [lax.ppermute(value, "clip", xor_pairs(clip_total, 1)) for value in reached]
    steps = own // block
    early_steps = (steps + 1) // 2 if steps > 1 else 0
    middle = reached + others if early_steps else reached
    work_of = [
        ([near[0], near[1]], (2,) * steps),
        (middle, (len(middle),) * early_steps + (len(reached),) * (steps - early_steps)),
        (others, (0,) * early_steps + (len(others),) * (steps - early_steps)),
    ]
    rounds = [("sess", masks) for masks in rounds_of(sess_total)] + [("clip", masks) for masks in rounds_of(clip_total)]
    held = ()
    for step, (axis, masks) in enumerate(rounds):
        got = [core] + [lax.ppermute(core, axis, xor_pairs(lax.axis_size(axis), mask)) for mask in masks]
        if step < len(work_of):
            held = owned_rows(*work_of[step], held, step == len(work_of) - 1)
            got, held = lax.optimization_barrier((got, held))
        if step < len(rounds) - 1:
            core = pl.pallas_call(
                add_kernel,
                out_shape=jax.ShapeDtypeStruct(core.shape, F32),
                compiler_params=params(),
                name="add",
            )(*got)
            core, held = lax.optimization_barrier((core, held))
    mask_grad, feat_grad, grad_rbias = held
    grad_conv, grad_cb, grad_mix, grad_mb, loss = pl.pallas_call(
        unpack_kernel,
        out_shape=(
            jax.ShapeDtypeStruct((channels, taps), F32),
            jax.ShapeDtypeStruct((1, channels), F32),
            jax.ShapeDtypeStruct((channels, channels), F32),
            jax.ShapeDtypeStruct((1, channels), F32),
            jax.ShapeDtypeStruct((1, 1), F32),
        ),
        compiler_params=params(),
        name="unpack",
    )(*got)
    return (
        loss.reshape(()),
        grad_conv,
        grad_cb.reshape(channels),
        grad_mix,
        grad_mb.reshape(channels),
        jnp.swapaxes(mask_grad[None], 1, 2),
        jnp.swapaxes(feat_grad[None], 1, 2),
        grad_rbias,
    )


def solution(mesh):
    return jax.shard_map(
        per_device,
        mesh=mesh,
        in_specs=(
            P("clip", "sess", None),
            P("clip", "sess", None),
            P("clip"),
            P("sess"),
            P(),
            P(),
            P(),
            P(),
            P("sess", None, None),
            P("sess", None, None),
            P("sess", None),
        ),
        out_specs=(
            P(),
            P(),
            P(),
            P(),
            P(),
            P("sess", "clip", None),
            P("sess", "clip", None),
            P("sess", "clip"),
        ),
        check_vma=False,
    )
```

```python
import functools

import jax
import jax.numpy as jnp
from jax import lax
from jax.experimental import pallas as pl
from jax.experimental.pallas import tpu as pltpu
from jax.sharding import PartitionSpec as P

HH = 36
WW = 64
KS = 7
KT = 3
DX = 8
PACK = 256
SEG = 64
CHUNK = 4 * WW
BF = jnp.bfloat16
F32 = jnp.float32
NT = (((1,), (1,)), ((), ()))


def dot(a, b, dims=(((1,), (0,)), ((), ())), precision=None):
    return lax.dot_general(a, b, dims, precision=precision, preferred_element_type=F32)


def iota(shape, axis):
    return lax.broadcasted_iota(jnp.int32, shape, axis)


def bias_column(row):
    size = row.shape[1]
    return jnp.sum(jnp.where(iota((size, size), 0) == iota((size, size), 1), row, 0.0), axis=1, keepdims=True)


def select_kernel(assign, video, responses, out):
    owners, lines, width = out.shape
    clips, pix = video.shape
    neurons = responses.shape[1]
    pick = (iota((owners, clips), 0) == assign[...]).astype(BF)
    first = dot(pick, responses[...])
    second = dot(pick, video[...])
    rows = [first[:, p : p + width] for p in range(0, neurons, width)]
    for p in range(0, pix, width):
        piece = second[:, p : p + width]
        if piece.shape[1] < width:
            piece = jnp.concatenate([piece, jnp.zeros((owners, width - piece.shape[1]), F32)], axis=1)
        rows.append(piece)
    while len(rows) < lines:
        rows.append(jnp.zeros((owners, width), F32))
    out[...] = jnp.stack(rows, axis=1).astype(BF)


def fill_table(table, frames):
    t = iota(table.shape, 0)
    l = iota(table.shape, 1)
    dy = l // (DX * frames)
    dx = (l // frames) % DX
    place = dy * KS + dx
    hit = (t == place) | (t == place + KS * KS) | (t == place + 2 * KS * KS)
    last = (t == KT * KS * KS) & (l == KS * frames)
    table[...] = jnp.where(((dx < KS) & hit & (t < KT * KS * KS)) | last, 1.0, 0.0).astype(BF)


def pool_weights(shape, pixel_axis):
    pixel = iota(shape, pixel_axis)
    target = (pixel // (2 * WW)) * (WW // 2) + (pixel % WW) // 2
    return jnp.where(target == iota(shape, 1 - pixel_axis), 0.25, 0.0).astype(BF)


def prep_kernel(frames, weight, cbias, mix, mbias, wbig, blocks, blocks_t, bias, pool, table):
    channels, taps = weight.shape
    patch_cols = wbig.shape[1]
    group = blocks.shape[0] // channels
    fill_table(table, frames)
    pool[...] = pool_weights(pool.shape, 0)
    size = channels * group
    same = (iota((size, size), 0) // channels) == (iota((size, size), 1) // channels)
    square = mix[...].astype(F32)
    for ref, base in ((blocks, square), (blocks_t, square.T)):
        wide = jnp.concatenate([base] * group, axis=1)
        ref[...] = jnp.where(same, jnp.concatenate([wide] * group, axis=0), 0.0).astype(BF)
    bias[0] = jnp.broadcast_to(bias_column(cbias[...]), bias.shape[1:])
    bias[1] = jnp.broadcast_to(bias_column(mbias[...]), bias.shape[1:])
    tap = iota((channels, taps), 1)
    weights = weight[...].astype(F32)
    split = [
        jnp.where((tap >= dt * KS * KS) & (tap < (dt + 1) * KS * KS), weights, 0.0).astype(BF)
        for dt in range(KT)
    ]
    spread = dot(jnp.concatenate(split, axis=0), table[0:taps, :])
    source = iota((channels, patch_cols), 1) % frames
    for f in range(frames):
        total = jnp.zeros((channels, patch_cols), F32)
        for dt in range(KT):
            total = total + jnp.where(source == f + dt - 1, spread[dt * channels : (dt + 1) * channels], 0.0)
        wbig[f * channels : (f + 1) * channels, :] = total.astype(BF)


def core_forward_kernel(
    recv,
    wbig,
    blocks,
    bias,
    pool,
    mask_in,
    pay,
    target,
    act1,
    slope1,
    slope2,
    xcol,
    mask,
    pre0,
    pre1,
    mid0,
    mid1,
    feats,
    sems,
):
    copy_count = mask.shape[0] // SEG

    def mask_copy(k):
        rows_at = pl.ds(pl.multiple_of(k * SEG, SEG), SEG)
        return pltpu.make_async_copy(mask_in.at[rows_at, :], mask.at[rows_at, :], sems.at[k])

    @pl.loop(0, copy_count)
    def _(k):
        mask_copy(k).start()

    frames, _, width = recv.shape
    rows, pix = act1.shape
    channels = bias.shape[1]
    neurons = target.shape[1]
    span = blocks.shape[0]
    packet = recv[...].astype(F32)
    lines = [packet[:, j, :] for j in range((neurons + pix + width - 1) // width)]
    held = neurons // width
    for j in range(held):
        target[:, j * width : (j + 1) * width] = lines[j]
    video = jnp.concatenate(lines[held:], axis=1)[:, 0:pix]
    lane = iota((frames, pix), 1)
    col = lane % WW
    row = lane // WW
    per_store = max(1, 16 // frames)
    for dx0 in range(0, DX, per_store):
        shifted = []
        for dx in range(dx0, dx0 + per_store):
            s = dx - KS // 2
            if dx == KS:
                shifted.append(None)
            elif s == 0:
                shifted.append(video)
            else:
                rolled = pltpu.roll(video, (-s) % pix, 1)
                shifted.append(jnp.where((col + s >= 0) & (col + s < WW), rolled, 0.0))
        for dy in range(KS):
            t = dy - KS // 2
            parts = []
            for item in shifted:
                if item is None:
                    parts.append(jnp.ones((frames, pix), F32))
                elif t == 0:
                    parts.append(item)
                else:
                    moved = pltpu.roll(item, (-t * WW) % pix, 1)
                    parts.append(jnp.where((row + t >= 0) & (row + t < HH), moved, 0.0))
            base = (dy * DX + dx0) * frames
            block = parts[0] if len(parts) == 1 else jnp.concatenate(parts, axis=0)
            xcol[base : base + per_store * frames, :] = block.astype(BF)
    half = 2 * WW
    pre = (pre0, pre1)
    mid = (mid0, mid1)
    count = pix // CHUNK
    wide = wbig[...]

    def activate(source, which, act, slope, at):
        add = jnp.concatenate([bias[which]] * (CHUNK // 128), axis=1)
        for r in range(0, rows, channels):
            x = source[r : r + channels, :] + add
            e = jnp.exp(jnp.minimum(x, 0.0))
            act[r : r + channels, at] = (jnp.maximum(x, 0.0) + (e - 1.0)).astype(BF)
            slope[r : r + channels, at] = e.astype(BF)

    for t in range(count + 2):
        if t < count:
            pre[t % 2][...] = dot(wide, xcol[:, t * CHUNK : (t + 1) * CHUNK])
        if 1 <= t <= count:
            at = slice((t - 1) * CHUNK, t * CHUNK)
            activate(pre[(t - 1) % 2], 0, act1, slope1, at)
            for r in range(0, rows, span):
                mid[(t - 1) % 2][r : r + span, :] = dot(blocks[...], act1[r : r + span, at])
        if t >= 2:
            at = slice((t - 2) * CHUNK, (t - 1) * CHUNK)
            activate(mid[t % 2], 1, feats, slope2, at)
            if t % 2 == 1:
                first = (t - 3) * CHUNK
                pooled = dot(feats[:, first : first + 2 * CHUNK], pool[...])
                pay[:, first // 4 : first // 4 + half] = pooled.astype(BF)
    p = pix - CHUNK
    tail = dot(feats[:, p:pix], pool[0:CHUNK, :])
    pieces = []
    for t in range(neurons // half):
        at = t * half
        tile = lines[at // width][:, at % width : at % width + half]
        pieces += [pltpu.roll(tile, SEG, 1), tile]
    packed = jnp.concatenate(pieces, axis=0)
    pay[:, p // 4 : p // 4 + half] = jnp.where(iota((rows, half), 1) < SEG, tail, packed).astype(BF)

    @pl.loop(0, copy_count)
    def _(k):
        mask_copy(k).wait()


def drive_terms(projected, target, w, rbias, alive, scale, channels):
    frames = target.shape[0]
    sums = [
        jnp.sum(projected[f * channels : (f + 1) * channels, :] * w, axis=0, keepdims=True)
        for f in range(frames)
    ]
    drive = jnp.concatenate(sums, axis=0) + rbias
    e = jnp.exp(-jnp.abs(drive))
    rate = jnp.maximum(drive, 0.0) + jnp.log(1.0 + e) + 0.1
    sig = jnp.where(drive >= 0, 1.0, e) / (1.0 + e)
    grad = jnp.where(alive, (1.0 - target / rate) * sig, 0.0) * scale
    return rate, grad


def readout_kernel(
    scale,
    where,
    count,
    target,
    pay,
    mask,
    wt,
    rbias,
    pooled_grad,
    loss,
    mask_own,
    wt_own,
    proj0,
    proj1,
    mixed,
    acc,
):
    pooled_n, neurons = mask.shape
    own = mask_own.shape[1]
    channels = wt.shape[0]
    frames = target.shape[0]
    proj = (proj0, proj1)
    block = proj0.shape[1]
    steps = neurons // block
    first = pl.multiple_of(where[0] * own, own)
    mask_own[...] = mask[:, pl.ds(first, own)]
    wt_own[...] = wt[:, pl.ds(first, own)]
    pooled = pay[:, 0:pooled_n]
    loss_sum = jnp.zeros((frames, block), F32)
    begun = False
    for t in range(steps + 2):
        if t < steps:
            proj[t % 2][...] = dot(pooled, mask[:, t * block : (t + 1) * block])
        if 1 <= t <= steps:
            at = slice((t - 1) * block, t * block)
            w = wt[:, at].astype(F32)
            goal = target[:, at]
            alive = ((t - 1) * block + iota((frames, block), 1)) < count[0]
            rate, grad = drive_terms(proj[(t - 1) % 2], goal, w, rbias[:, at], alive, scale, channels)
            loss_sum = loss_sum + jnp.where(alive, rate - goal * jnp.log(rate), 0.0)
            for f in range(frames):
                mixed[f * channels : (f + 1) * channels, at] = (grad[f : f + 1] * w).astype(BF)
        last = t - 2
        if last >= 0 and (last % 4 == 3 or last == steps - 1):
            low = last // 4 * 4 * block
            at = slice(low, (last + 1) * block)
            part = dot(mask[:, at], mixed[:, at], NT)
            acc[...] = acc[...] + part if begun else part
            begun = True
    pooled_grad[...] = acc[...].T.astype(BF)
    loss[...] = jnp.broadcast_to(jnp.sum(loss_sum, keepdims=True) * scale, loss.shape)


def core_backward_kernel(
    channels, pooled_grad, loss, act1, slope1, slope2, xcol, blocks_t, out, up0, up1, down0, down1, g2, g1, table
):
    rows, pix = act1.shape
    frames = rows // channels
    span = blocks_t.shape[0]
    group = span // channels
    patch_cols = xcol.shape[0]
    up = (up0, up1)
    down = (down0, down1)
    count = pix // CHUNK
    half = 2 * WW
    unpool = pool_weights((half, 4 * half), 1)
    fill_table(table, frames)
    bias_sum = jnp.zeros((channels, 128), F32)
    for t in range(count + 2):
        if t < count:
            first = (t // 2) * half
            wide = min(half, pooled_grad.shape[1] - first)
            side = (t % 2) * CHUNK
            up[t % 2][...] = dot(pooled_grad[:, first : first + wide], unpool[0:wide, side : side + CHUNK])
        if 1 <= t <= count:
            at = slice((t - 1) * CHUNK, t * CHUNK)
            for r in range(0, rows, channels):
                g = (up[(t - 1) % 2][r : r + channels, :] * slope2[r : r + channels, at].astype(F32)).astype(BF)
                g2[r : r + channels, at] = g
                g = g.astype(F32)
                for c in range(0, CHUNK, 128):
                    bias_sum = bias_sum + g[:, c : c + 128]
            for r in range(0, rows, span):
                down[(t - 1) % 2][r : r + span, :] = dot(blocks_t[...], g2[r : r + span, at])
        if t >= 2:
            at = slice((t - 2) * CHUNK, (t - 1) * CHUNK)
            for r in range(0, rows, channels):
                g = down[t % 2][r : r + channels, :] * slope1[r : r + channels, at].astype(F32)
                g1[r : r + channels, at] = g.astype(BF)
    mix_bias_grad = jnp.sum(bias_sum, axis=1, keepdims=True)
    mix_grad = jnp.zeros((channels, span), F32)
    same = (iota((span, span), 0) // channels) == (iota((span, span), 1) // channels)
    for r in range(0, rows, span):
        full = jnp.where(same, dot(g2[r : r + span, :], act1[r : r + span, :], NT), 0.0)
        for a in range(group):
            mix_grad = mix_grad + full[a * channels : (a + 1) * channels]
    fold = 2 * channels
    folded = mix_grad[:, 0:fold]
    for k in range(fold, span, fold):
        folded = folded + mix_grad[:, k : k + fold]
    folded = folded + pltpu.roll(folded, channels, 1)
    full = dot(g1[...], xcol[...], NT)
    source = iota((channels, patch_cols), 1) % frames
    parts = [jnp.zeros((channels, patch_cols), F32) for _ in range(KT + 1)]
    for f in range(frames):
        piece = full[f * channels : (f + 1) * channels]
        for dt in range(KT):
            parts[dt] = parts[dt] + jnp.where(source == f + dt - 1, piece, 0.0)
        parts[KT] = parts[KT] + piece
    left = jnp.concatenate(parts, axis=0)
    taps = jnp.zeros((left.shape[0], PACK), F32)
    for _ in range(3):
        term = left.astype(BF)
        left = left - term.astype(F32)
        taps = taps + dot(term, table[...], NT)
    lane = iota((channels, PACK), 1)
    conv = jnp.zeros((channels, PACK), F32)
    for dt in range(KT + 1):
        inside = (lane >= dt * KS * KS) & (lane < (dt + 1) * KS * KS)
        conv = conv + jnp.where(inside, taps[dt * channels : (dt + 1) * channels], 0.0)
    used = KT * KS * KS + 1
    low = lane[:, 0:128]
    upper = jnp.where(low < used - 128, conv[:, 128:256], 0.0)
    upper = jnp.where(low == used - 128, mix_bias_grad, upper)
    upper = jnp.where((low == used - 127) & (iota((channels, 128), 0) == 0), loss[0:1, 0:1], upper)
    upper = jnp.where(low >= channels, folded, upper)
    out[0:channels, :] = conv[:, 0:128]
    out[channels:, :] = upper


def pair_sum(values):
    while len(values) > 1:
        values = [values[k] + values[k + 1] for k in range(0, len(values), 2)]
    return values[0]


def add_kernel(*refs):
    refs[-1][...] = pair_sum([ref[...] for ref in refs[:-1]])


def unpack_kernel(*refs):
    conv, conv_bias, mix, mix_bias, loss = refs[-5:]
    channels, taps = conv.shape
    both = pair_sum([ref[...] for ref in refs[:-5]])
    low = both[0:channels]
    high = both[channels:]
    rest = taps - 128
    conv[...] = jnp.concatenate([low, high], axis=1)[:, 0:taps]
    mix[...] = pltpu.roll(high, 128 - channels, 1)[:, 0:channels]
    same = iota((channels, channels), 0) == iota((channels, channels), 1)
    conv_bias[...] = jnp.sum(jnp.where(same, high[:, rest : rest + 1], 0.0), axis=0, keepdims=True)
    mix_bias[...] = jnp.sum(jnp.where(same, high[:, rest + 1 : rest + 2], 0.0), axis=0, keepdims=True)
    loss[...] = high[0:1, rest + 2 : rest + 3]


def owned_rows_kernel(scale, clips, own, block, held, last, where, count, *refs):
    pays = refs[:clips]
    wt, rbias, mask = refs[clips : clips + 3]
    before = refs[clips + 3 : clips + 3 + held]
    outs = refs[clips + 3 + held : -7]
    proj0, proj1, mixed0, mixed1, turned, stage, sems = refs[-7:]
    proj = (proj0, proj1)
    mixed = (mixed0, mixed1)
    pooled_n = mask.shape[0]
    channels = wt.shape[0]
    low_rows = pooled_n + channels
    rows = pays[0].shape[0]
    frames = rows // channels
    steps = own // block
    first = pl.multiple_of(where[0] * own, own)
    segs = block // SEG
    low = iota((frames, 128), 1) < SEG
    items = [(k, c) for k in range(steps) for c in range(clips)]
    feats = [jnp.zeros((channels, block), F32) for _ in range(steps)]
    biases = [jnp.zeros((frames, block), F32) for _ in range(steps)]
    stores = []
    for t in range(len(items) + 2):
        if t < len(items):
            k, c = items[t]
            if k == 0:
                turned[:, c * rows : (c + 1) * rows] = pays[c][:, 0:pooled_n].T
            proj[t % 2][...] = dot(pays[c][:, 0:pooled_n], mask[:, k * block : (k + 1) * block])
        if 1 <= t <= len(items):
            k, c = items[t - 1]
            start = pl.multiple_of(first + k * block, block)
            base = pl.multiple_of(start // SEG * frames, segs * frames)
            packed = pays[c][pl.ds(base, segs * frames), pooled_n - SEG : pooled_n + SEG].astype(F32)
            tiles = []
            for j in range(0, segs, 2):
                even = packed[j * frames : (j + 1) * frames]
                odd = packed[(j + 1) * frames : (j + 2) * frames]
                tiles.append(jnp.where(low, pltpu.roll(even, SEG, 1), odd))
            target = jnp.concatenate(tiles, axis=1)
            w = wt[:, k * block : (k + 1) * block].astype(F32)
            alive = (start + iota((frames, block), 1)) < count[0]
            now = proj[(t - 1) % 2]
            _, grad = drive_terms(now, target, w, rbias[:, pl.ds(start, block)], alive, scale, channels)
            for f in range(frames):
                feats[k] = feats[k] + grad[f : f + 1] * now[f * channels : (f + 1) * channels, :]
                at = c * rows + f * channels
                mixed[k % 2][at : at + channels, :] = (grad[f : f + 1] * w).astype(BF)
            biases[k] = biases[k] + grad
        if t >= 2 and items[t - 2][1] == clips - 1:
            k = items[t - 2][0]
            at = slice(k * block, (k + 1) * block)
            total = dot(turned[...], mixed[k % 2][...])
            feat = feats[k]
            bias = jnp.sum(biases[k], axis=0, keepdims=True)
            if held:
                total = total + before[0][0:pooled_n, at]
                feat = feat + before[0][pooled_n:low_rows, at]
                bias = bias + before[0][low_rows : low_rows + 1, at]
            if last:
                stage[:, at] = total
                outs[1][:, at] = feat
                outs[2][:, at] = bias
                stores.append(pltpu.make_async_copy(stage.at[:, at], outs[0].at[:, at], sems.at[k]))
                stores[-1].start()
            else:
                outs[0][0:pooled_n, at] = total
                outs[0][pooled_n:low_rows, at] = feat
                outs[0][low_rows:, at] = jnp.broadcast_to(bias, (8, block))
    for store in stores:
        store.wait()


def params(rows=512):
    return pltpu.CompilerParams(vmem_limit_bytes=min(56, 20 * max(1, rows // 512)) << 20)


def cost(flops, moved=1 << 20):
    return pl.CostEstimate(flops=int(flops), transcendentals=0, bytes_accessed=int(moved))


def in_hbm(*arrays):
    return [pltpu.with_memory_space_constraint(a, pltpu.HBM) for a in arrays]


def rounds_of(size):
    assert size & (size - 1) == 0
    bits = [1 << k for k in range(size.bit_length() - 1)]
    groups = [bits[:1]] if len(bits) % 2 else []
    bits = bits[len(bits) % 2 :]
    groups += [[low, low * 2, low * 3] for low in bits[::2]]
    return groups


def xor_pairs(size, mask):
    return [(i, i ^ mask) for i in range(size)]


def per_device(
    video, responses, assignment, counts, conv_weight, conv_bias, mix_weight, mix_bias, masks, feat_w, readout_bias
):
    sess_total = lax.axis_size("sess")
    clip_total = lax.axis_size("clip")
    clip_block, frame_block, pix = video.shape
    neurons = responses.shape[2]
    pooled_n = masks.shape[2]
    channels, taps = conv_weight.shape
    frames = frame_block * sess_total
    rows = frames * channels
    own = neurons // clip_total
    block = min(512, own)
    assert clip_block == sess_total and frame_block == 1 and masks.shape[0] == 1
    assert neurons == channels * SEG and pooled_n % 128 == SEG and pix == HH * WW
    scale = 1.0 / (clip_block * clip_total * frames)

    group = max(1, 256 // channels)
    lines = 16
    packet = 512
    assert neurons + pix <= lines * packet
    send = pl.pallas_call(
        select_kernel,
        out_shape=jax.ShapeDtypeStruct((sess_total, lines, packet), BF),
        compiler_params=params(),
        name="select",
    )(*in_hbm(assignment[None, :], video.reshape(clip_block, pix), responses.reshape(clip_block, neurons)))
    where = lax.axis_index("clip").astype(jnp.int32)[None]
    send, where = lax.optimization_barrier((send, where))
    recv = lax.all_to_all(send, "sess", split_axis=0, concat_axis=0, tiled=True)

    patch_cols = KS * DX * frames
    span = channels * group
    half = 2 * WW
    wbig, blocks, blocks_t, bias, pool = pl.pallas_call(
        functools.partial(prep_kernel, frames),
        out_shape=(
            jax.ShapeDtypeStruct((rows, patch_cols), BF),
            jax.ShapeDtypeStruct((span, span), BF),
            jax.ShapeDtypeStruct((span, span), BF),
            jax.ShapeDtypeStruct((2, channels, 128), F32),
            jax.ShapeDtypeStruct((4 * half, half), BF),
        ),
        scratch_shapes=[pltpu.VMEM((PACK, patch_cols), BF)],
        compiler_params=params(),
        cost_estimate=cost(1 << 27),
        name="prep",
    )(*in_hbm(conv_weight, conv_bias[None, :], mix_weight, mix_bias[None, :]))

    wt = jnp.swapaxes(feat_w, 1, 2).reshape(channels, neurons)
    mask_t = jnp.swapaxes(masks, 1, 2).reshape(pooled_n, neurons)
    rbias = readout_bias
    (mask_far,) = in_hbm(mask_t)
    width = pooled_n + SEG
    vmem = pl.BlockSpec(memory_space=pltpu.VMEM)
    anywhere = pl.BlockSpec(memory_space=pl.ANY)
    smem = pl.BlockSpec(memory_space=pltpu.SMEM)
    pay, target, act1, slope1, slope2, xcol, mask_near = pl.pallas_call(
        core_forward_kernel,
        out_shape=(
            jax.ShapeDtypeStruct((rows, width), BF),
            jax.ShapeDtypeStruct((frames, neurons), F32),
            jax.ShapeDtypeStruct((rows, pix), BF),
            jax.ShapeDtypeStruct((rows, pix), BF),
            jax.ShapeDtypeStruct((rows, pix), BF),
            jax.ShapeDtypeStruct((patch_cols, pix), BF),
            jax.ShapeDtypeStruct((pooled_n, neurons), BF),
        ),
        in_specs=[vmem] * 5 + [anywhere],
        scratch_shapes=[pltpu.VMEM((rows, CHUNK), F32)] * 4
        + [pltpu.VMEM((rows, pix), BF), pltpu.SemaphoreType.DMA((pooled_n // SEG,))],
        compiler_params=params(),
        cost_estimate=cost(2 * rows * pix * patch_cols, 8 * rows * pix),
        name="core_forward",
    )(recv, wbig, blocks, bias, pool, mask_far)

    near = {0: pay}
    for mask in range(1, clip_total):
        if mask % 2 == 0 or mask == 1:
            near[mask] = lax.ppermute(pay, "clip", xor_pairs(clip_total, mask))

    big = min(512, neurons)
    work = 2 * rows * neurons * pooled_n
    pooled_grad, loss, mask_own, wt_own = pl.pallas_call(
        functools.partial(readout_kernel, scale),
        in_specs=[smem, smem] + [vmem] * 5,
        out_shape=(
            jax.ShapeDtypeStruct((rows, pooled_n), BF),
            jax.ShapeDtypeStruct((8, 128), F32),
            jax.ShapeDtypeStruct((pooled_n, own), BF),
            jax.ShapeDtypeStruct((channels, own), BF),
        ),
        scratch_shapes=[pltpu.VMEM((rows, big), F32)] * 2
        + [pltpu.VMEM((rows, neurons), BF), pltpu.VMEM((pooled_n, rows), F32)],
        compiler_params=params(),
        cost_estimate=cost(2 * work, 2 * neurons * pooled_n),
        name="readout",
    )(where, counts, target, pay, mask_near, wt, rbias)

    core = pl.pallas_call(
        functools.partial(core_backward_kernel, channels),
        out_shape=jax.ShapeDtypeStruct((2 * channels, 128), F32),
        scratch_shapes=[pltpu.VMEM((rows, CHUNK), F32)] * 4
        + [pltpu.VMEM((rows, pix), BF)] * 2
        + [pltpu.VMEM((PACK, patch_cols), BF)],
        compiler_params=params(),
        cost_estimate=cost(2 * work, 8 * rows * pix),
        name="core_backward",
    )(pooled_grad, loss, act1, slope1, slope2, xcol, blocks_t)

    def owned_rows(clips, held, last):
        return pl.pallas_call(
            functools.partial(owned_rows_kernel, scale, len(clips), own, block, len(held), last),
            in_specs=[smem, smem] + [vmem] * (len(clips) + 3 + len(held)),
            out_specs=[anywhere, vmem, vmem] if last else [vmem],
            out_shape=[
                jax.ShapeDtypeStruct((pooled_n, own), F32),
                jax.ShapeDtypeStruct((channels, own), F32),
                jax.ShapeDtypeStruct((1, own), F32),
            ]
            if last
            else [jax.ShapeDtypeStruct((pooled_n + channels + 8, own), F32)],
            scratch_shapes=[pltpu.VMEM((rows, block), F32)] * 2
            + [pltpu.VMEM((len(clips) * rows, block), BF)] * 2
            + [
                pltpu.VMEM((pooled_n, len(clips) * rows), BF),
                pltpu.VMEM((pooled_n, own) if last else (8, 128), F32),
                pltpu.SemaphoreType.DMA((own // block,)),
            ],
            compiler_params=params(rows),
            cost_estimate=cost(2 * work * len(clips) // clip_total, 4 * own * pooled_n),
            name="owned_rows",
        )(where, counts, *clips, wt_own, rbias, mask_own, *held)

    far = [mask for mask in near if mask > 1]
    reached, _ = lax.optimization_barrier(([near[mask] for mask in far], core))
    others = [lax.ppermute(value, "clip", xor_pairs(clip_total, 1)) for value in reached]
    work_of = [[near[0], near[1]], reached, others]
    rounds = [("clip", masks) for masks in rounds_of(clip_total)] + [("sess", masks) for masks in rounds_of(sess_total)]
    held = ()
    for step, (axis, masks) in enumerate(rounds):
        got = [core] + [lax.ppermute(core, axis, xor_pairs(lax.axis_size(axis), mask)) for mask in masks]
        if step < len(work_of):
            held = owned_rows(work_of[step], held, step == len(work_of) - 1)
            got, held = lax.optimization_barrier((got, held))
        if step < len(rounds) - 1:
            core = pl.pallas_call(
                add_kernel,
                out_shape=jax.ShapeDtypeStruct(core.shape, F32),
                compiler_params=params(),
                name="add",
            )(*got)
            core, held = lax.optimization_barrier((core, held))
    mask_grad, feat_grad, grad_rbias = held
    grad_conv, grad_cb, grad_mix, grad_mb, loss = pl.pallas_call(
        unpack_kernel,
        out_shape=(
            jax.ShapeDtypeStruct((channels, taps), F32),
            jax.ShapeDtypeStruct((1, channels), F32),
            jax.ShapeDtypeStruct((channels, channels), F32),
            jax.ShapeDtypeStruct((1, channels), F32),
            jax.ShapeDtypeStruct((1, 1), F32),
        ),
        compiler_params=params(),
        name="unpack",
    )(*got)
    return (
        loss.reshape(()),
        grad_conv,
        grad_cb.reshape(channels),
        grad_mix,
        grad_mb.reshape(channels),
        jnp.swapaxes(mask_grad[None], 1, 2),
        jnp.swapaxes(feat_grad[None], 1, 2),
        grad_rbias,
    )


def solution(mesh):
    return jax.shard_map(
        per_device,
        mesh=mesh,
        in_specs=(
            P("clip", "sess", None),
            P("clip", "sess", None),
            P("clip"),
            P("sess"),
            P(),
            P(),
            P(),
            P(),
            P("sess", None, None),
            P("sess", None, None),
            P("sess", None),
        ),
        out_specs=(
            P(),
            P(),
            P(),
            P(),
            P(),
            P("sess", "clip", None),
            P("sess", "clip", None),
            P("sess", "clip"),
        ),
        check_vma=False,
    )
```
